256 devices in a mesh: section: 8 (over y, core), ctx: 32 (over z, x).
Axes of the slice: x: 4, y: 4, z: 8, core: 2. Of those that a mesh axis runs over, the one named last changes fastest.
Arguments:
- section_input: bfloat16 [2, 4096, 2048], P(None, 'ctx'), may hold values from -6 to 6
- cotangent: bfloat16 [2, 4096, 2048], P(None, 'ctx'), may hold values from -6 to 6
- w_query: bfloat16 [8, 2048, 1024], P('section', 'ctx'), may hold values from -0.125 to 0.125
- w_key: bfloat16 [8, 2048, 1024], P('section', 'ctx'), may hold values from -0.125 to 0.125
- w_value: bfloat16 [8, 2048, 1024], P('section', 'ctx'), may hold values from -0.125 to 0.125
- w_out: bfloat16 [8, 1024, 2048], P('section', 'ctx'), may hold values from -0.1875 to 0.1875
- block_mask: int32 [2, 128, 2], P(None, 'ctx'), may hold values 0 or 1
Outputs:
- section_output: bfloat16 [8, 2, 4096, 2048], P('section', None, 'ctx')
- input_grad: bfloat16 [8, 2, 4096, 2048], P('section', None, 'ctx')
The draws below stay inside these ranges and needn't reach their ends.
Inputs may be any that keep to these rules, and one draw needn't show every extreme that they name: A block always attends to itself; column 0 and 1 of block_mask choose its two neighbour blocks.
All inputs are finite; a program needn't handle non-finite values.
Results may differ from the reference program's by a relative error of at most 0.03.
Values may be sent and summed in bfloat16 or wider, within the bound.
No kernel may reach another device: no remote copies, remote signals or barrier semaphores. Data moves between devices by JAX's collectives and lax.ppermute only.
A program may use at most 128 MiB of HBM per device.

```python
import jax
import jax.numpy as jnp
from jax import lax

D = 2048
HEADS = 8
HDIM = 128
MICRO = 2
BLK = 32
SEQ = 4096
NB = 128
SECTIONS = 8


def touch_ends(result, stream_key, low, largest):
    longest = result.shape.index(max(result.shape))
    spots = []
    for shift in (0, 1):
        where = [jax.random.randint(jax.random.fold_in(stream_key, axis), (), 0, length) for axis, length in enumerate(result.shape)]
        where[longest] = (where[longest] + shift) % result.shape[longest]
        spots.append(tuple(where))
    return result.at[spots[0]].set(low).at[spots[1]].set(largest)


def block_levels(own_key, dims, shards, least, high):
    def one(axis_at, blocks):
        heights = jax.random.uniform(jax.random.fold_in(jax.random.fold_in(own_key, 6), axis_at), (blocks,), jnp.float32, least / len(shards), high / len(shards))
        return jnp.repeat(jnp.exp(heights), dims[axis_at] // blocks).reshape((-1,) + (1,) * (len(dims) - axis_at - 1))

    factor_of = one(*shards[0])
    for cut in shards[1:]:
        factor_of = factor_of * one(*cut)
    return factor_of


def gaussian(stream_key, extent, deviation, limit, split=(), kind=jnp.bfloat16):
    entries = deviation * jax.random.normal(stream_key, extent, jnp.float32)
    if split:
        entries = entries * block_levels(stream_key, extent, split, -0.22, 0.18)
    return jnp.clip(entries, -limit, limit).astype(kind)


def setup_inputs(seed: int = 0) -> dict:
    arg_keys = jax.random.split(jax.random.key(seed), 8)
    section_input = gaussian(arg_keys[0], (MICRO, SEQ, D), 1.0, 6.0, ((1, 32),))
    cotangent = gaussian(arg_keys[1], (MICRO, SEQ, D), 1.0, 6.0, ((1, 32),))
    w_query = gaussian(arg_keys[2], (SECTIONS, D, HEADS * HDIM), D ** -0.5, 0.125, ((0, 8), (1, 32)))
    w_key = gaussian(arg_keys[3], (SECTIONS, D, HEADS * HDIM), D ** -0.5, 0.125, ((0, 8), (1, 32)))
    w_value = gaussian(arg_keys[4], (SECTIONS, D, HEADS * HDIM), D ** -0.5, 0.125, ((0, 8), (1, 32)))
    w_out = gaussian(arg_keys[5], (SECTIONS, HEADS * HDIM, D), (HEADS * HDIM) ** -0.5, 0.1875, ((0, 8), (1, 32)))
    block_mask = touch_ends((jax.random.randint(arg_keys[6], (MICRO, NB, 2), 0, 4) < 3).astype(jnp.int32), jax.random.fold_in(arg_keys[6], 1), 0, 1)
    return dict(section_input=section_input, cotangent=cotangent, w_query=w_query, w_key=w_key, w_value=w_value, w_out=w_out, block_mask=block_mask)


def rms_scale(values):
    return values * lax.rsqrt(lax.optimization_barrier(jnp.mean(values * values, axis=-1, keepdims=True)) + 1e-06)

def allowed_keys(mask_rows, block_ids, block_count):
    mask_float = mask_rows.astype(jnp.float32)
    left = mask_float[:, 0] * (block_ids > 0).astype(jnp.float32)
    right = mask_float[:, 1] * (block_ids < block_count - 1).astype(jnp.float32)
    return jnp.stack([left, jnp.ones_like(left), right], axis=1)

def project(layer_in, w_query, w_key, w_value):
    length = layer_in.shape[0]
    normed = rms_scale(layer_in.astype(jnp.float32)).astype(jnp.bfloat16)

    def head_normed(weight):
        out = jnp.dot(normed, weight, preferred_element_type=jnp.float32)
        out = rms_scale(out.reshape(length, HEADS, HDIM))
        return out.reshape(length, HEADS * HDIM).astype(jnp.bfloat16)
    query = head_normed(w_query)
    key = head_normed(w_key)
    value = jnp.dot(normed, w_value, preferred_element_type=jnp.float32).astype(jnp.bfloat16)
    return (query, key, value)

def attend(query, keys_ext, values_ext, allow, layer_in, w_out):
    length = query.shape[0]
    nblock = length // BLK
    queries = query.reshape(nblock, BLK, HEADS, HDIM)

    def windows(extended):
        grid = extended.reshape(nblock + 2, BLK, HEADS, HDIM)
        return jnp.concatenate([grid[:-2], grid[1:-1], grid[2:]], axis=1)
    keys = windows(keys_ext)
    values = windows(values_ext)
    scores = jnp.einsum('bqhd,bkhd->bhqk', queries, keys, preferred_element_type=jnp.float32) * HDIM ** (-0.5)
    weight = jnp.repeat(allow, BLK, axis=1)[:, None, None, :]
    probs = jnp.exp(scores) * weight
    total = lax.optimization_barrier(jnp.sum(probs, axis=-1))
    attended = jnp.einsum('bhqk,bkhd->bqhd', probs.astype(jnp.bfloat16), values, preferred_element_type=jnp.float32)
    attended = attended / jnp.transpose(total, (0, 2, 1))[..., None]
    attended = attended.reshape(length, HEADS * HDIM).astype(jnp.bfloat16)
    update = jnp.dot(attended, w_out, preferred_element_type=jnp.float32)
    return (layer_in.astype(jnp.float32) + update).astype(jnp.bfloat16)

def layer(layer_in, w_query, w_key, w_value, w_out, allow):
    query, key, value = project(layer_in, w_query, w_key, w_value)
    padding = jnp.zeros((BLK, HEADS * HDIM), jnp.bfloat16)
    keys_ext = jnp.concatenate([padding, key, padding], axis=0)
    values_ext = jnp.concatenate([padding, value, padding], axis=0)
    return attend(query, keys_ext, values_ext, allow, layer_in, w_out)

def reference(section_input, cotangent, w_query, w_key, w_value, w_out, block_mask):
    block_ids = jnp.arange(NB)
    outputs = []
    grads = []
    for micro_id in range(MICRO):
        allow = allowed_keys(block_mask[micro_id], block_ids, NB)
        current = section_input[micro_id]
        saved = []
        forward_out = []
        for section in range(SECTIONS):
            saved.append(current)
            current = layer(current, w_query[section], w_key[section], w_value[section], w_out[section], allow)
            forward_out.append(current)
        grad = cotangent[micro_id]
        backward_out = [None] * SECTIONS
        for section in reversed(range(SECTIONS)):

            def section_fn(values, section=section):
                return layer(values, w_query[section], w_key[section], w_value[section], w_out[section], allow)
            _, pull = jax.vjp(section_fn, saved[section])
            grad = pull(grad)[0]
            backward_out[section] = grad
        outputs.append(jnp.stack(forward_out))
        grads.append(jnp.stack(backward_out))
    return (jnp.stack(outputs, axis=1), jnp.stack(grads, axis=1))
```

```python
import jax
import jax.numpy as jnp
from jax import lax
from jax.experimental import pallas as pl
from jax.experimental.pallas import tpu as pltpu
from jax.sharding import PartitionSpec as P

D = 2048
HEADS = 8
HDIM = 128
BLOCKS_DEV = 4
BLK = 32
ROWS = BLK * BLOCKS_DEV
EXT = ROWS + 2 * BLK
WIDTH = HEADS * HDIM
PACK = 2 * WIDTH + 128
EPS = 1e-06
VMEM_LIMIT = 24 << 20
SCALE = HDIM ** (-0.5)
F32 = jnp.float32
BF16 = jnp.bfloat16

NT = (((1,), (1,)), ((), ()))
NN = (((1,), (0,)), ((), ()))
TN = (((0,), (0,)), ((), ()))


def dot(a, b, dims=NN):
    return lax.dot_general(a, b, dims, preferred_element_type=F32)


def wtile(w_ref, row, count, col, width):
    tile = w_ref[:, row : row + count, col : col + width]
    return tile.reshape(tile.shape[0] * count, width)


def forward_body(
    flags,
    x0_ref,
    x_ref,
    xl_ref,
    xr_ref,
    mask_ref,
    w_ref,
    xs_in,
    out_in,
    qa_in,
    kv_in,
    rr_in,
    next_ref,
    left_ref,
    right_ref,
    xs_ref,
    out_ref,
    qa_ref,
    kv_ref,
    rr_ref,
    xe,
    normed,
    qa,
    kv,
    rr,
    result,
    sem_in,
    sem_out,
):
    active, slot, first = flags[0], flags[1], flags[2]

    @pl.when(active == 1)
    def _():
        @pl.when(first == 1)
        def _():
            copy = pltpu.make_async_copy(x0_ref.at[slot], xe, sem_in.at[0])
            copy.start()
            copy.wait()

        @pl.when(first == 0)
        def _():
            copies = [
                pltpu.make_async_copy(xl_ref, xe.at[:BLK], sem_in.at[0]),
                pltpu.make_async_copy(x_ref, xe.at[BLK : BLK + ROWS], sem_in.at[1]),
                pltpu.make_async_copy(xr_ref, xe.at[BLK + ROWS :], sem_in.at[2]),
            ]
            for copy in copies:
                copy.start()
            for copy in copies:
                copy.wait()

        saves = [pltpu.make_async_copy(xe.at[BLK : BLK + ROWS], xs_ref.at[slot], sem_out.at[0])]
        saves[0].start()
        for lo in range(0, EXT, BLK):
            rows = xe[lo : lo + BLK].astype(F32)
            scale = lax.rsqrt(jnp.mean(rows * rows, axis=-1, keepdims=True) + EPS)
            normed[lo : lo + BLK] = (rows * scale).astype(BF16)
        lane = lax.broadcasted_iota(jnp.int32, (ROWS, 128), 1)
        r_all = jnp.zeros((ROWS, 128), F32)
        inv_all = jnp.zeros((ROWS, 128), F32)
        mask = mask_ref[slot]

        def project(pair):
            col = pair * 256
            query = dot(normed[BLK : BLK + ROWS], wtile(w_ref, 0, 64, col, 256))
            key = dot(normed[...], wtile(w_ref, 64, 64, col, 256))
            value = dot(normed[...], wtile(w_ref, 128, 64, col, 256))
            return query, key, value

        current = project(0)
        for pair in range(4):
            following = project(pair + 1) if pair < 3 else None
            for half in range(2):
                head = pair * 2 + half
                cols = slice(half * HDIM, (half + 1) * HDIM)
                at = slice(head * HDIM, (head + 1) * HDIM)
                query, key, value = (part[:, cols] for part in current)
                rq = lax.rsqrt(jnp.mean(query * query, axis=-1, keepdims=True) + EPS)
                rk = lax.rsqrt(jnp.mean(key * key, axis=-1, keepdims=True) + EPS)
                query = (query * rq).astype(BF16)
                key = (key * rk).astype(BF16)
                value = value.astype(BF16)
                probs = jnp.exp(dot(query, key, NT) * SCALE) * mask
                inv = 1.0 / jnp.sum(probs, axis=-1, keepdims=True)
                attended = dot(probs.astype(BF16), value) * inv
                qa[:, at] = query
                qa[:, WIDTH + head * HDIM : WIDTH + (head + 1) * HDIM] = attended.astype(BF16)
                kv[:, at] = key
                kv[:, WIDTH + head * HDIM : WIDTH + (head + 1) * HDIM] = value
                high = inv.astype(BF16).astype(F32)
                r_all = jnp.where(lane == head, rq, r_all)
                r_all = jnp.where(lane == HEADS + head, rk[BLK : BLK + ROWS], r_all)
                inv_all = jnp.where(lane == head, high, inv_all)
                inv_all = jnp.where(lane == HEADS + head, inv - high, inv_all)
            current = following
        qa[:, 2 * WIDTH :] = inv_all.astype(BF16)
        rr[...] = r_all
        for index, (source, target) in enumerate(((qa, qa_ref), (kv, kv_ref), (rr, rr_ref))):
            copy = pltpu.make_async_copy(source, target.at[slot], sem_out.at[1 + index])
            copy.start()
            saves.append(copy)
        for tile in range(8):
            col = tile * 256
            update = dot(
                qa[:, WIDTH : 2 * WIDTH],
                wtile(w_ref, 192 + 32 * (tile // 4), 32, col % 1024, 256),
            )
            result[:, col : col + 256] = (
                xe[BLK : BLK + ROWS, col : col + 256].astype(F32) + update
            ).astype(BF16)
        for index, (source, target) in enumerate(
            (
                (result, next_ref),
                (result.at[:BLK], left_ref),
                (result.at[ROWS - BLK :], right_ref),
                (result, out_ref.at[slot]),
            )
        ):
            copy = pltpu.make_async_copy(source, target, sem_out.at[4 + index])
            copy.start()
            saves.append(copy)
        for copy in saves:
            copy.wait()


def spaces(*names):
    table = dict(s=pltpu.SMEM, v=pltpu.VMEM, a=pl.ANY)
    return [pl.BlockSpec(memory_space=table[n]) for n in names]


def shape_of(a):
    return jax.ShapeDtypeStruct(a.shape, a.dtype)


def forward_call(flags, x0, x, xl, xr, mask, w, saved):
    rows = jax.ShapeDtypeStruct((ROWS, D), BF16)
    edge = jax.ShapeDtypeStruct((BLK, D), BF16)
    outs = pl.pallas_call(
        forward_body,
        name="forward_layer",
        out_shape=(rows, edge, edge) + tuple(shape_of(a) for a in saved),
        in_specs=spaces("s", "a", "a", "a", "a", "v", "v", "a", "a", "a", "a", "a"),
        out_specs=spaces(*"aaaaaaaa"),
        scratch_shapes=[
            pltpu.VMEM((EXT, D), BF16),
            pltpu.VMEM((EXT, D), BF16),
            pltpu.VMEM((ROWS, PACK), BF16),
            pltpu.VMEM((EXT, 2 * WIDTH), BF16),
            pltpu.VMEM((ROWS, 128), F32),
            pltpu.VMEM((ROWS, D), BF16),
            pltpu.SemaphoreType.DMA((3,)),
            pltpu.SemaphoreType.DMA((8,)),
        ],
        input_output_aliases={7: 3, 8: 4, 9: 5, 10: 6, 11: 7},
        compiler_params=pltpu.CompilerParams(vmem_limit_bytes=VMEM_LIMIT),
    )(flags, x0, x, xl, xr, mask, w, *saved)
    return outs[:3], outs[3:]

def load_body(g_ref, w_ref, sem):
    copy = pltpu.make_async_copy(g_ref, w_ref, sem)
    copy.start()
    copy.wait()


def load_call(g):
    return pl.pallas_call(
        load_body,
        name="load_weights",
        out_shape=pltpu.VMEM(g.shape, g.dtype),
        in_specs=spaces("a"),
        out_specs=pl.BlockSpec(memory_space=pltpu.VMEM),
        scratch_shapes=[pltpu.SemaphoreType.DMA],
        compiler_params=pltpu.CompilerParams(vmem_limit_bytes=20 << 20),
    )(g)


def backward_body(
    flags,
    c0_ref,
    g_ref,
    gl_ref,
    gr_ref,
    mask_ref,
    w_ref,
    xs_ref,
    qa_ref,
    qal_ref,
    qar_ref,
    kv_ref,
    rr_ref,
    grad_in,
    next_ref,
    left_ref,
    right_ref,
    grad_ref,
    ge,
    xs,
    qa,
    kv,
    rr,
    dz,
    dn,
    result,
    sem_in,
    sem_save,
    sem_out,
):
    active, slot, last = flags[0], flags[1], flags[2]
    own = slice(BLK, BLK + ROWS)

    @pl.when(active == 1)
    def _():
        loads = [
            pltpu.make_async_copy(source.at[slot], target, sem_save.at[index])
            for index, (source, target) in enumerate(
                (
                    (qal_ref, qa.at[:BLK]),
                    (qa_ref, qa.at[own]),
                    (qar_ref, qa.at[BLK + ROWS :]),
                    (kv_ref, kv),
                    (rr_ref, rr),
                    (xs_ref, xs),
                )
            )
        ]

        @pl.when(last == 1)
        def _():
            copy = pltpu.make_async_copy(c0_ref.at[slot], ge, sem_in.at[0])
            copy.start()
            for load in loads:
                load.start()
            copy.wait()

        @pl.when(last == 0)
        def _():
            copies = [
                pltpu.make_async_copy(gl_ref, ge.at[:BLK], sem_in.at[0]),
                pltpu.make_async_copy(g_ref, ge.at[own], sem_in.at[1]),
                pltpu.make_async_copy(gr_ref, ge.at[BLK + ROWS :], sem_in.at[2]),
            ]
            for copy in copies:
                copy.start()
            for load in loads:
                load.start()
            for copy in copies:
                copy.wait()

        for load in loads:
            load.wait()
        mask = mask_ref[slot]

        def spread(pair):
            low = w_ref[8 * pair : 8 * pair + 8, 192:224, :].reshape(256, 1024)
            high = w_ref[8 * pair : 8 * pair + 8, 224:256, :].reshape(256, 1024)
            return dot(ge[:, :1024], low, NT) + dot(ge[:, 1024:], high, NT)

        current = spread(0)
        for pair in range(4):
            following = spread(pair + 1) if pair < 3 else None
            for half in range(2):
                head = pair * 2 + half
                at = slice(head * HDIM, (head + 1) * HDIM)
                beyond = slice(WIDTH + head * HDIM, WIDTH + (head + 1) * HDIM)
                d_att = current[:, half * HDIM : (half + 1) * HDIM]
                d_att = d_att.astype(BF16).astype(F32)
                query, key, value = qa[:, at], kv[:, at], kv[:, beyond]
                col = 2 * WIDTH + head
                inv = qa[:, col : col + 1].astype(F32) + qa[
                    :, col + HEADS : col + HEADS + 1
                ].astype(F32)
                d_sum = (d_att * inv).astype(BF16)
                d_total = -inv * jnp.sum(
                    d_att * qa[:, beyond].astype(F32), axis=-1, keepdims=True
                )
                probs = jnp.exp(dot(query, key, NT) * SCALE) * mask
                d_probs = dot(d_sum, value, NT)
                d_scores = (probs * (d_probs + d_total) * SCALE).astype(BF16)
                d_value = dot(probs.astype(BF16), d_sum, TN)[own]
                d_key = dot(d_scores, query, TN)[own]
                d_query = dot(d_scores[own], key)

                def unnorm(grad, unit, r):
                    grad = grad.astype(BF16).astype(F32)
                    unit = unit.astype(F32)
                    return r * (grad - unit * jnp.mean(grad * unit, axis=-1, keepdims=True))

                dz[:, at] = unnorm(d_query, query[own], rr[:, head : head + 1]).astype(BF16)
                dz[:, beyond] = unnorm(
                    d_key, key[own], rr[:, HEADS + head : HEADS + head + 1]
                ).astype(BF16)
                dz[:, 2 * WIDTH + head * HDIM : 2 * WIDTH + (head + 1) * HDIM] = d_value.astype(BF16)
            current = following
        x = xs[...].astype(F32)
        scale = lax.rsqrt(jnp.mean(x * x, axis=-1, keepdims=True) + EPS)
        inner = jnp.zeros((ROWS, 1), F32)
        for tile in range(8):
            grad = jnp.zeros((ROWS, 256), F32)
            for part in range(3):
                weight = w_ref[4 * tile : 4 * tile + 4, 64 * part : 64 * part + 64, :]
                grad += dot(
                    dz[:, part * WIDTH : (part + 1) * WIDTH], weight.reshape(256, WIDTH), NT
                )
            cols = slice(tile * 256, (tile + 1) * 256)
            grad = grad.astype(BF16).astype(F32)
            dn[:, cols] = grad
            inner += jnp.sum(grad * xs[:, cols].astype(F32), axis=-1, keepdims=True)
        inner = inner * scale * scale * (1.0 / D)
        for tile in range(8):
            cols = slice(tile * 256, (tile + 1) * 256)
            value = dn[:, cols] - xs[:, cols].astype(F32) * inner
            result[:, cols] = (ge[own, cols].astype(F32) + scale * value).astype(BF16)
        saves = [
            pltpu.make_async_copy(source, target, sem_out.at[index])
            for index, (source, target) in enumerate(
                (
                    (result, next_ref),
                    (result.at[:BLK], left_ref),
                    (result.at[ROWS - BLK :], right_ref),
                    (result, grad_ref.at[slot]),
                )
            )
        ]
        for copy in saves:
            copy.start()
        for copy in saves:
            copy.wait()


def backward_call(flags, c0, g, gl, gr, mask, w, xs, qa, qal, qar, kv, rr, grads):
    rows = jax.ShapeDtypeStruct((ROWS, D), BF16)
    edge = jax.ShapeDtypeStruct((BLK, D), BF16)
    outs = pl.pallas_call(
        backward_body,
        name="backward_layer",
        out_shape=(rows, edge, edge, shape_of(grads)),
        in_specs=spaces(*"saaaavvaaaaaaa"),
        out_specs=spaces(*"aaaa"),
        scratch_shapes=[
            pltpu.VMEM((EXT, D), BF16),
            pltpu.VMEM((ROWS, D), BF16),
            pltpu.VMEM((EXT, PACK), BF16),
            pltpu.VMEM((EXT, 2 * WIDTH), BF16),
            pltpu.VMEM((ROWS, 128), F32),
            pltpu.VMEM((ROWS, 3 * WIDTH), BF16),
            pltpu.VMEM((ROWS, D), F32),
            pltpu.VMEM((ROWS, D), BF16),
            pltpu.SemaphoreType.DMA((3,)),
            pltpu.SemaphoreType.DMA((6,)),
            pltpu.SemaphoreType.DMA((4,)),
        ],
        input_output_aliases={13: 3},
        compiler_params=pltpu.CompilerParams(vmem_limit_bytes=VMEM_LIMIT),
    )(flags, c0, g, gl, gr, mask, w, xs, qa, qal, qar, kv, rr, grads)
    return outs[:3], outs[3]


BOTH = ("section", "ctx")


def neighbours(n_ctx, distance):
    return [(c, c + distance) for c in range(n_ctx) if 0 <= c + distance < n_ctx]


def hop(sections, step, n_ctx, distance):
    return [
        (s * n_ctx + source, (s + step) * n_ctx + target)
        for s in sections
        for source, target in neighbours(n_ctx, distance)
    ]


def relay(parts, sections, step, n_ctx):
    rows, left, right = parts
    rows = lax.ppermute(rows, BOTH, hop(sections, step, n_ctx, 0))
    from_left = lax.ppermute(right, BOTH, hop(sections, step, n_ctx, 1))
    from_right = lax.ppermute(left, BOTH, hop(sections, step, n_ctx, -1))
    return rows, from_left, from_right


def edges(block, dim, width, n_ctx):
    size = block.shape[dim]
    tail = lax.slice_in_dim(block, size - width, size, axis=dim)
    head = lax.slice_in_dim(block, 0, width, axis=dim)
    from_left = lax.ppermute(tail, "ctx", neighbours(n_ctx, 1))
    from_right = lax.ppermute(head, "ctx", neighbours(n_ctx, -1))
    return from_left, from_right


def key_weights(block_mask, place, n_ctx):
    block_ids = place * BLOCKS_DEV + jnp.arange(BLOCKS_DEV)
    mask = block_mask.astype(F32)
    left = mask[:, :, 0] * (block_ids > 0).astype(F32)
    right = mask[:, :, 1] * (block_ids < BLOCKS_DEV * n_ctx - 1).astype(F32)
    allow = jnp.stack([left, jnp.ones_like(left), right], axis=2)
    before, after = edges(allow, 1, 1, n_ctx)
    allow = jnp.concatenate([before, allow, after], axis=1)
    allow = jnp.repeat(allow, BLK, axis=1)
    block = jnp.arange(EXT) // BLK
    offset = block[None, :] - block[:, None] + 1
    return sum(
        jnp.where(offset == side, allow[:, :, side : side + 1], 0.0) for side in range(3)
    )


def per_device(section_input, cotangent, w_query, w_key, w_value, w_out, block_mask):
    n_section = lax.axis_size("section")
    n_ctx = lax.axis_size("ctx")
    section = lax.axis_index("section")
    place = lax.axis_index("ctx")
    micro = section_input.shape[0]
    steps = n_section + micro - 1

    shard = jnp.concatenate(
        [w_query[0], w_key[0], w_value[0], w_out[0][:, :WIDTH], w_out[0][:, WIDTH:]], axis=0
    )
    gathered = lax.all_gather(shard, "ctx", axis=0, tiled=False)
    before, after = edges(jnp.stack([section_input, cotangent]), 2, BLK, n_ctx)
    extended = jnp.concatenate(
        [before, jnp.stack([section_input, cotangent]), after], axis=2
    )
    mask = key_weights(block_mask, place, n_ctx)
    weights = load_call(gathered)

    def plan(step, position):
        micro_id = step - position
        active = (micro_id >= 0) & (micro_id < micro)
        return jnp.stack(
            [active, jnp.clip(micro_id, 0, micro - 1), position == 0]
        ).astype(jnp.int32)

    saved = (
        jnp.zeros((micro, ROWS, D), BF16),
        jnp.zeros((micro, ROWS, D), BF16),
        jnp.zeros((micro, ROWS, PACK), BF16),
        jnp.zeros((micro, EXT, 2 * WIDTH), BF16),
        jnp.zeros((micro, ROWS, 128), F32),
    )
    zero_rows = jnp.zeros((ROWS, D), BF16)
    zero_edge = jnp.zeros((BLK, D), BF16)
    incoming = (zero_rows, zero_edge, zero_edge)
    forward_mask = mask[:, BLK : BLK + ROWS]
    for step in range(steps):
        parts, saved = forward_call(
            plan(step, section), extended[0], *incoming, forward_mask, weights, saved
        )
        senders = [s for s in range(step - micro + 1, step + 1) if 0 <= s < n_section - 1]
        if senders:
            incoming = relay(parts, senders, 1, n_ctx)
    xs, outputs, qa, kv, rr = saved
    qa_left, qa_right = edges(qa, 1, BLK, n_ctx)
    grads = jnp.zeros((micro, ROWS, D), BF16)
    incoming = (zero_rows, zero_edge, zero_edge)
    for step in range(steps):
        parts, grads = backward_call(
            plan(step, n_section - 1 - section),
            extended[1],
            *incoming,
            mask,
            weights,
            xs,
            qa,
            qa_left,
            qa_right,
            kv,
            rr,
            grads,
        )
        top = n_section - 1 - step
        senders = [s for s in range(top, top + micro) if 0 < s < n_section]
        if senders:
            incoming = relay(parts, senders, -1, n_ctx)
    return (outputs[None], grads[None])


def solution(mesh):
    return jax.shard_map(
        per_device,
        mesh=mesh,
        in_specs=(
            P(None, "ctx", None),
            P(None, "ctx", None),
            P("section", "ctx", None),
            P("section", "ctx", None),
            P("section", "ctx", None),
            P("section", "ctx", None),
            P(None, "ctx", None),
        ),
        out_specs=(P("section", None, "ctx", None), P("section", None, "ctx", None)),
        check_vma=False,
    )
```

```python
import functools

import jax
import jax.numpy as jnp
from jax import lax
from jax.experimental import pallas as pl
from jax.experimental.pallas import tpu as pltpu
from jax.sharding import PartitionSpec as P

D = 2048
HEADS = 8
HDIM = 128
BLOCKS_DEV = 4
BLK = 32
MICRO = 2
ROWS = BLK * BLOCKS_DEV
EXT = ROWS + 2 * BLK
WIDTH = HEADS * HDIM
PACK = 2 * WIDTH + 128
EPS = 1e-06
VMEM_LIMIT = 16 << 20
SCALE = HDIM ** (-0.5)
F32 = jnp.float32
BF16 = jnp.bfloat16

NT = (((1,), (1,)), ((), ()))
NN = (((1,), (0,)), ((), ()))
TN = (((0,), (0,)), ((), ()))


def dot(a, b, dims=NN):
    return lax.dot_general(a, b, dims, preferred_element_type=F32)


def wtile(w_ref, row, count, col, width):
    tile = w_ref[:, row : row + count, col : col + width]
    return tile.reshape(tile.shape[0] * count, width)


def schedule(step, position):
    micro_id = step - position
    active = (micro_id >= 0) & (micro_id < MICRO)
    return active, jnp.clip(micro_id, 0, MICRO - 1), position == 0


def forward_body(
    step,
    section_ref,
    x0_ref,
    x_ref,
    xl_ref,
    xr_ref,
    mask_ref,
    w_ref,
    xs_in,
    out_in,
    qa_in,
    kv_in,
    rr_in,
    next_ref,
    xs_ref,
    out_ref,
    qa_ref,
    kv_ref,
    rr_ref,
    xe,
    normed,
    qa,
    kv,
    rr,
    result,
    inverse,
    mask,
    sem_in,
    sem_out,
):
    active, slot, first = schedule(step, section_ref[0])

    @pl.when(active)
    def _():
        mask_copy = pltpu.make_async_copy(mask_ref.at[slot], mask, sem_in.at[3])
        mask_copy.start()

        @pl.when(first)
        def _():
            copy = pltpu.make_async_copy(x0_ref.at[slot], xe, sem_in.at[0])
            copy.start()
            copy.wait()

        @pl.when(jnp.logical_not(first))
        def _():
            copies = [
                pltpu.make_async_copy(xl_ref, xe.at[:BLK], sem_in.at[0]),
                pltpu.make_async_copy(x_ref, xe.at[BLK : BLK + ROWS], sem_in.at[1]),
                pltpu.make_async_copy(xr_ref, xe.at[BLK + ROWS :], sem_in.at[2]),
            ]
            for copy in copies:
                copy.start()
            for copy in copies:
                copy.wait()

        saves = [pltpu.make_async_copy(xe.at[BLK : BLK + ROWS], xs_ref.at[slot], sem_out.at[0])]
        saves[0].start()

        @pl.loop(0, EXT // BLK)
        def _(block):
            at = pl.ds(pl.multiple_of(block * BLK, BLK), BLK)
            rows = xe[at].astype(F32)
            scale = lax.rsqrt(jnp.mean(rows * rows, axis=-1, keepdims=True) + EPS)
            normed[at] = (rows * scale).astype(BF16)

        rr[...] = jnp.zeros((ROWS, 128), F32)
        inverse[...] = jnp.zeros((ROWS, 128), F32)
        mask_copy.wait()

        @pl.loop(0, 4)
        def _(pair):
            lane = lax.broadcasted_iota(jnp.int32, (ROWS, 128), 1)
            tile = pl.ds(pl.multiple_of(pair * 256, 256), 256)
            queries = dot(normed[BLK : BLK + ROWS], w_ref[:, 0:64, tile].reshape(D, 256))
            keys = dot(normed[...], w_ref[:, 64:128, tile].reshape(D, 256))
            values = dot(normed[...], w_ref[:, 128:192, tile].reshape(D, 256))
            for half in range(2):
                head = pair * 2 + half
                cols = slice(half * HDIM, (half + 1) * HDIM)
                at = pl.ds(pl.multiple_of(head * HDIM, HDIM), HDIM)
                beyond = pl.ds(pl.multiple_of(WIDTH + head * HDIM, HDIM), HDIM)
                query, key, value = queries[:, cols], keys[:, cols], values[:, cols]
                rq = lax.rsqrt(jnp.mean(query * query, axis=-1, keepdims=True) + EPS)
                rk = lax.rsqrt(jnp.mean(key * key, axis=-1, keepdims=True) + EPS)
                query = (query * rq).astype(BF16)
                key = (key * rk).astype(BF16)
                value = value.astype(BF16)
                probs = jnp.exp(dot(query, key, NT) * SCALE) * mask[...]
                inv = 1.0 / jnp.sum(probs, axis=-1, keepdims=True)
                attended = dot(probs.astype(BF16), value) * inv
                qa[:, at] = query
                qa[:, beyond] = attended.astype(BF16)
                kv[:, at] = key
                kv[:, beyond] = value
                high = inv.astype(BF16).astype(F32)
                stored = jnp.where(lane == head, rq, rr[...])
                rr[...] = jnp.where(lane == HEADS + head, rk[BLK : BLK + ROWS], stored)
                stored = jnp.where(lane == head, high, inverse[...])
                inverse[...] = jnp.where(lane == HEADS + head, inv - high, stored)

        qa[:, 2 * WIDTH :] = inverse[...].astype(BF16)
        for index, (source, target) in enumerate(((qa, qa_ref), (kv, kv_ref), (rr, rr_ref))):
            copy = pltpu.make_async_copy(source, target.at[slot], sem_out.at[1 + index])
            copy.start()
            saves.append(copy)

        for half in range(2):
            @pl.loop(0, 4)
            def _(tile):
                source = pl.ds(pl.multiple_of(tile * 256, 256), 256)
                cols = pl.ds(pl.multiple_of(half * 1024 + tile * 256, 256), 256)
                low = 192 + 32 * half
                weight = w_ref[:, low : low + 32, source].reshape(WIDTH, 256)
                update = dot(qa[:, WIDTH : 2 * WIDTH], weight)
                result[:, cols] = (xe[BLK : BLK + ROWS, cols].astype(F32) + update).astype(BF16)

        for index, (source, target) in enumerate(
            (
                (result, next_ref),
                (result, out_ref.at[slot]),
            )
        ):
            copy = pltpu.make_async_copy(source, target, sem_out.at[4 + index])
            copy.start()
            saves.append(copy)
        for copy in saves:
            copy.wait()


def spaces(*names):
    table = dict(s=pltpu.SMEM, v=pltpu.VMEM, a=pltpu.HBM)
    return [pl.BlockSpec(memory_space=table[n]) for n in names]


def shape_of(a):
    return jax.ShapeDtypeStruct(a.shape, a.dtype)


def forward_call(step, position, x0, x, xl, xr, mask, w, saved):
    rows = jax.ShapeDtypeStruct((ROWS, D), BF16)
    outs = pl.pallas_call(
        functools.partial(forward_body, step),
        name="forward_layer",
        out_shape=(rows,) + tuple(shape_of(a) for a in saved),
        in_specs=spaces(*"saaaaavaaaaa"),
        out_specs=spaces(*"aaaaaa"),
        scratch_shapes=[
            pltpu.VMEM((EXT, D), BF16),
            pltpu.VMEM((EXT, D), BF16),
            pltpu.VMEM((ROWS, PACK), BF16),
            pltpu.VMEM((EXT, 2 * WIDTH), BF16),
            pltpu.VMEM((ROWS, 128), F32),
            pltpu.VMEM((ROWS, D), BF16),
            pltpu.VMEM((ROWS, 128), F32),
            pltpu.VMEM((ROWS, EXT), F32),
            pltpu.SemaphoreType.DMA((4,)),
            pltpu.SemaphoreType.DMA((6,)),
        ],
        input_output_aliases={7: 1, 8: 2, 9: 3, 10: 4, 11: 5},
        compiler_params=pltpu.CompilerParams(vmem_limit_bytes=VMEM_LIMIT),
    )(position, x0, x, xl, xr, mask, w, *saved)
    return outs[0], outs[1:]

def load_body(g_ref, w_ref, sem):
    copy = pltpu.make_async_copy(g_ref, w_ref, sem)
    copy.start()
    copy.wait()


def load_call(g):
    return pl.pallas_call(
        load_body,
        name="load_weights",
        out_shape=pltpu.VMEM(g.shape, g.dtype),
        in_specs=spaces("a"),
        out_specs=pl.BlockSpec(memory_space=pltpu.VMEM),
        scratch_shapes=[pltpu.SemaphoreType.DMA],
        compiler_params=pltpu.CompilerParams(vmem_limit_bytes=20 << 20),
    )(g)


def backward_body(
    step,
    section_ref,
    c0_ref,
    g_ref,
    gl_ref,
    gr_ref,
    mask_ref,
    w_ref,
    xs_ref,
    qa_ref,
    qal_ref,
    qar_ref,
    kv_ref,
    rr_ref,
    grad_in,
    next_ref,
    grad_ref,
    ge,
    xs,
    qa,
    kv,
    rr,
    dz,
    dn,
    result,
    mask,
    inner_ref,
    sem_in,
    sem_save,
    sem_out,
):
    active, slot, last = schedule(step, section_ref[0])
    own = slice(BLK, BLK + ROWS)

    @pl.when(active)
    def _():
        loads = [
            pltpu.make_async_copy(source.at[slot], target, sem_save.at[index])
            for index, (source, target) in enumerate(
                (
                    (qal_ref, qa.at[:BLK]),
                    (qa_ref, qa.at[own]),
                    (qar_ref, qa.at[BLK + ROWS :]),
                    (kv_ref, kv),
                    (rr_ref, rr),
                    (xs_ref, xs),
                    (mask_ref, mask),
                )
            )
        ]

        @pl.when(last)
        def _():
            copy = pltpu.make_async_copy(c0_ref.at[slot], ge, sem_in.at[0])
            copy.start()
            for load in loads:
                load.start()
            copy.wait()

        @pl.when(jnp.logical_not(last))
        def _():
            copies = [
                pltpu.make_async_copy(gl_ref, ge.at[:BLK], sem_in.at[0]),
                pltpu.make_async_copy(g_ref, ge.at[own], sem_in.at[1]),
                pltpu.make_async_copy(gr_ref, ge.at[BLK + ROWS :], sem_in.at[2]),
            ]
            for copy in copies:
                copy.start()
            for load in loads:
                load.start()
            for copy in copies:
                copy.wait()

        for load in loads:
            load.wait()

        @pl.loop(0, 4)
        def _(pair):
            lane = lax.broadcasted_iota(jnp.int32, (EXT, 128), 1)
            rows = pl.ds(pl.multiple_of(8 * pair, 8), 8)
            low = w_ref[rows, 192:224, :].reshape(256, 1024)
            high = w_ref[rows, 224:256, :].reshape(256, 1024)
            spread = dot(ge[:, :1024], low, NT) + dot(ge[:, 1024:], high, NT)
            for half in range(2):
                head = pair * 2 + half
                at = pl.ds(pl.multiple_of(head * HDIM, HDIM), HDIM)
                beyond = pl.ds(pl.multiple_of(WIDTH + head * HDIM, HDIM), HDIM)
                third = pl.ds(pl.multiple_of(2 * WIDTH + head * HDIM, HDIM), HDIM)
                d_att = spread[:, half * HDIM : (half + 1) * HDIM].astype(BF16).astype(F32)
                query, key, value = qa[:, at], kv[:, at], kv[:, beyond]
                picked = (lane == head) | (lane == HEADS + head)
                inv = jnp.sum(
                    jnp.where(picked, qa[:, 2 * WIDTH :].astype(F32), 0.0),
                    axis=-1,
                    keepdims=True,
                )
                d_sum = (d_att * inv).astype(BF16)
                d_total = -inv * jnp.sum(
                    d_att * qa[:, beyond].astype(F32), axis=-1, keepdims=True
                )
                probs = jnp.exp(dot(query, key, NT) * SCALE) * mask[...]
                d_probs = dot(d_sum, value, NT)
                d_scores = (probs * (d_probs + d_total) * SCALE).astype(BF16)
                d_value = dot(probs.astype(BF16), d_sum, TN)[own]
                d_key = dot(d_scores, query, TN)[own]
                d_query = dot(d_scores[own], key)

                def unnorm(grad, unit, which):
                    grad = grad.astype(BF16).astype(F32)
                    unit = unit.astype(F32)
                    r = jnp.sum(
                        jnp.where(lane[:ROWS] == which, rr[...], 0.0), axis=-1, keepdims=True
                    )
                    return r * (grad - unit * jnp.mean(grad * unit, axis=-1, keepdims=True))

                dz[:, at] = unnorm(d_query, query[own], head).astype(BF16)
                dz[:, beyond] = unnorm(d_key, key[own], HEADS + head).astype(BF16)
                dz[:, third] = d_value.astype(BF16)

        inner_ref[...] = jnp.zeros((ROWS, 128), F32)

        @pl.loop(0, 8)
        def _(tile):
            rows = pl.ds(pl.multiple_of(4 * tile, 4), 4)
            cols = pl.ds(pl.multiple_of(tile * 256, 256), 256)
            grad = jnp.zeros((ROWS, 256), F32)
            for part in range(3):
                weight = w_ref[rows, 64 * part : 64 * part + 64, :].reshape(256, WIDTH)
                grad += dot(dz[:, part * WIDTH : (part + 1) * WIDTH], weight, NT)
            grad = grad.astype(BF16).astype(F32)
            dn[:, cols] = grad
            product = grad * xs[:, cols].astype(F32)
            inner_ref[...] += product[:, :128] + product[:, 128:]

        @pl.loop(0, ROWS // BLK)
        def _(block):
            at = pl.ds(pl.multiple_of(block * BLK, BLK), BLK)
            x = xs[at].astype(F32)
            scale = lax.rsqrt(jnp.mean(x * x, axis=-1, keepdims=True) + EPS)
            inner = jnp.sum(inner_ref[at], axis=-1, keepdims=True) * scale * scale * (1.0 / D)
            through = ge[pl.ds(pl.multiple_of(block * BLK + BLK, BLK), BLK)].astype(F32)
            result[at] = (through + scale * (dn[at] - x * inner)).astype(BF16)

        saves = [
            pltpu.make_async_copy(source, target, sem_out.at[index])
            for index, (source, target) in enumerate(
                (
                    (result, next_ref),
                    (result, grad_ref.at[slot]),
                )
            )
        ]
        for copy in saves:
            copy.start()
        for copy in saves:
            copy.wait()


def backward_call(step, position, c0, g, gl, gr, mask, w, xs, qa, qal, qar, kv, rr, grads):
    rows = jax.ShapeDtypeStruct((ROWS, D), BF16)
    outs = pl.pallas_call(
        functools.partial(backward_body, step),
        name="backward_layer",
        out_shape=(rows, shape_of(grads)),
        in_specs=spaces(*"saaaaavaaaaaaa"),
        out_specs=spaces(*"aa"),
        scratch_shapes=[
            pltpu.VMEM((EXT, D), BF16),
            pltpu.VMEM((ROWS, D), BF16),
            pltpu.VMEM((EXT, PACK), BF16),
            pltpu.VMEM((EXT, 2 * WIDTH), BF16),
            pltpu.VMEM((ROWS, 128), F32),
            pltpu.VMEM((ROWS, 3 * WIDTH), BF16),
            pltpu.VMEM((ROWS, D), F32),
            pltpu.VMEM((ROWS, D), BF16),
            pltpu.VMEM((EXT, EXT), F32),
            pltpu.VMEM((ROWS, 128), F32),
            pltpu.SemaphoreType.DMA((3,)),
            pltpu.SemaphoreType.DMA((7,)),
            pltpu.SemaphoreType.DMA((2,)),
        ],
        input_output_aliases={13: 1},
        compiler_params=pltpu.CompilerParams(vmem_limit_bytes=VMEM_LIMIT),
    )(position, c0, g, gl, gr, mask, w, xs, qa, qal, qar, kv, rr, grads)
    return outs

BOTH = ("section", "ctx")


def neighbours(n_ctx, distance):
    return [(c, c + distance) for c in range(n_ctx) if 0 <= c + distance < n_ctx]


def hop(sections, step, n_ctx):
    return [(s * n_ctx + c, (s + step) * n_ctx + c) for s in sections for c in range(n_ctx)]


def relay(rows, sections, step, n_ctx):
    rows = lax.ppermute(rows, BOTH, hop(sections, step, n_ctx))
    return (rows, *edges(rows, 0, BLK, n_ctx))


def edges(block, dim, width, n_ctx):
    size = block.shape[dim]
    tail = lax.slice_in_dim(block, size - width, size, axis=dim)
    head = lax.slice_in_dim(block, 0, width, axis=dim)
    from_left = lax.ppermute(tail, "ctx", neighbours(n_ctx, 1))
    from_right = lax.ppermute(head, "ctx", neighbours(n_ctx, -1))
    return from_left, from_right


def allowed_keys(block_mask, place, n_ctx):
    block_ids = place * BLOCKS_DEV + jnp.arange(BLOCKS_DEV)
    mask = block_mask.astype(F32)
    left = mask[:, :, 0] * (block_ids > 0).astype(F32)
    right = mask[:, :, 1] * (block_ids < BLOCKS_DEV * n_ctx - 1).astype(F32)
    return jnp.stack([left, jnp.ones_like(left), right], axis=2)


def key_weights(before, allow, after):
    allow = jnp.concatenate([before, allow, after], axis=1)
    allow = jnp.repeat(allow, BLK, axis=1)
    block = jnp.arange(EXT) // BLK
    offset = block[None, :] - block[:, None] + 1
    return sum(
        jnp.where(offset == side, allow[:, :, side : side + 1], 0.0) for side in range(3)
    )


def per_device(section_input, cotangent, w_query, w_key, w_value, w_out, block_mask):
    n_section = lax.axis_size("section")
    n_ctx = lax.axis_size("ctx")
    section = lax.axis_index("section")
    place = lax.axis_index("ctx")
    micro = section_input.shape[0]
    steps = n_section + micro - 1

    shard = jnp.concatenate(
        [w_query[0], w_key[0], w_value[0], w_out[0][:, :WIDTH], w_out[0][:, WIDTH:]], axis=0
    )
    gathered = lax.all_gather(shard, "ctx", axis=0, tiled=False)
    position = jnp.full((1,), section, jnp.int32)
    reverse = n_section - 1 - position
    allow = allowed_keys(block_mask, place, n_ctx)
    fields = jnp.stack([section_input, cotangent])

    def packed(part, block):
        lanes = jnp.pad(part.reshape(1, -1), ((0, 15), (0, D - part.size)))
        return jnp.concatenate([block.reshape(-1, D), lanes.astype(BF16)], axis=0)

    pieces = jnp.concatenate(
        [packed(allow[:, :1], fields[:, :, :BLK]), packed(allow[:, -1:], fields[:, :, -BLK:])]
    )
    size = pieces.shape[0] // 2
    before, after = edges(pieces, 0, size, n_ctx)

    def unpacked(piece):
        block = piece[: size - 16].reshape(2, micro, BLK, D)
        return block, piece[size - 16, : 3 * micro].astype(F32).reshape(micro, 1, 3)

    before, before_allow = unpacked(before)
    after, after_allow = unpacked(after)
    extended = jnp.concatenate([before, fields, after], axis=2)
    mask = key_weights(before_allow, allow, after_allow)
    forward_mask = mask[:, BLK : BLK + ROWS]
    weights = load_call(gathered)

    saved = (
        jnp.zeros((micro, ROWS, D), BF16),
        jnp.zeros((micro, ROWS, D), BF16),
        jnp.zeros((micro, ROWS, PACK), BF16),
        jnp.zeros((micro, EXT, 2 * WIDTH), BF16),
        jnp.zeros((micro, ROWS, 128), F32),
    )
    zero_rows = jnp.zeros((ROWS, D), BF16)
    zero_edge = jnp.zeros((BLK, D), BF16)
    incoming = (zero_rows, zero_edge, zero_edge)
    for step in range(steps):
        rows, saved = forward_call(
            step, position, extended[0], *incoming, forward_mask, weights, saved
        )
        senders = [s for s in range(step - micro + 1, step + 1) if 0 <= s < n_section - 1]
        if senders:
            incoming = relay(rows, senders, 1, n_ctx)
    xs, outputs, qa, kv, rr = saved
    qa_left, qa_right = edges(qa, 1, BLK, n_ctx)
    grads = jnp.zeros((micro, ROWS, D), BF16)
    incoming = (zero_rows, zero_edge, zero_edge)
    for step in range(steps):
        rows, grads = backward_call(
            step,
            reverse,
            extended[1],
            *incoming,
            mask,
            weights,
            xs,
            qa,
            qa_left,
            qa_right,
            kv,
            rr,
            grads,
        )
        top = n_section - 1 - step
        senders = [s for s in range(top, top + micro) if 0 < s < n_section]
        if senders:
            incoming = relay(rows, senders, -1, n_ctx)
    return (outputs[None], grads[None])


def solution(mesh):
    return jax.shard_map(
        per_device,
        mesh=mesh,
        in_specs=(
            P(None, "ctx", None),
            P(None, "ctx", None),
            P("section", "ctx", None),
            P("section", "ctx", None),
            P("section", "ctx", None),
            P("section", "ctx", None),
            P(None, "ctx", None),
        ),
        out_specs=(P("section", None, "ctx", None), P("section", None, "ctx", None)),
        check_vma=False,
    )
```

```python
import functools

import jax
import jax.numpy as jnp
from jax import lax
from jax.experimental import pallas as pl
from jax.experimental.pallas import tpu as pltpu
from jax.sharding import PartitionSpec as P

D = 2048
HEADS = 8
HDIM = 128
BLOCKS_DEV = 4
BLK = 32
MICRO = 2
ROWS = BLK * BLOCKS_DEV
EXT = ROWS + 2 * BLK
WIDTH = HEADS * HDIM
PACK = 2 * WIDTH + 128
EPS = 1e-06
VMEM_LIMIT = 16 << 20
SCALE = HDIM ** (-0.5)
F32 = jnp.float32
BF16 = jnp.bfloat16

NT = (((1,), (1,)), ((), ()))
NN = (((1,), (0,)), ((), ()))
TN = (((0,), (0,)), ((), ()))


def dot(a, b, dims=NN):
    return lax.dot_general(a, b, dims, preferred_element_type=F32)


def wtile(w_ref, row, count, col, width):
    tile = w_ref[:, row : row + count, col : col + width]
    return tile.reshape(tile.shape[0] * count, width)


def schedule(step, position):
    micro_id = step - position
    active = (micro_id >= 0) & (micro_id < MICRO)
    return active, jnp.clip(micro_id, 0, MICRO - 1), position == 0


def forward_body(
    step,
    section_ref,
    x0_ref,
    x_ref,
    xl_ref,
    xr_ref,
    mask_ref,
    w_ref,
    xs_in,
    out_in,
    qa_in,
    kv_in,
    rr_in,
    next_ref,
    left_ref,
    right_ref,
    xs_ref,
    out_ref,
    qa_ref,
    kv_ref,
    rr_ref,
    xe,
    normed,
    qa,
    kv,
    rr,
    result,
    inverse,
    mask,
    sem_in,
    sem_out,
):
    active, slot, first = schedule(step, section_ref[0])

    @pl.when(active)
    def _():
        mask_copy = pltpu.make_async_copy(mask_ref.at[slot], mask, sem_in.at[3])
        mask_copy.start()

        @pl.when(first)
        def _():
            copy = pltpu.make_async_copy(x0_ref.at[slot], xe, sem_in.at[0])
            copy.start()
            copy.wait()

        @pl.when(jnp.logical_not(first))
        def _():
            copies = [
                pltpu.make_async_copy(xl_ref, xe.at[:BLK], sem_in.at[0]),
                pltpu.make_async_copy(x_ref, xe.at[BLK : BLK + ROWS], sem_in.at[1]),
                pltpu.make_async_copy(xr_ref, xe.at[BLK + ROWS :], sem_in.at[2]),
            ]
            for copy in copies:
                copy.start()
            for copy in copies:
                copy.wait()

        saves = [pltpu.make_async_copy(xe.at[BLK : BLK + ROWS], xs_ref.at[slot], sem_out.at[0])]
        saves[0].start()

        @pl.loop(0, EXT // BLK)
        def _(block):
            at = pl.ds(pl.multiple_of(block * BLK, BLK), BLK)
            rows = xe[at].astype(F32)
            scale = lax.rsqrt(jnp.mean(rows * rows, axis=-1, keepdims=True) + EPS)
            normed[at] = (rows * scale).astype(BF16)

        rr[...] = jnp.zeros((ROWS, 128), F32)
        inverse[...] = jnp.zeros((ROWS, 128), F32)
        mask_copy.wait()

        @pl.loop(0, 2)
        def _(pair):
            lane = lax.broadcasted_iota(jnp.int32, (ROWS, 128), 1)
            tile = pl.ds(pl.multiple_of(pair * 512, 512), 512)
            queries = dot(normed[BLK : BLK + ROWS], w_ref[:, 0:64, tile].reshape(D, 512))
            keys = dot(normed[...], w_ref[:, 64:128, tile].reshape(D, 512))
            values = dot(normed[...], w_ref[:, 128:192, tile].reshape(D, 512))
            for half in range(4):
                head = pair * 4 + half
                cols = slice(half * HDIM, (half + 1) * HDIM)
                at = pl.ds(pl.multiple_of(head * HDIM, HDIM), HDIM)
                beyond = pl.ds(pl.multiple_of(WIDTH + head * HDIM, HDIM), HDIM)
                query, key, value = queries[:, cols], keys[:, cols], values[:, cols]
                rq = lax.rsqrt(jnp.mean(query * query, axis=-1, keepdims=True) + EPS)
                rk = lax.rsqrt(jnp.mean(key * key, axis=-1, keepdims=True) + EPS)
                query = (query * rq).astype(BF16)
                key = (key * rk).astype(BF16)
                value = value.astype(BF16)
                probs = jnp.exp(dot(query, key, NT) * SCALE) * mask[...]
                inv = 1.0 / jnp.sum(probs, axis=-1, keepdims=True)
                attended = dot(probs.astype(BF16), value) * inv
                qa[:, at] = query
                qa[:, beyond] = attended.astype(BF16)
                kv[:, at] = key
                kv[:, beyond] = value
                high = inv.astype(BF16).astype(F32)
                stored = jnp.where(lane == head, rq, rr[...])
                rr[...] = jnp.where(lane == HEADS + head, rk[BLK : BLK + ROWS], stored)
                stored = jnp.where(lane == head, high, inverse[...])
                inverse[...] = jnp.where(lane == HEADS + head, inv - high, stored)

        qa[:, 2 * WIDTH :] = inverse[...].astype(BF16)
        for index, (source, target) in enumerate(((qa, qa_ref), (kv, kv_ref), (rr, rr_ref))):
            copy = pltpu.make_async_copy(source, target.at[slot], sem_out.at[1 + index])
            copy.start()
            saves.append(copy)

        for half in range(2):
            @pl.loop(0, 2)
            def _(tile):
                source = pl.ds(pl.multiple_of(tile * 512, 512), 512)
                cols = pl.ds(pl.multiple_of(half * 1024 + tile * 512, 512), 512)
                low = 192 + 32 * half
                weight = w_ref[:, low : low + 32, source].reshape(WIDTH, 512)
                update = dot(qa[:, WIDTH : 2 * WIDTH], weight)
                result[:, cols] = (xe[BLK : BLK + ROWS, cols].astype(F32) + update).astype(BF16)

        for index, (source, target) in enumerate(
            (
                (result, next_ref),
                (result.at[:BLK], left_ref),
                (result.at[ROWS - BLK :], right_ref),
                (result, out_ref.at[slot]),
            )
        ):
            copy = pltpu.make_async_copy(source, target, sem_out.at[4 + index])
            copy.start()
            saves.append(copy)
        for copy in saves:
            copy.wait()


def spaces(*names):
    table = dict(s=pltpu.SMEM, v=pltpu.VMEM, a=pltpu.HBM)
    return [pl.BlockSpec(memory_space=table[n]) for n in names]


def shape_of(a):
    return jax.ShapeDtypeStruct(a.shape, a.dtype)


def forward_call(step, position, x0, x, xl, xr, mask, w, saved):
    rows = jax.ShapeDtypeStruct((ROWS, D), BF16)
    edge = jax.ShapeDtypeStruct((BLK, D), BF16)
    outs = pl.pallas_call(
        functools.partial(forward_body, step),
        name="forward_layer",
        out_shape=(rows, edge, edge) + tuple(shape_of(a) for a in saved),
        in_specs=spaces(*"saaaaavaaaaa"),
        out_specs=spaces(*"aaaaaaaa"),
        scratch_shapes=[
            pltpu.VMEM((EXT, D), BF16),
            pltpu.VMEM((EXT, D), BF16),
            pltpu.VMEM((ROWS, PACK), BF16),
            pltpu.VMEM((EXT, 2 * WIDTH), BF16),
            pltpu.VMEM((ROWS, 128), F32),
            pltpu.VMEM((ROWS, D), BF16),
            pltpu.VMEM((ROWS, 128), F32),
            pltpu.VMEM((ROWS, EXT), F32),
            pltpu.SemaphoreType.DMA((4,)),
            pltpu.SemaphoreType.DMA((8,)),
        ],
        input_output_aliases={7: 3, 8: 4, 9: 5, 10: 6, 11: 7},
        compiler_params=pltpu.CompilerParams(vmem_limit_bytes=VMEM_LIMIT),
    )(position, x0, x, xl, xr, mask, w, *saved)
    return outs[:3], outs[3:]

def load_body(g_ref, w_ref, sem):
    copy = pltpu.make_async_copy(g_ref, w_ref, sem)
    copy.start()
    copy.wait()


def load_call(g):
    return pl.pallas_call(
        load_body,
        name="load_weights",
        out_shape=pltpu.VMEM(g.shape, g.dtype),
        in_specs=spaces("a"),
        out_specs=pl.BlockSpec(memory_space=pltpu.VMEM),
        scratch_shapes=[pltpu.SemaphoreType.DMA],
        compiler_params=pltpu.CompilerParams(vmem_limit_bytes=20 << 20),
    )(g)


def backward_body(
    step,
    section_ref,
    c0_ref,
    g_ref,
    gl_ref,
    gr_ref,
    mask_ref,
    w_ref,
    xs_ref,
    qa_ref,
    qal_ref,
    qar_ref,
    kv_ref,
    rr_ref,
    grad_in,
    next_ref,
    left_ref,
    right_ref,
    grad_ref,
    ge,
    xs,
    qa,
    kv,
    rr,
    dz,
    dn,
    result,
    mask,
    inner_ref,
    sem_in,
    sem_save,
    sem_out,
):
    active, slot, last = schedule(step, section_ref[0])
    own = slice(BLK, BLK + ROWS)

    @pl.when(active)
    def _():
        loads = [
            pltpu.make_async_copy(source.at[slot], target, sem_save.at[index])
            for index, (source, target) in enumerate(
                (
                    (qal_ref, qa.at[:BLK]),
                    (qa_ref, qa.at[own]),
                    (qar_ref, qa.at[BLK + ROWS :]),
                    (kv_ref, kv),
                    (rr_ref, rr),
                    (xs_ref, xs),
                    (mask_ref, mask),
                )
            )
        ]

        @pl.when(last)
        def _():
            copy = pltpu.make_async_copy(c0_ref.at[slot], ge, sem_in.at[0])
            copy.start()
            for load in loads:
                load.start()
            copy.wait()

        @pl.when(jnp.logical_not(last))
        def _():
            copies = [
                pltpu.make_async_copy(gl_ref, ge.at[:BLK], sem_in.at[0]),
                pltpu.make_async_copy(g_ref, ge.at[own], sem_in.at[1]),
                pltpu.make_async_copy(gr_ref, ge.at[BLK + ROWS :], sem_in.at[2]),
            ]
            for copy in copies:
                copy.start()
            for load in loads:
                load.start()
            for copy in copies:
                copy.wait()

        for load in loads:
            load.wait()

        @pl.loop(0, 2)
        def _(pair):
            lane = lax.broadcasted_iota(jnp.int32, (EXT, 128), 1)
            rows = pl.ds(pl.multiple_of(16 * pair, 16), 16)
            low = w_ref[rows, 192:224, :].reshape(512, 1024)
            high = w_ref[rows, 224:256, :].reshape(512, 1024)
            spread = dot(ge[:, :1024], low, NT) + dot(ge[:, 1024:], high, NT)
            for half in range(4):
                head = pair * 4 + half
                at = pl.ds(pl.multiple_of(head * HDIM, HDIM), HDIM)
                beyond = pl.ds(pl.multiple_of(WIDTH + head * HDIM, HDIM), HDIM)
                third = pl.ds(pl.multiple_of(2 * WIDTH + head * HDIM, HDIM), HDIM)
                d_att = spread[:, half * HDIM : (half + 1) * HDIM].astype(BF16).astype(F32)
                query, key, value = qa[:, at], kv[:, at], kv[:, beyond]
                picked = (lane == head) | (lane == HEADS + head)
                inv = jnp.sum(
                    jnp.where(picked, qa[:, 2 * WIDTH :].astype(F32), 0.0),
                    axis=-1,
                    keepdims=True,
                )
                d_sum = (d_att * inv).astype(BF16)
                d_total = -inv * jnp.sum(
                    d_att * qa[:, beyond].astype(F32), axis=-1, keepdims=True
                )
                probs = jnp.exp(dot(query, key, NT) * SCALE) * mask[...]
                d_probs = dot(d_sum, value, NT)
                d_scores = (probs * (d_probs + d_total) * SCALE).astype(BF16)
                d_value = dot(probs.astype(BF16), d_sum, TN)[own]
                d_key = dot(d_scores, query, TN)[own]
                d_query = dot(d_scores[own], key)

                def unnorm(grad, unit, which):
                    grad = grad.astype(BF16).astype(F32)
                    unit = unit.astype(F32)
                    r = jnp.sum(
                        jnp.where(lane[:ROWS] == which, rr[...], 0.0), axis=-1, keepdims=True
                    )
                    return r * (grad - unit * jnp.mean(grad * unit, axis=-1, keepdims=True))

                dz[:, at] = unnorm(d_query, query[own], head).astype(BF16)
                dz[:, beyond] = unnorm(d_key, key[own], HEADS + head).astype(BF16)
                dz[:, third] = d_value.astype(BF16)

        inner_ref[...] = jnp.zeros((ROWS, 128), F32)

        @pl.loop(0, 4)
        def _(tile):
            rows = pl.ds(pl.multiple_of(8 * tile, 8), 8)
            cols = pl.ds(pl.multiple_of(tile * 512, 512), 512)
            grad = jnp.zeros((ROWS, 512), F32)
            for part in range(3):
                weight = w_ref[rows, 64 * part : 64 * part + 64, :].reshape(512, WIDTH)
                grad += dot(dz[:, part * WIDTH : (part + 1) * WIDTH], weight, NT)
            grad = grad.astype(BF16).astype(F32)
            dn[:, cols] = grad
            product = grad * xs[:, cols].astype(F32)
            inner_ref[...] += (product[:, :128] + product[:, 128:256]) + (product[:, 256:384] + product[:, 384:])

        @pl.loop(0, ROWS // BLK)
        def _(block):
            at = pl.ds(pl.multiple_of(block * BLK, BLK), BLK)
            x = xs[at].astype(F32)
            scale = lax.rsqrt(jnp.mean(x * x, axis=-1, keepdims=True) + EPS)
            inner = jnp.sum(inner_ref[at], axis=-1, keepdims=True) * scale * scale * (1.0 / D)
            through = ge[pl.ds(pl.multiple_of(block * BLK + BLK, BLK), BLK)].astype(F32)
            result[at] = (through + scale * (dn[at] - x * inner)).astype(BF16)

        saves = [
            pltpu.make_async_copy(source, target, sem_out.at[index])
            for index, (source, target) in enumerate(
                (
                    (result, next_ref),
                (result.at[:BLK], left_ref),
                (result.at[ROWS - BLK :], right_ref),
                    (result, grad_ref.at[slot]),
                )
            )
        ]
        for copy in saves:
            copy.start()
        for copy in saves:
            copy.wait()


def backward_call(step, position, c0, g, gl, gr, mask, w, xs, qa, qal, qar, kv, rr, grads):
    rows = jax.ShapeDtypeStruct((ROWS, D), BF16)
    edge = jax.ShapeDtypeStruct((BLK, D), BF16)
    outs = pl.pallas_call(
        functools.partial(backward_body, step),
        name="backward_layer",
        out_shape=(rows, edge, edge, shape_of(grads)),
        in_specs=spaces(*"saaaaavaaaaaaa"),
        out_specs=spaces(*"aaaa"),
        scratch_shapes=[
            pltpu.VMEM((EXT, D), BF16),
            pltpu.VMEM((ROWS, D), BF16),
            pltpu.VMEM((EXT, PACK), BF16),
            pltpu.VMEM((EXT, 2 * WIDTH), BF16),
            pltpu.VMEM((ROWS, 128), F32),
            pltpu.VMEM((ROWS, 3 * WIDTH), BF16),
            pltpu.VMEM((ROWS, D), F32),
            pltpu.VMEM((ROWS, D), BF16),
            pltpu.VMEM((EXT, EXT), F32),
            pltpu.VMEM((ROWS, 128), F32),
            pltpu.SemaphoreType.DMA((3,)),
            pltpu.SemaphoreType.DMA((7,)),
            pltpu.SemaphoreType.DMA((4,)),
        ],
        input_output_aliases={13: 3},
        compiler_params=pltpu.CompilerParams(vmem_limit_bytes=VMEM_LIMIT),
    )(position, c0, g, gl, gr, mask, w, xs, qa, qal, qar, kv, rr, grads)
    return outs[:3], outs[3]

BOTH = ("section", "ctx")


def neighbours(n_ctx, distance):
    return [(c, c + distance) for c in range(n_ctx) if 0 <= c + distance < n_ctx]


def hop(sections, step, n_ctx):
    return [(s * n_ctx + c, (s + step) * n_ctx + c) for s in sections for c in range(n_ctx)]


def diagonal(n_section, step, n_ctx, distance):
    return [
        (s * n_ctx + source, (s + step) * n_ctx + target)
        for s in range(n_section)
        if 0 <= s + step < n_section
        for source, target in neighbours(n_ctx, distance)
    ]


def relay(parts, sections, step, n_section, n_ctx):
    rows, left, right = parts
    rows = lax.ppermute(rows, BOTH, hop(sections, step, n_ctx))
    from_left = lax.ppermute(right, BOTH, diagonal(n_section, step, n_ctx, 1))
    from_right = lax.ppermute(left, BOTH, diagonal(n_section, step, n_ctx, -1))
    return rows, from_left, from_right


def edges(block, dim, width, n_ctx):
    size = block.shape[dim]
    tail = lax.slice_in_dim(block, size - width, size, axis=dim)
    head = lax.slice_in_dim(block, 0, width, axis=dim)
    from_left = lax.ppermute(tail, "ctx", neighbours(n_ctx, 1))
    from_right = lax.ppermute(head, "ctx", neighbours(n_ctx, -1))
    return from_left, from_right


def allowed_keys(block_mask, place, n_ctx):
    block_ids = place * BLOCKS_DEV + jnp.arange(BLOCKS_DEV)
    mask = block_mask.astype(F32)
    left = mask[:, :, 0] * (block_ids > 0).astype(F32)
    right = mask[:, :, 1] * (block_ids < BLOCKS_DEV * n_ctx - 1).astype(F32)
    return jnp.stack([left, jnp.ones_like(left), right], axis=2)


def key_weights(before, allow, after):
    allow = jnp.concatenate([before, allow, after], axis=1)
    allow = jnp.repeat(allow, BLK, axis=1)
    block = jnp.arange(EXT) // BLK
    offset = block[None, :] - block[:, None] + 1
    return sum(
        jnp.where(offset == side, allow[:, :, side : side + 1], 0.0) for side in range(3)
    )


def per_device(section_input, cotangent, w_query, w_key, w_value, w_out, block_mask):
    n_section = lax.axis_size("section")
    n_ctx = lax.axis_size("ctx")
    section = lax.axis_index("section")
    place = lax.axis_index("ctx")
    micro = section_input.shape[0]
    steps = n_section + micro - 1

    shard = jnp.concatenate(
        [w_query[0], w_key[0], w_value[0], w_out[0][:, :WIDTH], w_out[0][:, WIDTH:]], axis=0
    )
    gathered = lax.all_gather(shard, "ctx", axis=0, tiled=False)
    position = jnp.full((1,), section, jnp.int32)
    reverse = n_section - 1 - position
    allow = allowed_keys(block_mask, place, n_ctx)
    fields = jnp.stack([section_input, cotangent])

    def packed(part, block):
        lanes = jnp.pad(part.reshape(1, -1), ((0, 15), (0, D - part.size)))
        return jnp.concatenate([block.reshape(-1, D), lanes.astype(BF16)], axis=0)

    pieces = jnp.concatenate(
        [packed(allow[:, :1], fields[:, :, :BLK]), packed(allow[:, -1:], fields[:, :, -BLK:])]
    )
    size = pieces.shape[0] // 2
    before, after = edges(pieces, 0, size, n_ctx)

    def unpacked(piece):
        block = piece[: size - 16].reshape(2, micro, BLK, D)
        return block, piece[size - 16, : 3 * micro].astype(F32).reshape(micro, 1, 3)

    before, before_allow = unpacked(before)
    after, after_allow = unpacked(after)
    extended = jnp.concatenate([before, fields, after], axis=2)
    mask = key_weights(before_allow, allow, after_allow)
    forward_mask = mask[:, BLK : BLK + ROWS]
    weights = load_call(gathered)

    saved = (
        jnp.zeros((micro, ROWS, D), BF16),
        jnp.zeros((micro, ROWS, D), BF16),
        jnp.zeros((micro, ROWS, PACK), BF16),
        jnp.zeros((micro, EXT, 2 * WIDTH), BF16),
        jnp.zeros((micro, ROWS, 128), F32),
    )
    zero_rows = jnp.zeros((ROWS, D), BF16)
    zero_edge = jnp.zeros((BLK, D), BF16)
    incoming = (zero_rows, zero_edge, zero_edge)
    for step in range(steps):
        parts, saved = forward_call(
            step, position, extended[0], *incoming, forward_mask, weights, saved
        )
        senders = [s for s in range(step - micro + 1, step + 1) if 0 <= s < n_section - 1]
        if senders:
            incoming = relay(parts, senders, 1, n_section, n_ctx)
    xs, outputs, qa, kv, rr = saved
    qa_left, qa_right = edges(qa, 1, BLK, n_ctx)
    grads = jnp.zeros((micro, ROWS, D), BF16)
    incoming = (zero_rows, zero_edge, zero_edge)
    for step in range(steps):
        parts, grads = backward_call(
            step,
            reverse,
            extended[1],
            *incoming,
            mask,
            weights,
            xs,
            qa,
            qa_left,
            qa_right,
            kv,
            rr,
            grads,
        )
        top = n_section - 1 - step
        senders = [s for s in range(top, top + micro) if 0 < s < n_section]
        if senders:
            incoming = relay(parts, senders, -1, n_section, n_ctx)
    return (outputs[None], grads[None])


def solution(mesh):
    return jax.shard_map(
        per_device,
        mesh=mesh,
        in_specs=(
            P(None, "ctx", None),
            P(None, "ctx", None),
            P("section", "ctx", None),
            P("section", "ctx", None),
            P("section", "ctx", None),
            P("section", "ctx", None),
            P(None, "ctx", None),
        ),
        out_specs=(P("section", None, "ctx", None), P("section", None, "ctx", None)),
        check_vma=False,
    )
```

```python
import functools

import jax
import jax.numpy as jnp
from jax import lax
from jax.experimental import pallas as pl
from jax.experimental.pallas import tpu as pltpu
from jax.sharding import PartitionSpec as P

D = 2048
HEADS = 8
HDIM = 128
BLOCKS_DEV = 4
BLK = 32
MICRO = 2
ROWS = BLK * BLOCKS_DEV
EXT = ROWS + 2 * BLK
WIDTH = HEADS * HDIM
PACK = 2 * WIDTH + 128
EPS = 1e-06
VMEM_LIMIT = 16 << 20
SCALE = HDIM ** (-0.5)
F32 = jnp.float32
BF16 = jnp.bfloat16

NT = (((1,), (1,)), ((), ()))
NN = (((1,), (0,)), ((), ()))
TN = (((0,), (0,)), ((), ()))


def dot(a, b, dims=NN):
    return lax.dot_general(a, b, dims, preferred_element_type=F32)


def wtile(w_ref, row, count, col, width):
    tile = w_ref[:, row : row + count, col : col + width]
    return tile.reshape(tile.shape[0] * count, width)


def schedule(step, position):
    micro_id = step - position
    active = (micro_id >= 0) & (micro_id < MICRO)
    return active, jnp.clip(micro_id, 0, MICRO - 1), position == 0


def forward_body(
    step,
    section_ref,
    x0_ref,
    x_ref,
    xl_ref,
    xr_ref,
    mask_ref,
    w_ref,
    xs_in,
    out_in,
    qa_in,
    kv_in,
    rr_in,
    next_ref,
    left_ref,
    right_ref,
    xs_ref,
    out_ref,
    qa_ref,
    kv_ref,
    rr_ref,
    xe,
    normed,
    qa,
    kv,
    rr,
    result,
    inverse,
    mask,
    sem_in,
    sem_out,
):
    active, slot, first = schedule(step, section_ref[0])

    @pl.when(active)
    def _():
        mask_copy = pltpu.make_async_copy(mask_ref.at[slot], mask, sem_in.at[3])
        mask_copy.start()

        @pl.when(first)
        def _():
            copy = pltpu.make_async_copy(x0_ref.at[slot], xe, sem_in.at[0])
            copy.start()
            copy.wait()

        @pl.when(jnp.logical_not(first))
        def _():
            copies = [
                pltpu.make_async_copy(xl_ref, xe.at[:BLK], sem_in.at[0]),
                pltpu.make_async_copy(x_ref, xe.at[BLK : BLK + ROWS], sem_in.at[1]),
                pltpu.make_async_copy(xr_ref, xe.at[BLK + ROWS :], sem_in.at[2]),
            ]
            for copy in copies:
                copy.start()
            for copy in copies:
                copy.wait()

        saves = [pltpu.make_async_copy(xe.at[BLK : BLK + ROWS], xs_ref.at[slot], sem_out.at[0])]
        saves[0].start()

        @pl.loop(0, EXT // BLK)
        def _(block):
            at = pl.ds(pl.multiple_of(block * BLK, BLK), BLK)
            rows = xe[at].astype(F32)
            scale = lax.rsqrt(jnp.mean(rows * rows, axis=-1, keepdims=True) + EPS)
            normed[at] = (rows * scale).astype(BF16)

        rr[...] = jnp.zeros((ROWS, 128), F32)
        inverse[...] = jnp.zeros((ROWS, 128), F32)
        mask_copy.wait()

        @pl.loop(0, 2)
        def _(pair):
            lane = lax.broadcasted_iota(jnp.int32, (ROWS, 128), 1)
            tile = pl.ds(pl.multiple_of(pair * 512, 512), 512)
            queries = dot(normed[BLK : BLK + ROWS], w_ref[:, 0:64, tile].reshape(D, 512))
            keys = dot(normed[...], w_ref[:, 64:128, tile].reshape(D, 512))
            values = dot(normed[...], w_ref[:, 128:192, tile].reshape(D, 512))
            for half in range(4):
                head = pair * 4 + half
                cols = slice(half * HDIM, (half + 1) * HDIM)
                at = pl.ds(pl.multiple_of(head * HDIM, HDIM), HDIM)
                beyond = pl.ds(pl.multiple_of(WIDTH + head * HDIM, HDIM), HDIM)
                query, key, value = queries[:, cols], keys[:, cols], values[:, cols]
                rq = lax.rsqrt(jnp.mean(query * query, axis=-1, keepdims=True) + EPS)
                rk = lax.rsqrt(jnp.mean(key * key, axis=-1, keepdims=True) + EPS)
                query = (query * rq).astype(BF16)
                key = (key * rk).astype(BF16)
                value = value.astype(BF16)
                probs = jnp.exp(dot(query, key, NT) * SCALE) * mask[...]
                inv = 1.0 / jnp.sum(probs, axis=-1, keepdims=True)
                attended = dot(probs.astype(BF16), value) * inv
                qa[:, at] = query
                qa[:, beyond] = attended.astype(BF16)
                kv[:, at] = key
                kv[:, beyond] = value
                high = inv.astype(BF16).astype(F32)
                stored = jnp.where(lane == head, rq, rr[...])
                rr[...] = jnp.where(lane == HEADS + head, rk[BLK : BLK + ROWS], stored)
                stored = jnp.where(lane == head, high, inverse[...])
                inverse[...] = jnp.where(lane == HEADS + head, inv - high, stored)

        qa[:, 2 * WIDTH :] = inverse[...].astype(BF16)
        for index, (source, target) in enumerate(((qa, qa_ref), (kv, kv_ref), (rr, rr_ref))):
            copy = pltpu.make_async_copy(source, target.at[slot], sem_out.at[1 + index])
            copy.start()
            saves.append(copy)

        for half in range(2):
            @pl.loop(0, 2)
            def _(tile):
                source = pl.ds(pl.multiple_of(tile * 512, 512), 512)
                cols = pl.ds(pl.multiple_of(half * 1024 + tile * 512, 512), 512)
                low = 192 + 32 * half
                weight = w_ref[:, low : low + 32, source].reshape(WIDTH, 512)
                update = dot(qa[:, WIDTH : 2 * WIDTH], weight)
                result[:, cols] = (xe[BLK : BLK + ROWS, cols].astype(F32) + update).astype(BF16)

        for index, (source, target) in enumerate(
            (
                (result, next_ref),
                (result.at[:BLK], left_ref),
                (result.at[ROWS - BLK :], right_ref),
                (result, out_ref.at[slot]),
            )
        ):
            copy = pltpu.make_async_copy(source, target, sem_out.at[4 + index])
            copy.start()
            saves.append(copy)
        for copy in saves:
            copy.wait()


def spaces(*names):
    table = dict(s=pltpu.SMEM, v=pltpu.VMEM, a=pltpu.HBM)
    return [pl.BlockSpec(memory_space=table[n]) for n in names]


def shape_of(a):
    return jax.ShapeDtypeStruct(a.shape, a.dtype)


def fresh(body, position, count):
    def wrapped(*refs):
        return body(*refs[:position], *([None] * count), *refs[position:])

    return wrapped


def forward_call(step, position, x0, x, xl, xr, mask, w, saved, kinds):
    rows = jax.ShapeDtypeStruct((ROWS, D), BF16)
    edge = jax.ShapeDtypeStruct((BLK, D), BF16)
    body = functools.partial(forward_body, step)
    if not saved:
        body = fresh(body, 7, len(kinds))
    outs = pl.pallas_call(
        body,
        name="forward_layer",
        out_shape=(rows, edge, edge) + kinds,
        in_specs=spaces(*("saaaaav" + "a" * len(saved))),
        out_specs=spaces(*"aaaaaaaa"),
        scratch_shapes=[
            pltpu.VMEM((EXT, D), BF16),
            pltpu.VMEM((EXT, D), BF16),
            pltpu.VMEM((ROWS, PACK), BF16),
            pltpu.VMEM((EXT, 2 * WIDTH), BF16),
            pltpu.VMEM((ROWS, 128), F32),
            pltpu.VMEM((ROWS, D), BF16),
            pltpu.VMEM((ROWS, 128), F32),
            pltpu.VMEM((ROWS, EXT), F32),
            pltpu.SemaphoreType.DMA((4,)),
            pltpu.SemaphoreType.DMA((8,)),
        ],
        input_output_aliases={7 + i: 3 + i for i in range(len(saved))},
        compiler_params=pltpu.CompilerParams(vmem_limit_bytes=VMEM_LIMIT),
    )(position, x0, x, xl, xr, mask, w, *saved)
    return outs[:3], outs[3:]

def load_body(g_ref, w_ref, sem):
    copy = pltpu.make_async_copy(g_ref, w_ref, sem)
    copy.start()
    copy.wait()


def load_call(g):
    return pl.pallas_call(
        load_body,
        name="load_weights",
        out_shape=pltpu.VMEM(g.shape, g.dtype),
        in_specs=spaces("a"),
        out_specs=pl.BlockSpec(memory_space=pltpu.VMEM),
        scratch_shapes=[pltpu.SemaphoreType.DMA],
        compiler_params=pltpu.CompilerParams(vmem_limit_bytes=40 << 20),
    )(g)


def backward_body(
    step,
    section_ref,
    c0_ref,
    g_ref,
    gl_ref,
    gr_ref,
    mask_ref,
    w_ref,
    xs_ref,
    qa_ref,
    qal0_ref,
    qar0_ref,
    qal1_ref,
    qar1_ref,
    kv_ref,
    rr_ref,
    grad_in,
    next_ref,
    left_ref,
    right_ref,
    grad_ref,
    ge,
    xs,
    qa,
    kv,
    rr,
    dz,
    dn,
    result,
    mask,
    inner_ref,
    sem_in,
    sem_save,
    sem_out,
):
    active, slot, last = schedule(step, section_ref[0])
    own = slice(BLK, BLK + ROWS)

    @pl.when(active)
    def _():
        loads = [
            pltpu.make_async_copy(source.at[slot], target, sem_save.at[index])
            for index, (source, target) in enumerate(
                (
                    (qa_ref, qa.at[own]),
                    (kv_ref, kv),
                    (rr_ref, rr),
                    (xs_ref, xs),
                    (mask_ref, mask),
                )
            )
        ]

        def ends(left, right):
            return [
                pltpu.make_async_copy(left, qa.at[:BLK], sem_save.at[5]),
                pltpu.make_async_copy(right, qa.at[BLK + ROWS :], sem_save.at[6]),
            ]

        @pl.when(slot == 0)
        def _():
            for copy in ends(qal0_ref, qar0_ref):
                copy.start()

        @pl.when(slot == 1)
        def _():
            for copy in ends(qal1_ref, qar1_ref):
                copy.start()

        @pl.when(last)
        def _():
            copy = pltpu.make_async_copy(c0_ref.at[slot], ge, sem_in.at[0])
            copy.start()
            for load in loads:
                load.start()
            copy.wait()

        @pl.when(jnp.logical_not(last))
        def _():
            copies = [
                pltpu.make_async_copy(gl_ref, ge.at[:BLK], sem_in.at[0]),
                pltpu.make_async_copy(g_ref, ge.at[own], sem_in.at[1]),
                pltpu.make_async_copy(gr_ref, ge.at[BLK + ROWS :], sem_in.at[2]),
            ]
            for copy in copies:
                copy.start()
            for load in loads:
                load.start()
            for copy in copies:
                copy.wait()

        for load in loads + ends(qal0_ref, qar0_ref):
            load.wait()

        @pl.loop(0, 2)
        def _(pair):
            lane = lax.broadcasted_iota(jnp.int32, (EXT, 128), 1)
            rows = pl.ds(pl.multiple_of(16 * pair, 16), 16)
            low = w_ref[rows, 192:224, :].reshape(512, 1024)
            high = w_ref[rows, 224:256, :].reshape(512, 1024)
            spread = dot(ge[:, :1024], low, NT) + dot(ge[:, 1024:], high, NT)
            for half in range(4):
                head = pair * 4 + half
                at = pl.ds(pl.multiple_of(head * HDIM, HDIM), HDIM)
                beyond = pl.ds(pl.multiple_of(WIDTH + head * HDIM, HDIM), HDIM)
                third = pl.ds(pl.multiple_of(2 * WIDTH + head * HDIM, HDIM), HDIM)
                d_att = spread[:, half * HDIM : (half + 1) * HDIM].astype(BF16).astype(F32)
                query, key, value = qa[:, at], kv[:, at], kv[:, beyond]
                picked = (lane == head) | (lane == HEADS + head)
                inv = jnp.sum(
                    jnp.where(picked, qa[:, 2 * WIDTH :].astype(F32), 0.0),
                    axis=-1,
                    keepdims=True,
                )
                d_sum = (d_att * inv).astype(BF16)
                d_total = -inv * jnp.sum(
                    d_att * qa[:, beyond].astype(F32), axis=-1, keepdims=True
                )
                probs = jnp.exp(dot(query, key, NT) * SCALE) * mask[...]
                d_probs = dot(d_sum, value, NT)
                d_scores = (probs * (d_probs + d_total) * SCALE).astype(BF16)
                d_value = dot(probs.astype(BF16), d_sum, TN)[own]
                d_key = dot(d_scores, query, TN)[own]
                d_query = dot(d_scores[own], key)

                def unnorm(grad, unit, which):
                    grad = grad.astype(BF16).astype(F32)
                    unit = unit.astype(F32)
                    r = jnp.sum(
                        jnp.where(lane[:ROWS] == which, rr[...], 0.0), axis=-1, keepdims=True
                    )
                    return r * (grad - unit * jnp.mean(grad * unit, axis=-1, keepdims=True))

                dz[:, at] = unnorm(d_query, query[own], head).astype(BF16)
                dz[:, beyond] = unnorm(d_key, key[own], HEADS + head).astype(BF16)
                dz[:, third] = d_value.astype(BF16)

        inner_ref[...] = jnp.zeros((ROWS, 128), F32)

        @pl.loop(0, 4)
        def _(tile):
            rows = pl.ds(pl.multiple_of(8 * tile, 8), 8)
            cols = pl.ds(pl.multiple_of(tile * 512, 512), 512)
            grad = jnp.zeros((ROWS, 512), F32)
            for part in range(3):
                weight = w_ref[rows, 64 * part : 64 * part + 64, :].reshape(512, WIDTH)
                grad += dot(dz[:, part * WIDTH : (part + 1) * WIDTH], weight, NT)
            grad = grad.astype(BF16).astype(F32)
            dn[:, cols] = grad
            product = grad * xs[:, cols].astype(F32)
            inner_ref[...] += (product[:, :128] + product[:, 128:256]) + (product[:, 256:384] + product[:, 384:])

        @pl.loop(0, ROWS // BLK)
        def _(block):
            at = pl.ds(pl.multiple_of(block * BLK, BLK), BLK)
            x = xs[at].astype(F32)
            scale = lax.rsqrt(jnp.mean(x * x, axis=-1, keepdims=True) + EPS)
            inner = jnp.sum(inner_ref[at], axis=-1, keepdims=True) * scale * scale * (1.0 / D)
            through = ge[pl.ds(pl.multiple_of(block * BLK + BLK, BLK), BLK)].astype(F32)
            result[at] = (through + scale * (dn[at] - x * inner)).astype(BF16)

        saves = [
            pltpu.make_async_copy(source, target, sem_out.at[index])
            for index, (source, target) in enumerate(
                (
                    (result, next_ref),
                (result.at[:BLK], left_ref),
                (result.at[ROWS - BLK :], right_ref),
                    (result, grad_ref.at[slot]),
                )
            )
        ]
        for copy in saves:
            copy.start()
        for copy in saves:
            copy.wait()


def backward_call(step, position, c0, g, gl, gr, mask, w, xs, qa, ends, kv, rr, grads, kind):
    rows = jax.ShapeDtypeStruct((ROWS, D), BF16)
    edge = jax.ShapeDtypeStruct((BLK, D), BF16)
    body = functools.partial(backward_body, step)
    carried = () if grads is None else (grads,)
    if not carried:
        body = fresh(body, 15, 1)
    outs = pl.pallas_call(
        body,
        name="backward_layer",
        out_shape=(rows, edge, edge, kind),
        in_specs=spaces(*("saaaaav" + "a" * (8 + len(carried)))),
        out_specs=spaces(*"aaaa"),
        scratch_shapes=[
            pltpu.VMEM((EXT, D), BF16),
            pltpu.VMEM((ROWS, D), BF16),
            pltpu.VMEM((EXT, PACK), BF16),
            pltpu.VMEM((EXT, 2 * WIDTH), BF16),
            pltpu.VMEM((ROWS, 128), F32),
            pltpu.VMEM((ROWS, 3 * WIDTH), BF16),
            pltpu.VMEM((ROWS, D), F32),
            pltpu.VMEM((ROWS, D), BF16),
            pltpu.VMEM((EXT, EXT), F32),
            pltpu.VMEM((ROWS, 128), F32),
            pltpu.SemaphoreType.DMA((3,)),
            pltpu.SemaphoreType.DMA((7,)),
            pltpu.SemaphoreType.DMA((4,)),
        ],
        input_output_aliases={15: 3} if carried else {},
        compiler_params=pltpu.CompilerParams(vmem_limit_bytes=VMEM_LIMIT),
    )(position, c0, g, gl, gr, mask, w, xs, qa, *ends, kv, rr, *carried)
    return outs[:3], outs[3]


def pack_body(wq_ref, wk_ref, wv_ref, wo_ref, out_ref, sem):
    copies = [
        pltpu.make_async_copy(source, target, sem.at[index])
        for index, (source, target) in enumerate(
            (
                (wq_ref.at[0], out_ref.at[0:64]),
                (wk_ref.at[0], out_ref.at[64:128]),
                (wv_ref.at[0], out_ref.at[128:192]),
                (wo_ref.at[0, :, :WIDTH], out_ref.at[192:224]),
                (wo_ref.at[0, :, WIDTH:], out_ref.at[224:256]),
            )
        )
    ]
    for copy in copies:
        copy.start()
    for copy in copies:
        copy.wait()


def pack_call(*weights):
    return pl.pallas_call(
        pack_body,
        name="pack_weights",
        out_shape=jax.ShapeDtypeStruct((256, WIDTH), BF16),
        in_specs=spaces(*"aaaa"),
        out_specs=pl.BlockSpec(memory_space=pltpu.HBM),
        scratch_shapes=[pltpu.SemaphoreType.DMA((5,))],
    )(*weights)

BOTH = ("section", "ctx")


def neighbours(n_ctx, distance):
    return [(c, c + distance) for c in range(n_ctx) if 0 <= c + distance < n_ctx]


def hop(sections, step, n_ctx):
    return [(s * n_ctx + c, (s + step) * n_ctx + c) for s in sections for c in range(n_ctx)]


def diagonal(n_section, step, n_ctx, distance):
    return [
        (s * n_ctx + source, (s + step) * n_ctx + target)
        for s in range(n_section)
        if 0 <= s + step < n_section
        for source, target in neighbours(n_ctx, distance)
    ]


def relay(parts, sections, step, n_section, n_ctx):
    rows, left, right = parts
    rows = lax.ppermute(rows, BOTH, hop(sections, step, n_ctx))
    from_left = lax.ppermute(right, BOTH, diagonal(n_section, step, n_ctx, 1))
    from_right = lax.ppermute(left, BOTH, diagonal(n_section, step, n_ctx, -1))
    return rows, from_left, from_right


def edges(block, dim, width, n_ctx):
    size = block.shape[dim]
    tail = lax.slice_in_dim(block, size - width, size, axis=dim)
    head = lax.slice_in_dim(block, 0, width, axis=dim)
    from_left = lax.ppermute(tail, "ctx", neighbours(n_ctx, 1))
    from_right = lax.ppermute(head, "ctx", neighbours(n_ctx, -1))
    return from_left, from_right


def allowed_keys(block_mask, place, n_ctx):
    block_ids = place * BLOCKS_DEV + jnp.arange(BLOCKS_DEV)
    mask = block_mask.astype(F32)
    left = mask[:, :, 0] * (block_ids > 0).astype(F32)
    right = mask[:, :, 1] * (block_ids < BLOCKS_DEV * n_ctx - 1).astype(F32)
    return jnp.stack([left, jnp.ones_like(left), right], axis=2)


def key_weights(before, allow, after):
    allow = jnp.concatenate([before, allow, after], axis=1)
    allow = jnp.repeat(allow, BLK, axis=1)
    block = jnp.arange(EXT) // BLK
    offset = block[None, :] - block[:, None] + 1
    return sum(
        jnp.where(offset == side, allow[:, :, side : side + 1], 0.0) for side in range(3)
    )


def per_device(section_input, cotangent, w_query, w_key, w_value, w_out, block_mask):
    n_section = lax.axis_size("section")
    n_ctx = lax.axis_size("ctx")
    section = lax.axis_index("section")
    place = lax.axis_index("ctx")
    micro = section_input.shape[0]
    steps = n_section + micro - 1

    shard = pack_call(w_query, w_key, w_value, w_out)
    gathered = lax.all_gather(shard, "ctx", axis=0, tiled=False)
    position = jnp.full((1,), section, jnp.int32)
    reverse = n_section - 1 - position
    allow = allowed_keys(block_mask, place, n_ctx)
    fields = jnp.stack([section_input, cotangent])

    def packed(part, block):
        lanes = jnp.pad(part.reshape(1, -1), ((0, 15), (0, D - part.size)))
        return jnp.concatenate([block.reshape(-1, D), lanes.astype(BF16)], axis=0)

    pieces = jnp.concatenate(
        [packed(allow[:, :1], fields[:, :, :BLK]), packed(allow[:, -1:], fields[:, :, -BLK:])]
    )
    size = pieces.shape[0] // 2
    before, after = edges(pieces, 0, size, n_ctx)

    def unpacked(piece):
        block = piece[: size - 16].reshape(2, micro, BLK, D)
        return block, piece[size - 16, : 3 * micro].astype(F32).reshape(micro, 1, 3)

    before, before_allow = unpacked(before)
    after, after_allow = unpacked(after)
    extended = jnp.concatenate([before, fields, after], axis=2)
    mask = key_weights(before_allow, allow, after_allow)
    forward_mask = mask[:, BLK : BLK + ROWS]
    weights = load_call(gathered)

    kinds = (
        jax.ShapeDtypeStruct((micro, ROWS, D), BF16),
        jax.ShapeDtypeStruct((micro, ROWS, D), BF16),
        jax.ShapeDtypeStruct((micro, ROWS, PACK), BF16),
        jax.ShapeDtypeStruct((micro, EXT, 2 * WIDTH), BF16),
        jax.ShapeDtypeStruct((micro, ROWS, 128), F32),
    )
    zero_rows = jnp.zeros((ROWS, D), BF16)
    zero_edge = jnp.zeros((BLK, D), BF16)
    incoming = (zero_rows, zero_edge, zero_edge)

    def forward(step, incoming, saved):
        parts, saved = forward_call(
            step, position, extended[0], *incoming, forward_mask, weights, saved, kinds
        )
        senders = [s for s in range(step - micro + 1, step + 1) if 0 <= s < n_section - 1]
        if senders:
            incoming = relay(parts, senders, 1, n_section, n_ctx)
        return incoming, saved

    def backward(step, incoming, saved, ends, grads):
        xs, _, qa, kv, rr = saved
        parts, grads = backward_call(
            step, reverse, extended[1], *incoming, mask, weights, xs, qa, ends, kv, rr, grads, kinds[0]
        )
        top = n_section - 1 - step
        senders = [s for s in range(top, top + micro) if 0 < s < n_section]
        if senders:
            incoming = relay(parts, senders, -1, n_section, n_ctx)
        return incoming, grads

    saved = ()
    for step in range(n_section):
        incoming, saved = forward(step, incoming, saved)
    ends = edges(saved[2][0], 0, BLK, n_ctx)
    pulled, grads = backward(0, (zero_rows, zero_edge, zero_edge), saved, ends * 2, None)
    saved, grads = lax.optimization_barrier((saved, grads))
    for step in range(n_section, steps):
        incoming, saved = forward(step, incoming, saved)
    ends = ends + edges(saved[2][1], 0, BLK, n_ctx)
    for step in range(1, steps):
        pulled, grads = backward(step, pulled, saved, ends, grads)
    outputs = saved[1]
    return (outputs[None], grads[None])


def solution(mesh):
    return jax.shard_map(
        per_device,
        mesh=mesh,
        in_specs=(
            P(None, "ctx", None),
            P(None, "ctx", None),
            P("section", "ctx", None),
            P("section", "ctx", None),
            P("section", "ctx", None),
            P("section", "ctx", None),
            P(None, "ctx", None),
        ),
        out_specs=(P("section", None, "ctx", None), P("section", None, "ctx", None)),
        check_vma=False,
    )
```

```python
import functools

import jax
import jax.numpy as jnp
from jax import lax
from jax.experimental import pallas as pl
from jax.experimental.pallas import tpu as pltpu
from jax.sharding import PartitionSpec as P

D = 2048
HEADS = 8
HDIM = 128
BLOCKS_DEV = 4
BLK = 32
MICRO = 2
ROWS = BLK * BLOCKS_DEV
EXT = ROWS + 2 * BLK
WIDTH = HEADS * HDIM
PACK = 2 * WIDTH + 128
EPS = 1e-06
VMEM_LIMIT = 16 << 20
SCALE = HDIM ** (-0.5)
F32 = jnp.float32
BF16 = jnp.bfloat16

NT = (((1,), (1,)), ((), ()))
NN = (((1,), (0,)), ((), ()))
TN = (((0,), (0,)), ((), ()))


def dot(a, b, dims=NN):
    return lax.dot_general(a, b, dims, preferred_element_type=F32)


def wtile(w_ref, row, count, col, width):
    tile = w_ref[:, row : row + count, col : col + width]
    return tile.reshape(tile.shape[0] * count, width)


def schedule(step, position):
    micro_id = step - position
    active = (micro_id >= 0) & (micro_id < MICRO)
    return active, jnp.clip(micro_id, 0, MICRO - 1), position == 0


def forward_body(
    step,
    section_ref,
    x0_ref,
    x_ref,
    xl_ref,
    xr_ref,
    mask_ref,
    w_ref,
    xs_in,
    out_in,
    qa_in,
    kv_in,
    rr_in,
    next_ref,
    left_ref,
    right_ref,
    xs_ref,
    out_ref,
    qa_ref,
    kv_ref,
    rr_ref,
    xe,
    normed,
    qa,
    kv,
    rr,
    result,
    inverse,
    mask,
    sem_in,
    sem_out,
):
    active, slot, first = schedule(step, section_ref[0])

    @pl.when(active)
    def _():
        mask_copy = pltpu.make_async_copy(mask_ref.at[slot], mask, sem_in.at[3])
        mask_copy.start()

        @pl.when(first)
        def _():
            copy = pltpu.make_async_copy(x0_ref.at[slot], xe, sem_in.at[0])
            copy.start()
            copy.wait()

        @pl.when(jnp.logical_not(first))
        def _():
            copies = [
                pltpu.make_async_copy(xl_ref, xe.at[:BLK], sem_in.at[0]),
                pltpu.make_async_copy(x_ref, xe.at[BLK : BLK + ROWS], sem_in.at[1]),
                pltpu.make_async_copy(xr_ref, xe.at[BLK + ROWS :], sem_in.at[2]),
            ]
            for copy in copies:
                copy.start()
            for copy in copies:
                copy.wait()

        saves = [pltpu.make_async_copy(xe.at[BLK : BLK + ROWS], xs_ref.at[slot], sem_out.at[0])]
        saves[0].start()

        @pl.loop(0, EXT // BLK)
        def _(block):
            at = pl.ds(pl.multiple_of(block * BLK, BLK), BLK)
            rows = xe[at].astype(F32)
            scale = lax.rsqrt(jnp.mean(rows * rows, axis=-1, keepdims=True) + EPS)
            normed[at] = (rows * scale).astype(BF16)

        rr[...] = jnp.zeros((ROWS, 128), F32)
        inverse[...] = jnp.zeros((ROWS, 128), F32)
        mask_copy.wait()

        @pl.loop(0, 2)
        def _(pair):
            lane = lax.broadcasted_iota(jnp.int32, (ROWS, 128), 1)
            tile = pl.ds(pl.multiple_of(pair * 512, 512), 512)
            queries = dot(normed[BLK : BLK + ROWS], w_ref[:, 0:64, tile].reshape(D, 512))
            keys = dot(normed[...], w_ref[:, 64:128, tile].reshape(D, 512))
            values = dot(normed[...], w_ref[:, 128:192, tile].reshape(D, 512))
            for half in range(4):
                head = pair * 4 + half
                cols = slice(half * HDIM, (half + 1) * HDIM)
                at = pl.ds(pl.multiple_of(head * HDIM, HDIM), HDIM)
                beyond = pl.ds(pl.multiple_of(WIDTH + head * HDIM, HDIM), HDIM)
                query, key, value = queries[:, cols], keys[:, cols], values[:, cols]
                rq = lax.rsqrt(jnp.mean(query * query, axis=-1, keepdims=True) + EPS)
                rk = lax.rsqrt(jnp.mean(key * key, axis=-1, keepdims=True) + EPS)
                query = (query * rq).astype(BF16)
                key = (key * rk).astype(BF16)
                value = value.astype(BF16)
                probs = jnp.exp(dot(query, key, NT) * SCALE) * mask[...]
                inv = 1.0 / jnp.sum(probs, axis=-1, keepdims=True)
                attended = dot(probs.astype(BF16), value) * inv
                qa[:, at] = query
                qa[:, beyond] = attended.astype(BF16)
                kv[:, at] = key
                kv[:, beyond] = value
                high = inv.astype(BF16).astype(F32)
                stored = jnp.where(lane == head, rq, rr[...])
                rr[...] = jnp.where(lane == HEADS + head, rk[BLK : BLK + ROWS], stored)
                stored = jnp.where(lane == head, high, inverse[...])
                inverse[...] = jnp.where(lane == HEADS + head, inv - high, stored)

        qa[:, 2 * WIDTH :] = inverse[...].astype(BF16)
        for index, (source, target) in enumerate(((qa, qa_ref), (kv, kv_ref), (rr, rr_ref))):
            copy = pltpu.make_async_copy(source, target.at[slot], sem_out.at[1 + index])
            copy.start()
            saves.append(copy)

        for half in range(2):
            @pl.loop(0, 2)
            def _(tile):
                source = pl.ds(pl.multiple_of(tile * 512, 512), 512)
                cols = pl.ds(pl.multiple_of(half * 1024 + tile * 512, 512), 512)
                low = 192 + 32 * half
                weight = w_ref[:, low : low + 32, source].reshape(WIDTH, 512)
                update = dot(qa[:, WIDTH : 2 * WIDTH], weight)
                result[:, cols] = (xe[BLK : BLK + ROWS, cols].astype(F32) + update).astype(BF16)

        for index, (source, target) in enumerate(
            (
                (result, next_ref),
                (result.at[:BLK], left_ref),
                (result.at[ROWS - BLK :], right_ref),
                (result, out_ref.at[slot]),
            )
        ):
            copy = pltpu.make_async_copy(source, target, sem_out.at[4 + index])
            copy.start()
            saves.append(copy)
        for copy in saves:
            copy.wait()


def spaces(*names):
    table = dict(s=pltpu.SMEM, v=pltpu.VMEM, a=pltpu.HBM)
    return [pl.BlockSpec(memory_space=table[n]) for n in names]


def shape_of(a):
    return jax.ShapeDtypeStruct(a.shape, a.dtype)


def fresh(body, position, count):
    def wrapped(*refs):
        return body(*refs[:position], *([None] * count), *refs[position:])

    return wrapped


def forward_call(step, position, x0, x, xl, xr, mask, w, saved, kinds):
    rows = jax.ShapeDtypeStruct((ROWS, D), BF16)
    edge = jax.ShapeDtypeStruct((BLK, D), BF16)
    body = functools.partial(forward_body, step)
    if not saved:
        body = fresh(body, 7, len(kinds))
    outs = pl.pallas_call(
        body,
        name="forward_layer",
        out_shape=(rows, edge, edge) + kinds,
        in_specs=spaces(*("saaaaav" + "a" * len(saved))),
        out_specs=spaces(*"aaaaaaaa"),
        scratch_shapes=[
            pltpu.VMEM((EXT, D), BF16),
            pltpu.VMEM((EXT, D), BF16),
            pltpu.VMEM((ROWS, PACK), BF16),
            pltpu.VMEM((EXT, 2 * WIDTH), BF16),
            pltpu.VMEM((ROWS, 128), F32),
            pltpu.VMEM((ROWS, D), BF16),
            pltpu.VMEM((ROWS, 128), F32),
            pltpu.VMEM((ROWS, EXT), F32),
            pltpu.SemaphoreType.DMA((4,)),
            pltpu.SemaphoreType.DMA((8,)),
        ],
        input_output_aliases={7 + i: 3 + i for i in range(len(saved))},
        compiler_params=pltpu.CompilerParams(vmem_limit_bytes=VMEM_LIMIT),
    )(position, x0, x, xl, xr, mask, w, *saved)
    return outs[:3], outs[3:]

def load_body(g_ref, w_ref, sem):
    copy = pltpu.make_async_copy(g_ref, w_ref, sem)
    copy.start()
    copy.wait()


def load_call(g):
    return pl.pallas_call(
        load_body,
        name="load_weights",
        out_shape=pltpu.VMEM(g.shape, g.dtype),
        in_specs=spaces("a"),
        out_specs=pl.BlockSpec(memory_space=pltpu.VMEM),
        scratch_shapes=[pltpu.SemaphoreType.DMA],
        compiler_params=pltpu.CompilerParams(vmem_limit_bytes=40 << 20),
    )(g)


def backward_body(
    step,
    section_ref,
    c0_ref,
    g_ref,
    gl_ref,
    gr_ref,
    mask_ref,
    w_ref,
    xs_ref,
    qa_ref,
    qal0_ref,
    qar0_ref,
    qal1_ref,
    qar1_ref,
    kv_ref,
    rr_ref,
    grad_in,
    next_ref,
    left_ref,
    right_ref,
    grad_ref,
    ge,
    xs,
    qa,
    kv,
    rr,
    dz,
    dn,
    result,
    mask,
    inner_ref,
    sem_in,
    sem_save,
    sem_out,
):
    active, slot, last = schedule(step, section_ref[0])
    own = slice(BLK, BLK + ROWS)

    @pl.when(active)
    def _():
        loads = [
            pltpu.make_async_copy(source.at[slot], target, sem_save.at[index])
            for index, (source, target) in enumerate(
                (
                    (qa_ref, qa.at[own]),
                    (kv_ref, kv),
                    (rr_ref, rr),
                    (xs_ref, xs),
                    (mask_ref, mask),
                )
            )
        ]

        def ends(left, right):
            return [
                pltpu.make_async_copy(left, qa.at[:BLK], sem_save.at[5]),
                pltpu.make_async_copy(right, qa.at[BLK + ROWS :], sem_save.at[6]),
            ]

        @pl.when(slot == 0)
        def _():
            for copy in ends(qal0_ref, qar0_ref):
                copy.start()

        @pl.when(slot == 1)
        def _():
            for copy in ends(qal1_ref, qar1_ref):
                copy.start()

        @pl.when(last)
        def _():
            copy = pltpu.make_async_copy(c0_ref.at[slot], ge, sem_in.at[0])
            copy.start()
            for load in loads:
                load.start()
            copy.wait()

        @pl.when(jnp.logical_not(last))
        def _():
            copies = [
                pltpu.make_async_copy(gl_ref, ge.at[:BLK], sem_in.at[0]),
                pltpu.make_async_copy(g_ref, ge.at[own], sem_in.at[1]),
                pltpu.make_async_copy(gr_ref, ge.at[BLK + ROWS :], sem_in.at[2]),
            ]
            for copy in copies:
                copy.start()
            for load in loads:
                load.start()
            for copy in copies:
                copy.wait()

        for load in loads + ends(qal0_ref, qar0_ref):
            load.wait()

        @pl.loop(0, 2)
        def _(pair):
            lane = lax.broadcasted_iota(jnp.int32, (EXT, 128), 1)
            rows = pl.ds(pl.multiple_of(16 * pair, 16), 16)
            low = w_ref[rows, 192:224, :].reshape(512, 1024)
            high = w_ref[rows, 224:256, :].reshape(512, 1024)
            spread = dot(ge[:, :1024], low, NT) + dot(ge[:, 1024:], high, NT)
            for half in range(4):
                head = pair * 4 + half
                at = pl.ds(pl.multiple_of(head * HDIM, HDIM), HDIM)
                beyond = pl.ds(pl.multiple_of(WIDTH + head * HDIM, HDIM), HDIM)
                third = pl.ds(pl.multiple_of(2 * WIDTH + head * HDIM, HDIM), HDIM)
                d_att = spread[:, half * HDIM : (half + 1) * HDIM].astype(BF16).astype(F32)
                query, key, value = qa[:, at], kv[:, at], kv[:, beyond]
                picked = (lane == head) | (lane == HEADS + head)
                inv = jnp.sum(
                    jnp.where(picked, qa[:, 2 * WIDTH :].astype(F32), 0.0),
                    axis=-1,
                    keepdims=True,
                )
                d_sum = (d_att * inv).astype(BF16)
                d_total = -inv * jnp.sum(
                    d_att * qa[:, beyond].astype(F32), axis=-1, keepdims=True
                )
                probs = jnp.exp(dot(query, key, NT) * SCALE) * mask[...]
                d_probs = dot(d_sum, value, NT)
                d_scores = (probs * (d_probs + d_total) * SCALE).astype(BF16)
                d_value = dot(probs.astype(BF16), d_sum, TN)[own]
                d_key = dot(d_scores, query, TN)[own]
                d_query = dot(d_scores[own], key)

                def unnorm(grad, unit, which):
                    grad = grad.astype(BF16).astype(F32)
                    unit = unit.astype(F32)
                    r = jnp.sum(
                        jnp.where(lane[:ROWS] == which, rr[...], 0.0), axis=-1, keepdims=True
                    )
                    return r * (grad - unit * jnp.mean(grad * unit, axis=-1, keepdims=True))

                dz[:, at] = unnorm(d_query, query[own], head).astype(BF16)
                dz[:, beyond] = unnorm(d_key, key[own], HEADS + head).astype(BF16)
                dz[:, third] = d_value.astype(BF16)

        inner_ref[...] = jnp.zeros((ROWS, 128), F32)

        @pl.loop(0, 4)
        def _(tile):
            rows = pl.ds(pl.multiple_of(8 * tile, 8), 8)
            cols = pl.ds(pl.multiple_of(tile * 512, 512), 512)
            grad = jnp.zeros((ROWS, 512), F32)
            for part in range(3):
                weight = w_ref[rows, 64 * part : 64 * part + 64, :].reshape(512, WIDTH)
                grad += dot(dz[:, part * WIDTH : (part + 1) * WIDTH], weight, NT)
            grad = grad.astype(BF16).astype(F32)
            dn[:, cols] = grad
            product = grad * xs[:, cols].astype(F32)
            inner_ref[...] += (product[:, :128] + product[:, 128:256]) + (product[:, 256:384] + product[:, 384:])

        @pl.loop(0, ROWS // BLK)
        def _(block):
            at = pl.ds(pl.multiple_of(block * BLK, BLK), BLK)
            x = xs[at].astype(F32)
            scale = lax.rsqrt(jnp.mean(x * x, axis=-1, keepdims=True) + EPS)
            inner = jnp.sum(inner_ref[at], axis=-1, keepdims=True) * scale * scale * (1.0 / D)
            through = ge[pl.ds(pl.multiple_of(block * BLK + BLK, BLK), BLK)].astype(F32)
            result[at] = (through + scale * (dn[at] - x * inner)).astype(BF16)

        saves = [
            pltpu.make_async_copy(source, target, sem_out.at[index])
            for index, (source, target) in enumerate(
                (
                    (result, next_ref),
                (result.at[:BLK], left_ref),
                (result.at[ROWS - BLK :], right_ref),
                    (result, grad_ref.at[slot]),
                )
            )
        ]
        for copy in saves:
            copy.start()
        for copy in saves:
            copy.wait()


def backward_call(step, position, c0, g, gl, gr, mask, w, xs, qa, ends, kv, rr, grads, kind):
    rows = jax.ShapeDtypeStruct((ROWS, D), BF16)
    edge = jax.ShapeDtypeStruct((BLK, D), BF16)
    body = functools.partial(backward_body, step)
    carried = () if grads is None else (grads,)
    if not carried:
        body = fresh(body, 15, 1)
    outs = pl.pallas_call(
        body,
        name="backward_layer",
        out_shape=(rows, edge, edge, kind),
        in_specs=spaces(*("saaaaav" + "a" * (8 + len(carried)))),
        out_specs=spaces(*"aaaa"),
        scratch_shapes=[
            pltpu.VMEM((EXT, D), BF16),
            pltpu.VMEM((ROWS, D), BF16),
            pltpu.VMEM((EXT, PACK), BF16),
            pltpu.VMEM((EXT, 2 * WIDTH), BF16),
            pltpu.VMEM((ROWS, 128), F32),
            pltpu.VMEM((ROWS, 3 * WIDTH), BF16),
            pltpu.VMEM((ROWS, D), F32),
            pltpu.VMEM((ROWS, D), BF16),
            pltpu.VMEM((EXT, EXT), F32),
            pltpu.VMEM((ROWS, 128), F32),
            pltpu.SemaphoreType.DMA((3,)),
            pltpu.SemaphoreType.DMA((7,)),
            pltpu.SemaphoreType.DMA((4,)),
        ],
        input_output_aliases={15: 3} if carried else {},
        compiler_params=pltpu.CompilerParams(vmem_limit_bytes=VMEM_LIMIT),
    )(position, c0, g, gl, gr, mask, w, xs, qa, *ends, kv, rr, *carried)
    return outs[:3], outs[3]


def pack_body(wq_ref, wk_ref, wv_ref, wo_ref, out_ref):
    out_ref[0:64] = wq_ref[0]
    out_ref[64:128] = wk_ref[0]
    out_ref[128:192] = wv_ref[0]
    out_ref[192:224] = wo_ref[0, :, :WIDTH]
    out_ref[224:256] = wo_ref[0, :, WIDTH:]


def pack_call(*weights):
    return pl.pallas_call(
        pack_body,
        name="pack_weights",
        out_shape=jax.ShapeDtypeStruct((256, WIDTH), BF16),
        in_specs=spaces(*"vvvv"),
        out_specs=pl.BlockSpec(memory_space=pltpu.VMEM),
    )(*weights)

BOTH = ("section", "ctx")


def neighbours(n_ctx, distance):
    return [(c, c + distance) for c in range(n_ctx) if 0 <= c + distance < n_ctx]


def hop(sections, step, n_ctx):
    return [(s * n_ctx + c, (s + step) * n_ctx + c) for s in sections for c in range(n_ctx)]


def diagonal(n_section, step, n_ctx, distance):
    return [
        (s * n_ctx + source, (s + step) * n_ctx + target)
        for s in range(n_section)
        if 0 <= s + step < n_section
        for source, target in neighbours(n_ctx, distance)
    ]


def relay(parts, sections, step, n_section, n_ctx):
    rows, left, right = parts
    rows = lax.ppermute(rows, BOTH, hop(sections, step, n_ctx))
    from_left = lax.ppermute(right, BOTH, diagonal(n_section, step, n_ctx, 1))
    from_right = lax.ppermute(left, BOTH, diagonal(n_section, step, n_ctx, -1))
    return rows, from_left, from_right


def edges(block, dim, width, n_ctx):
    size = block.shape[dim]
    tail = lax.slice_in_dim(block, size - width, size, axis=dim)
    head = lax.slice_in_dim(block, 0, width, axis=dim)
    from_left = lax.ppermute(tail, "ctx", neighbours(n_ctx, 1))
    from_right = lax.ppermute(head, "ctx", neighbours(n_ctx, -1))
    return from_left, from_right


def allowed_keys(block_mask, place, n_ctx):
    block_ids = place * BLOCKS_DEV + jnp.arange(BLOCKS_DEV)
    mask = block_mask.astype(F32)
    left = mask[:, :, 0] * (block_ids > 0).astype(F32)
    right = mask[:, :, 1] * (block_ids < BLOCKS_DEV * n_ctx - 1).astype(F32)
    return jnp.stack([left, jnp.ones_like(left), right], axis=2)


def key_weights(before, allow, after):
    allow = jnp.concatenate([before, allow, after], axis=1)
    allow = jnp.repeat(allow, BLK, axis=1)
    block = jnp.arange(EXT) // BLK
    offset = block[None, :] - block[:, None] + 1
    return sum(
        jnp.where(offset == side, allow[:, :, side : side + 1], 0.0) for side in range(3)
    )


def per_device(section_input, cotangent, w_query, w_key, w_value, w_out, block_mask):
    n_section = lax.axis_size("section")
    n_ctx = lax.axis_size("ctx")
    section = lax.axis_index("section")
    place = lax.axis_index("ctx")
    micro = section_input.shape[0]
    steps = n_section + micro - 1

    shard = pack_call(w_query, w_key, w_value, w_out)
    gathered = lax.all_gather(shard, "ctx", axis=0, tiled=False)
    position = jnp.full((1,), section, jnp.int32)
    reverse = n_section - 1 - position
    allow = allowed_keys(block_mask, place, n_ctx)
    fields = jnp.stack([section_input, cotangent])

    def packed(part, block):
        lanes = jnp.pad(part.reshape(1, -1), ((0, 15), (0, D - part.size)))
        return jnp.concatenate([block.reshape(-1, D), lanes.astype(BF16)], axis=0)

    pieces = jnp.concatenate(
        [packed(allow[:, :1], fields[:, :, :BLK]), packed(allow[:, -1:], fields[:, :, -BLK:])]
    )
    size = pieces.shape[0] // 2
    before, after = edges(pieces, 0, size, n_ctx)

    def unpacked(piece):
        block = piece[: size - 16].reshape(2, micro, BLK, D)
        return block, piece[size - 16, : 3 * micro].astype(F32).reshape(micro, 1, 3)

    before, before_allow = unpacked(before)
    after, after_allow = unpacked(after)
    extended = jnp.concatenate([before, fields, after], axis=2)
    mask = key_weights(before_allow, allow, after_allow)
    forward_mask = mask[:, BLK : BLK + ROWS]
    weights = load_call(gathered)

    kinds = (
        jax.ShapeDtypeStruct((micro, ROWS, D), BF16),
        jax.ShapeDtypeStruct((micro, ROWS, D), BF16),
        jax.ShapeDtypeStruct((micro, ROWS, PACK), BF16),
        jax.ShapeDtypeStruct((micro, EXT, 2 * WIDTH), BF16),
        jax.ShapeDtypeStruct((micro, ROWS, 128), F32),
    )
    zero_rows = jnp.zeros((ROWS, D), BF16)
    zero_edge = jnp.zeros((BLK, D), BF16)
    incoming = (zero_rows, zero_edge, zero_edge)

    def forward(step, incoming, saved):
        parts, saved = forward_call(
            step, position, extended[0], *incoming, forward_mask, weights, saved, kinds
        )
        senders = [s for s in range(step - micro + 1, step + 1) if 0 <= s < n_section - 1]
        if senders:
            incoming = relay(parts, senders, 1, n_section, n_ctx)
        return incoming, saved

    def backward(step, incoming, saved, ends, grads):
        xs, _, qa, kv, rr = saved
        parts, grads = backward_call(
            step, reverse, extended[1], *incoming, mask, weights, xs, qa, ends, kv, rr, grads, kinds[0]
        )
        top = n_section - 1 - step
        senders = [s for s in range(top, top + micro) if 0 < s < n_section]
        if senders:
            incoming = relay(parts, senders, -1, n_section, n_ctx)
        return incoming, grads

    saved = ()
    for step in range(n_section):
        incoming, saved = forward(step, incoming, saved)
    ends = edges(saved[2][0], 0, BLK, n_ctx)
    pulled, grads = backward(0, (zero_rows, zero_edge, zero_edge), saved, ends * 2, None)
    saved, grads = lax.optimization_barrier((saved, grads))
    for step in range(n_section, steps):
        incoming, saved = forward(step, incoming, saved)
    ends = ends + edges(saved[2][1], 0, BLK, n_ctx)
    for step in range(1, steps):
        pulled, grads = backward(step, pulled, saved, ends, grads)
    outputs = saved[1]
    return (outputs[None], grads[None])


def solution(mesh):
    return jax.shard_map(
        per_device,
        mesh=mesh,
        in_specs=(
            P(None, "ctx", None),
            P(None, "ctx", None),
            P("section", "ctx", None),
            P("section", "ctx", None),
            P("section", "ctx", None),
            P("section", "ctx", None),
            P(None, "ctx", None),
        ),
        out_specs=(P("section", None, "ctx", None), P("section", None, "ctx", None)),
        check_vma=False,
    )
```

```python
import functools

import jax
import jax.numpy as jnp
from jax import lax
from jax.experimental import pallas as pl
from jax.experimental.pallas import tpu as pltpu
from jax.sharding import PartitionSpec as P

D = 2048
HEADS = 8
HDIM = 128
BLOCKS_DEV = 4
BLK = 32
MICRO = 2
ROWS = BLK * BLOCKS_DEV
EXT = ROWS + 2 * BLK
WIDTH = HEADS * HDIM
PACK = 2 * WIDTH + 128
EPS = 1e-06
VMEM_LIMIT = 16 << 20
SCALE = HDIM ** (-0.5)
F32 = jnp.float32
BF16 = jnp.bfloat16

NT = (((1,), (1,)), ((), ()))
NN = (((1,), (0,)), ((), ()))
TN = (((0,), (0,)), ((), ()))


def dot(a, b, dims=NN):
    return lax.dot_general(a, b, dims, preferred_element_type=F32)


def wtile(w_ref, row, count, col, width):
    tile = w_ref[:, row : row + count, col : col + width]
    return tile.reshape(tile.shape[0] * count, width)


def schedule(step, position):
    micro_id = step - position
    active = (micro_id >= 0) & (micro_id < MICRO)
    return active, jnp.clip(micro_id, 0, MICRO - 1), position == 0


def forward_body(
    step,
    section_ref,
    x0_ref,
    x_ref,
    xl_ref,
    xr_ref,
    mask_ref,
    w_ref,
    xs_in,
    out_in,
    qa_in,
    kv_in,
    rr_in,
    next_ref,
    left_ref,
    right_ref,
    xs_ref,
    out_ref,
    qa_ref,
    kv_ref,
    rr_ref,
    xe,
    normed,
    qa,
    kv,
    rr,
    result,
    inverse,
    mask,
    sem_in,
    sem_out,
):
    active, slot, first = schedule(step, section_ref[0])

    @pl.when(active)
    def _():
        mask_copy = pltpu.make_async_copy(mask_ref.at[slot], mask, sem_in.at[3])
        mask_copy.start()

        @pl.when(first)
        def _():
            copy = pltpu.make_async_copy(x0_ref.at[slot], xe, sem_in.at[0])
            copy.start()
            copy.wait()

        @pl.when(jnp.logical_not(first))
        def _():
            copies = [
                pltpu.make_async_copy(xl_ref, xe.at[:BLK], sem_in.at[0]),
                pltpu.make_async_copy(x_ref, xe.at[BLK : BLK + ROWS], sem_in.at[1]),
                pltpu.make_async_copy(xr_ref, xe.at[BLK + ROWS :], sem_in.at[2]),
            ]
            for copy in copies:
                copy.start()
            for copy in copies:
                copy.wait()

        saves = [pltpu.make_async_copy(xe.at[BLK : BLK + ROWS], xs_ref.at[slot], sem_out.at[0])]
        saves[0].start()

        @pl.loop(0, EXT // BLK)
        def _(block):
            at = pl.ds(pl.multiple_of(block * BLK, BLK), BLK)
            rows = xe[at].astype(F32)
            scale = lax.rsqrt(jnp.mean(rows * rows, axis=-1, keepdims=True) + EPS)
            normed[at] = (rows * scale).astype(BF16)

        rr[...] = jnp.zeros((ROWS, 128), F32)
        inverse[...] = jnp.zeros((ROWS, 128), F32)
        mask_copy.wait()

        @pl.loop(0, 2)
        def _(pair):
            lane = lax.broadcasted_iota(jnp.int32, (ROWS, 128), 1)
            tile = pl.ds(pl.multiple_of(pair * 512, 512), 512)
            queries = dot(normed[BLK : BLK + ROWS], w_ref[:, 0:64, tile].reshape(D, 512))
            keys = dot(normed[...], w_ref[:, 64:128, tile].reshape(D, 512))
            values = dot(normed[...], w_ref[:, 128:192, tile].reshape(D, 512))
            for half in range(4):
                head = pair * 4 + half
                cols = slice(half * HDIM, (half + 1) * HDIM)
                at = pl.ds(pl.multiple_of(head * HDIM, HDIM), HDIM)
                beyond = pl.ds(pl.multiple_of(WIDTH + head * HDIM, HDIM), HDIM)
                query, key, value = queries[:, cols], keys[:, cols], values[:, cols]
                rq = lax.rsqrt(jnp.mean(query * query, axis=-1, keepdims=True) + EPS)
                rk = lax.rsqrt(jnp.mean(key * key, axis=-1, keepdims=True) + EPS)
                query = (query * rq).astype(BF16)
                key = (key * rk).astype(BF16)
                value = value.astype(BF16)
                probs = jnp.exp(dot(query, key, NT) * SCALE) * mask[...]
                inv = 1.0 / jnp.sum(probs, axis=-1, keepdims=True)
                attended = dot(probs.astype(BF16), value) * inv
                qa[:, at] = query
                qa[:, beyond] = attended.astype(BF16)
                kv[:, at] = key
                kv[:, beyond] = value
                high = inv.astype(BF16).astype(F32)
                stored = jnp.where(lane == head, rq, rr[...])
                rr[...] = jnp.where(lane == HEADS + head, rk[BLK : BLK + ROWS], stored)
                stored = jnp.where(lane == head, high, inverse[...])
                inverse[...] = jnp.where(lane == HEADS + head, inv - high, stored)

        qa[:, 2 * WIDTH :] = inverse[...].astype(BF16)
        for index, (source, target) in enumerate(((qa, qa_ref), (kv, kv_ref), (rr, rr_ref))):
            copy = pltpu.make_async_copy(source, target.at[slot], sem_out.at[1 + index])
            copy.start()
            saves.append(copy)

        for half in range(2):
            @pl.loop(0, 2)
            def _(tile):
                source = pl.ds(pl.multiple_of(tile * 512, 512), 512)
                cols = pl.ds(pl.multiple_of(half * 1024 + tile * 512, 512), 512)
                low = 192 + 32 * half
                weight = w_ref[:, low : low + 32, source].reshape(WIDTH, 512)
                update = dot(qa[:, WIDTH : 2 * WIDTH], weight)
                result[:, cols] = (xe[BLK : BLK + ROWS, cols].astype(F32) + update).astype(BF16)

        for index, (source, target) in enumerate(
            (
                (result, next_ref),
                (result.at[:BLK], left_ref),
                (result.at[ROWS - BLK :], right_ref),
                (result, out_ref.at[slot]),
            )
        ):
            copy = pltpu.make_async_copy(source, target, sem_out.at[4 + index])
            copy.start()
            saves.append(copy)
        for copy in saves:
            copy.wait()


def spaces(*names):
    table = dict(s=pltpu.SMEM, v=pltpu.VMEM, a=pltpu.HBM)
    return [pl.BlockSpec(memory_space=table[n]) for n in names]


def shape_of(a):
    return jax.ShapeDtypeStruct(a.shape, a.dtype)


def fresh(body, position, count):
    def wrapped(*refs):
        return body(*refs[:position], *([None] * count), *refs[position:])

    return wrapped


def forward_call(step, position, x0, x, xl, xr, mask, w, saved, kinds):
    rows = jax.ShapeDtypeStruct((ROWS, D), BF16)
    edge = jax.ShapeDtypeStruct((BLK, D), BF16)
    body = functools.partial(forward_body, step)
    if not saved:
        body = fresh(body, 7, len(kinds))
    outs = pl.pallas_call(
        body,
        name="forward_layer",
        out_shape=(rows, edge, edge) + kinds,
        in_specs=spaces(*("saaaaav" + "a" * len(saved))),
        out_specs=spaces(*"aaaaaaaa"),
        scratch_shapes=[
            pltpu.VMEM((EXT, D), BF16),
            pltpu.VMEM((EXT, D), BF16),
            pltpu.VMEM((ROWS, PACK), BF16),
            pltpu.VMEM((EXT, 2 * WIDTH), BF16),
            pltpu.VMEM((ROWS, 128), F32),
            pltpu.VMEM((ROWS, D), BF16),
            pltpu.VMEM((ROWS, 128), F32),
            pltpu.VMEM((ROWS, EXT), F32),
            pltpu.SemaphoreType.DMA((4,)),
            pltpu.SemaphoreType.DMA((8,)),
        ],
        input_output_aliases={7 + i: 3 + i for i in range(len(saved))},
        compiler_params=pltpu.CompilerParams(vmem_limit_bytes=VMEM_LIMIT),
    )(position, x0, x, xl, xr, mask, w, *saved)
    return outs[:3], outs[3:]

ACROSS = 4
SPLIT = 112
REST = 256 - SPLIT
X_ORDER = (0, -1, 1, 2)
Z_ORDER = (0, -1, -2, -3, 4, 1, 2, 3)


def load_body(n_ctx, place_ref, *refs):
    sources, w_ref, sem = refs[:-2], refs[-2], refs[-1]
    depth = n_ctx // ACROSS
    z, x = place_ref[0] // ACROSS, lax.rem(place_ref[0], ACROSS)

    def owner(dx, dz):
        return lax.rem(z + dz + depth, depth) * ACROSS + lax.rem(x + dx + ACROSS, ACROSS)

    moves = []
    for ref, dz, blocks in zip(
        sources[:9],
        (0, -1, -2, -3, 4, 4, 1, 2, 3),
        (X_ORDER,) * 4 + (X_ORDER[:2], X_ORDER[2:]) + (X_ORDER,) * 3,
    ):
        for index, dx in enumerate(blocks):
            piece = ref.at[index * SPLIT : (index + 1) * SPLIT]
            moves.append((piece, w_ref.at[owner(dx, dz), 0:SPLIT]))
    for ref, dx, blocks in zip(
        sources[9:], (0, -1, 2, 2, 1), (Z_ORDER, Z_ORDER, Z_ORDER[:4], Z_ORDER[4:], Z_ORDER)
    ):
        for index, dz in enumerate(blocks):
            piece = ref.at[index * REST : (index + 1) * REST]
            moves.append((piece, w_ref.at[owner(dx, dz), SPLIT:256]))
    copies = [
        pltpu.make_async_copy(source, target, sem.at[index])
        for index, (source, target) in enumerate(moves)
    ]
    for copy in copies:
        copy.start()
    for copy in copies:
        copy.wait()


def load_call(place, n_ctx, pieces):
    return pl.pallas_call(
        functools.partial(load_body, n_ctx),
        name="load_weights",
        out_shape=pltpu.VMEM((n_ctx, 256, WIDTH), BF16),
        in_specs=spaces("s", *("a" * len(pieces))),
        out_specs=pl.BlockSpec(memory_space=pltpu.VMEM),
        scratch_shapes=[pltpu.SemaphoreType.DMA((2 * n_ctx,))],
        compiler_params=pltpu.CompilerParams(vmem_limit_bytes=40 << 20),
    )(place, *pieces)


def turn(block, dx, dz, n_ctx):
    depth = n_ctx // ACROSS
    pairs = [
        (z * ACROSS + x, (z + dz) % depth * ACROSS + (x + dx) % ACROSS)
        for z in range(depth)
        for x in range(ACROSS)
    ]
    return lax.ppermute(block, "ctx", pairs)


def ring_x(block, n_ctx):
    half = block.shape[0] // 2
    below, above = turn(block, 1, 0, n_ctx), turn(block, -1, 0, n_ctx)
    return below, turn(below[:half], 1, 0, n_ctx), turn(above[half:], -1, 0, n_ctx), above


def ring_z(block, n_ctx):
    half = block.shape[0] // 2
    below, above = [block], [block]
    for _ in range(n_ctx // ACROSS // 2 - 1):
        below.append(turn(below[-1], 0, 1, n_ctx))
        above.append(turn(above[-1], 0, -1, n_ctx))
    low, high = turn(below[-1][:half], 0, 1, n_ctx), turn(above[-1][half:], 0, -1, n_ctx)
    return (*below[1:], low, high, *above[1:])


def gather_weights(first, second, place, n_ctx):
    below, low, high, above = ring_x(first, n_ctx)
    wide = jnp.concatenate([first, below, above, low, high])
    tall = jnp.concatenate([second, *ring_z(second, n_ctx)])
    wide, tall = lax.optimization_barrier((wide, tall))
    pieces = (wide, *ring_z(wide, n_ctx), tall, *ring_x(tall, n_ctx))
    return load_call(place, n_ctx, pieces)


def backward_body(
    step,
    section_ref,
    c0_ref,
    g_ref,
    gl_ref,
    gr_ref,
    mask_ref,
    w_ref,
    xs_ref,
    qa_ref,
    qal0_ref,
    qar0_ref,
    qal1_ref,
    qar1_ref,
    kv_ref,
    rr_ref,
    grad_in,
    next_ref,
    left_ref,
    right_ref,
    grad_ref,
    ge,
    xs,
    qa,
    kv,
    rr,
    dz,
    dn,
    result,
    mask,
    inner_ref,
    sem_in,
    sem_save,
    sem_out,
):
    active, slot, last = schedule(step, section_ref[0])
    own = slice(BLK, BLK + ROWS)

    @pl.when(active)
    def _():
        loads = [
            pltpu.make_async_copy(source.at[slot], target, sem_save.at[index])
            for index, (source, target) in enumerate(
                (
                    (qa_ref, qa.at[own]),
                    (kv_ref, kv),
                    (rr_ref, rr),
                    (xs_ref, xs),
                    (mask_ref, mask),
                )
            )
        ]

        def ends(left, right):
            return [
                pltpu.make_async_copy(left, qa.at[:BLK], sem_save.at[5]),
                pltpu.make_async_copy(right, qa.at[BLK + ROWS :], sem_save.at[6]),
            ]

        @pl.when(slot == 0)
        def _():
            for copy in ends(qal0_ref, qar0_ref):
                copy.start()

        @pl.when(slot == 1)
        def _():
            for copy in ends(qal1_ref, qar1_ref):
                copy.start()

        @pl.when(last)
        def _():
            copy = pltpu.make_async_copy(c0_ref.at[slot], ge, sem_in.at[0])
            copy.start()
            for load in loads:
                load.start()
            copy.wait()

        @pl.when(jnp.logical_not(last))
        def _():
            copies = [
                pltpu.make_async_copy(gl_ref, ge.at[:BLK], sem_in.at[0]),
                pltpu.make_async_copy(g_ref, ge.at[own], sem_in.at[1]),
                pltpu.make_async_copy(gr_ref, ge.at[BLK + ROWS :], sem_in.at[2]),
            ]
            for copy in copies:
                copy.start()
            for load in loads:
                load.start()
            for copy in copies:
                copy.wait()

        for load in loads + ends(qal0_ref, qar0_ref):
            load.wait()

        @pl.loop(0, 2)
        def _(pair):
            lane = lax.broadcasted_iota(jnp.int32, (EXT, 128), 1)
            rows = pl.ds(pl.multiple_of(16 * pair, 16), 16)
            low = w_ref[rows, 192:224, :].reshape(512, 1024)
            high = w_ref[rows, 224:256, :].reshape(512, 1024)
            spread = dot(ge[:, :1024], low, NT) + dot(ge[:, 1024:], high, NT)
            for half in range(4):
                head = pair * 4 + half
                at = pl.ds(pl.multiple_of(head * HDIM, HDIM), HDIM)
                beyond = pl.ds(pl.multiple_of(WIDTH + head * HDIM, HDIM), HDIM)
                third = pl.ds(pl.multiple_of(2 * WIDTH + head * HDIM, HDIM), HDIM)
                d_att = spread[:, half * HDIM : (half + 1) * HDIM].astype(BF16).astype(F32)
                query, key, value = qa[:, at], kv[:, at], kv[:, beyond]
                picked = (lane == head) | (lane == HEADS + head)
                inv = jnp.sum(
                    jnp.where(picked, qa[:, 2 * WIDTH :].astype(F32), 0.0),
                    axis=-1,
                    keepdims=True,
                )
                d_sum = (d_att * inv).astype(BF16)
                d_total = -inv * jnp.sum(
                    d_att * qa[:, beyond].astype(F32), axis=-1, keepdims=True
                )
                probs = jnp.exp(dot(query, key, NT) * SCALE) * mask[...]
                d_probs = dot(d_sum, value, NT)
                d_scores = (probs * (d_probs + d_total) * SCALE).astype(BF16)
                d_value = dot(probs.astype(BF16), d_sum, TN)[own]
                d_key = dot(d_scores, query, TN)[own]
                d_query = dot(d_scores[own], key)

                def unnorm(grad, unit, which):
                    grad = grad.astype(BF16).astype(F32)
                    unit = unit.astype(F32)
                    r = jnp.sum(
                        jnp.where(lane[:ROWS] == which, rr[...], 0.0), axis=-1, keepdims=True
                    )
                    return r * (grad - unit * jnp.mean(grad * unit, axis=-1, keepdims=True))

                dz[:, at] = unnorm(d_query, query[own], head).astype(BF16)
                dz[:, beyond] = unnorm(d_key, key[own], HEADS + head).astype(BF16)
                dz[:, third] = d_value.astype(BF16)

        inner_ref[...] = jnp.zeros((ROWS, 128), F32)

        @pl.loop(0, 4)
        def _(tile):
            rows = pl.ds(pl.multiple_of(8 * tile, 8), 8)
            cols = pl.ds(pl.multiple_of(tile * 512, 512), 512)
            grad = jnp.zeros((ROWS, 512), F32)
            for part in range(3):
                weight = w_ref[rows, 64 * part : 64 * part + 64, :].reshape(512, WIDTH)
                grad += dot(dz[:, part * WIDTH : (part + 1) * WIDTH], weight, NT)
            grad = grad.astype(BF16).astype(F32)
            dn[:, cols] = grad
            product = grad * xs[:, cols].astype(F32)
            inner_ref[...] += (product[:, :128] + product[:, 128:256]) + (product[:, 256:384] + product[:, 384:])

        @pl.loop(0, ROWS // BLK)
        def _(block):
            at = pl.ds(pl.multiple_of(block * BLK, BLK), BLK)
            x = xs[at].astype(F32)
            scale = lax.rsqrt(jnp.mean(x * x, axis=-1, keepdims=True) + EPS)
            inner = jnp.sum(inner_ref[at], axis=-1, keepdims=True) * scale * scale * (1.0 / D)
            through = ge[pl.ds(pl.multiple_of(block * BLK + BLK, BLK), BLK)].astype(F32)
            result[at] = (through + scale * (dn[at] - x * inner)).astype(BF16)

        saves = [
            pltpu.make_async_copy(source, target, sem_out.at[index])
            for index, (source, target) in enumerate(
                (
                    (result, next_ref),
                (result.at[:BLK], left_ref),
                (result.at[ROWS - BLK :], right_ref),
                    (result, grad_ref.at[slot]),
                )
            )
        ]
        for copy in saves:
            copy.start()
        for copy in saves:
            copy.wait()


def backward_call(step, position, c0, g, gl, gr, mask, w, xs, qa, ends, kv, rr, grads, kind):
    rows = jax.ShapeDtypeStruct((ROWS, D), BF16)
    edge = jax.ShapeDtypeStruct((BLK, D), BF16)
    body = functools.partial(backward_body, step)
    carried = () if grads is None else (grads,)
    if not carried:
        body = fresh(body, 15, 1)
    outs = pl.pallas_call(
        body,
        name="backward_layer",
        out_shape=(rows, edge, edge, kind),
        in_specs=spaces(*("saaaaav" + "a" * (8 + len(carried)))),
        out_specs=spaces(*"aaaa"),
        scratch_shapes=[
            pltpu.VMEM((EXT, D), BF16),
            pltpu.VMEM((ROWS, D), BF16),
            pltpu.VMEM((EXT, PACK), BF16),
            pltpu.VMEM((EXT, 2 * WIDTH), BF16),
            pltpu.VMEM((ROWS, 128), F32),
            pltpu.VMEM((ROWS, 3 * WIDTH), BF16),
            pltpu.VMEM((ROWS, D), F32),
            pltpu.VMEM((ROWS, D), BF16),
            pltpu.VMEM((EXT, EXT), F32),
            pltpu.VMEM((ROWS, 128), F32),
            pltpu.SemaphoreType.DMA((3,)),
            pltpu.SemaphoreType.DMA((7,)),
            pltpu.SemaphoreType.DMA((4,)),
        ],
        input_output_aliases={15: 3} if carried else {},
        compiler_params=pltpu.CompilerParams(vmem_limit_bytes=VMEM_LIMIT),
    )(position, c0, g, gl, gr, mask, w, xs, qa, *ends, kv, rr, *carried)
    return outs[:3], outs[3]


def pack_body(wq_ref, wk_ref, wv_ref, wo_ref, first_ref, second_ref):
    first_ref[0:64] = wq_ref[0]
    first_ref[64:SPLIT] = wk_ref[0, : SPLIT - 64]
    second_ref[: 128 - SPLIT] = wk_ref[0, SPLIT - 64 :]
    second_ref[128 - SPLIT : 192 - SPLIT] = wv_ref[0]
    second_ref[192 - SPLIT : 224 - SPLIT] = wo_ref[0, :, :WIDTH]
    second_ref[224 - SPLIT :] = wo_ref[0, :, WIDTH:]


def pack_call(*weights):
    return pl.pallas_call(
        pack_body,
        name="pack_weights",
        out_shape=(
            jax.ShapeDtypeStruct((SPLIT, WIDTH), BF16),
            jax.ShapeDtypeStruct((REST, WIDTH), BF16),
        ),
        in_specs=spaces(*"vvvv"),
        out_specs=spaces(*"vv"),
    )(*weights)

BOTH = ("section", "ctx")


def neighbours(n_ctx, distance):
    return [(c, c + distance) for c in range(n_ctx) if 0 <= c + distance < n_ctx]


def hop(sections, step, n_ctx):
    return [(s * n_ctx + c, (s + step) * n_ctx + c) for s in sections for c in range(n_ctx)]


def diagonal(n_section, step, n_ctx, distance):
    return [
        (s * n_ctx + source, (s + step) * n_ctx + target)
        for s in range(n_section)
        if 0 <= s + step < n_section
        for source, target in neighbours(n_ctx, distance)
    ]


def relay(parts, sections, step, n_section, n_ctx):
    rows, left, right = parts
    rows = lax.ppermute(rows, BOTH, hop(sections, step, n_ctx))
    from_left = lax.ppermute(right, BOTH, diagonal(n_section, step, n_ctx, 1))
    from_right = lax.ppermute(left, BOTH, diagonal(n_section, step, n_ctx, -1))
    return rows, from_left, from_right


def edges(block, dim, width, n_ctx):
    size = block.shape[dim]
    tail = lax.slice_in_dim(block, size - width, size, axis=dim)
    head = lax.slice_in_dim(block, 0, width, axis=dim)
    from_left = lax.ppermute(tail, "ctx", neighbours(n_ctx, 1))
    from_right = lax.ppermute(head, "ctx", neighbours(n_ctx, -1))
    return from_left, from_right


def allowed_keys(block_mask, place, n_ctx):
    block_ids = place * BLOCKS_DEV + jnp.arange(BLOCKS_DEV)
    mask = block_mask.astype(F32)
    left = mask[:, :, 0] * (block_ids > 0).astype(F32)
    right = mask[:, :, 1] * (block_ids < BLOCKS_DEV * n_ctx - 1).astype(F32)
    return jnp.stack([left, jnp.ones_like(left), right], axis=2)


def key_weights(before, allow, after):
    allow = jnp.concatenate([before, allow, after], axis=1)
    allow = jnp.repeat(allow, BLK, axis=1)
    block = jnp.arange(EXT) // BLK
    offset = block[None, :] - block[:, None] + 1
    return sum(
        jnp.where(offset == side, allow[:, :, side : side + 1], 0.0) for side in range(3)
    )


def per_device(section_input, cotangent, w_query, w_key, w_value, w_out, block_mask):
    n_section = lax.axis_size("section")
    n_ctx = lax.axis_size("ctx")
    section = lax.axis_index("section")
    place = lax.axis_index("ctx")
    micro = section_input.shape[0]
    steps = n_section + micro - 1

    first, second = pack_call(w_query, w_key, w_value, w_out)
    position = jnp.full((1,), section, jnp.int32)
    reverse = n_section - 1 - position
    allow = allowed_keys(block_mask, place, n_ctx)
    fields = jnp.stack([section_input, cotangent])

    def packed(part, block):
        lanes = jnp.pad(part.reshape(1, -1), ((0, 15), (0, D - part.size)))
        return jnp.concatenate([block.reshape(-1, D), lanes.astype(BF16)], axis=0)

    pieces = jnp.concatenate(
        [packed(allow[:, :1], fields[:, :, :BLK]), packed(allow[:, -1:], fields[:, :, -BLK:])]
    )
    size = pieces.shape[0] // 2
    before, after = edges(pieces, 0, size, n_ctx)

    def unpacked(piece):
        block = piece[: size - 16].reshape(2, micro, BLK, D)
        return block, piece[size - 16, : 3 * micro].astype(F32).reshape(micro, 1, 3)

    before, before_allow = unpacked(before)
    after, after_allow = unpacked(after)
    extended = jnp.concatenate([before, fields, after], axis=2)
    mask = key_weights(before_allow, allow, after_allow)
    forward_mask = mask[:, BLK : BLK + ROWS]
    weights = gather_weights(first, second, jnp.full((1,), place, jnp.int32), n_ctx)

    kinds = (
        jax.ShapeDtypeStruct((micro, ROWS, D), BF16),
        jax.ShapeDtypeStruct((micro, ROWS, D), BF16),
        jax.ShapeDtypeStruct((micro, ROWS, PACK), BF16),
        jax.ShapeDtypeStruct((micro, EXT, 2 * WIDTH), BF16),
        jax.ShapeDtypeStruct((micro, ROWS, 128), F32),
    )
    zero_rows = jnp.zeros((ROWS, D), BF16)
    zero_edge = jnp.zeros((BLK, D), BF16)
    incoming = (zero_rows, zero_edge, zero_edge)

    def forward(step, incoming, saved):
        parts, saved = forward_call(
            step, position, extended[0], *incoming, forward_mask, weights, saved, kinds
        )
        senders = [s for s in range(step - micro + 1, step + 1) if 0 <= s < n_section - 1]
        if senders:
            incoming = relay(parts, senders, 1, n_section, n_ctx)
        return incoming, saved

    def backward(step, incoming, saved, ends, grads):
        xs, _, qa, kv, rr = saved
        parts, grads = backward_call(
            step, reverse, extended[1], *incoming, mask, weights, xs, qa, ends, kv, rr, grads, kinds[0]
        )
        top = n_section - 1 - step
        senders = [s for s in range(top, top + micro) if 0 < s < n_section]
        if senders:
            incoming = relay(parts, senders, -1, n_section, n_ctx)
        return incoming, grads

    saved = ()
    for step in range(n_section):
        incoming, saved = forward(step, incoming, saved)
    ends = edges(saved[2][0], 0, BLK, n_ctx)
    pulled, grads = backward(0, (zero_rows, zero_edge, zero_edge), saved, ends * 2, None)
    saved, grads = lax.optimization_barrier((saved, grads))
    for step in range(n_section, steps):
        incoming, saved = forward(step, incoming, saved)
    ends = ends + edges(saved[2][1], 0, BLK, n_ctx)
    for step in range(1, steps):
        pulled, grads = backward(step, pulled, saved, ends, grads)
    outputs = saved[1]
    return (outputs[None], grads[None])


def solution(mesh):
    return jax.shard_map(
        per_device,
        mesh=mesh,
        in_specs=(
            P(None, "ctx", None),
            P(None, "ctx", None),
            P("section", "ctx", None),
            P("section", "ctx", None),
            P("section", "ctx", None),
            P("section", "ctx", None),
            P(None, "ctx", None),
        ),
        out_specs=(P("section", None, "ctx", None), P("section", None, "ctx", None)),
        check_vma=False,
    )
```

```python
import functools

import jax
import jax.numpy as jnp
from jax import lax
from jax.experimental import pallas as pl
from jax.experimental.pallas import tpu as pltpu
from jax.sharding import PartitionSpec as P

D = 2048
HEADS = 8
HDIM = 128
BLOCKS_DEV = 4
BLK = 32
MICRO = 2
ROWS = BLK * BLOCKS_DEV
EXT = ROWS + 2 * BLK
WIDTH = HEADS * HDIM
PACK = 2 * WIDTH + 128
EPS = 1e-06
VMEM_LIMIT = 16 << 20
SCALE = HDIM ** (-0.5)
F32 = jnp.float32
BF16 = jnp.bfloat16

NT = (((1,), (1,)), ((), ()))
NN = (((1,), (0,)), ((), ()))
TN = (((0,), (0,)), ((), ()))


def dot(a, b, dims=NN):
    return lax.dot_general(a, b, dims, preferred_element_type=F32)


def wtile(w_ref, row, count, col, width):
    tile = w_ref[:, row : row + count, col : col + width]
    return tile.reshape(tile.shape[0] * count, width)


def schedule(step, position):
    micro_id = step - position
    active = (micro_id >= 0) & (micro_id < MICRO)
    return active, jnp.clip(micro_id, 0, MICRO - 1), position == 0


def forward_body(
    step,
    section_ref,
    x0_ref,
    x_ref,
    xl_ref,
    xr_ref,
    mask_ref,
    w_ref,
    xs_in,
    out_in,
    qa_in,
    kv_in,
    rr_in,
    next_ref,
    left_ref,
    right_ref,
    xs_ref,
    out_ref,
    qa_ref,
    kv_ref,
    rr_ref,
    xe,
    normed,
    qa,
    kv,
    rr,
    result,
    inverse,
    mask,
    sem_in,
    sem_out,
):
    active, slot, first = schedule(step, section_ref[0])

    @pl.when(active)
    def _():
        mask_copy = pltpu.make_async_copy(mask_ref.at[slot], mask, sem_in.at[3])
        mask_copy.start()

        @pl.when(first)
        def _():
            copy = pltpu.make_async_copy(x0_ref.at[slot], xe, sem_in.at[0])
            copy.start()
            copy.wait()

        @pl.when(jnp.logical_not(first))
        def _():
            copies = [
                pltpu.make_async_copy(xl_ref, xe.at[:BLK], sem_in.at[0]),
                pltpu.make_async_copy(x_ref, xe.at[BLK : BLK + ROWS], sem_in.at[1]),
                pltpu.make_async_copy(xr_ref, xe.at[BLK + ROWS :], sem_in.at[2]),
            ]
            for copy in copies:
                copy.start()
            for copy in copies:
                copy.wait()

        saves = [pltpu.make_async_copy(xe.at[BLK : BLK + ROWS], xs_ref.at[slot], sem_out.at[0])]
        saves[0].start()

        @pl.loop(0, EXT // BLK)
        def _(block):
            at = pl.ds(pl.multiple_of(block * BLK, BLK), BLK)
            rows = xe[at].astype(F32)
            scale = lax.rsqrt(jnp.mean(rows * rows, axis=-1, keepdims=True) + EPS)
            normed[at] = (rows * scale).astype(BF16)

        rr[...] = jnp.zeros((ROWS, 128), F32)
        inverse[...] = jnp.zeros((ROWS, 128), F32)
        mask_copy.wait()

        @pl.loop(0, 2)
        def _(pair):
            lane = lax.broadcasted_iota(jnp.int32, (ROWS, 128), 1)
            tile = pl.ds(pl.multiple_of(pair * 512, 512), 512)
            queries = dot(normed[BLK : BLK + ROWS], w_ref[:, 0:64, tile].reshape(D, 512))
            keys = dot(normed[...], w_ref[:, 64:128, tile].reshape(D, 512))
            values = dot(normed[...], w_ref[:, 128:192, tile].reshape(D, 512))
            for half in range(4):
                head = pair * 4 + half
                cols = slice(half * HDIM, (half + 1) * HDIM)
                at = pl.ds(pl.multiple_of(head * HDIM, HDIM), HDIM)
                beyond = pl.ds(pl.multiple_of(WIDTH + head * HDIM, HDIM), HDIM)
                query, key, value = queries[:, cols], keys[:, cols], values[:, cols]
                rq = lax.rsqrt(jnp.mean(query * query, axis=-1, keepdims=True) + EPS)
                rk = lax.rsqrt(jnp.mean(key * key, axis=-1, keepdims=True) + EPS)
                query = (query * rq).astype(BF16)
                key = (key * rk).astype(BF16)
                value = value.astype(BF16)
                probs = jnp.exp(dot(query, key, NT) * SCALE) * mask[...]
                inv = 1.0 / jnp.sum(probs, axis=-1, keepdims=True)
                attended = dot(probs.astype(BF16), value) * inv
                qa[:, at] = query
                qa[:, beyond] = attended.astype(BF16)
                kv[:, at] = key
                kv[:, beyond] = value
                high = inv.astype(BF16).astype(F32)
                stored = jnp.where(lane == head, rq, rr[...])
                rr[...] = jnp.where(lane == HEADS + head, rk[BLK : BLK + ROWS], stored)
                stored = jnp.where(lane == head, high, inverse[...])
                inverse[...] = jnp.where(lane == HEADS + head, inv - high, stored)

        qa[:, 2 * WIDTH :] = inverse[...].astype(BF16)
        for index, (source, target) in enumerate(((qa, qa_ref), (kv, kv_ref), (rr, rr_ref))):
            copy = pltpu.make_async_copy(source, target.at[slot], sem_out.at[1 + index])
            copy.start()
            saves.append(copy)

        for half in range(2):
            @pl.loop(0, 2)
            def _(tile):
                source = pl.ds(pl.multiple_of(tile * 512, 512), 512)
                cols = pl.ds(pl.multiple_of(half * 1024 + tile * 512, 512), 512)
                low = 192 + 32 * half
                weight = w_ref[:, low : low + 32, source].reshape(WIDTH, 512)
                update = dot(qa[:, WIDTH : 2 * WIDTH], weight)
                result[:, cols] = (xe[BLK : BLK + ROWS, cols].astype(F32) + update).astype(BF16)

        for index, (source, target) in enumerate(
            (
                (result, next_ref),
                (result.at[:BLK], left_ref),
                (result.at[ROWS - BLK :], right_ref),
                (result, out_ref.at[slot]),
            )
        ):
            copy = pltpu.make_async_copy(source, target, sem_out.at[4 + index])
            copy.start()
            saves.append(copy)
        for copy in saves:
            copy.wait()


def spaces(*names):
    table = dict(s=pltpu.SMEM, v=pltpu.VMEM, a=pltpu.HBM)
    return [pl.BlockSpec(memory_space=table[n]) for n in names]


def shape_of(a):
    return jax.ShapeDtypeStruct(a.shape, a.dtype)


def fresh(body, position, count):
    def wrapped(*refs):
        return body(*refs[:position], *([None] * count), *refs[position:])

    return wrapped


def forward_call(step, position, x0, x, xl, xr, mask, w, saved, kinds):
    rows = jax.ShapeDtypeStruct((ROWS, D), BF16)
    edge = jax.ShapeDtypeStruct((BLK, D), BF16)
    body = functools.partial(forward_body, step)
    if not saved:
        body = fresh(body, 7, len(kinds))
    outs = pl.pallas_call(
        body,
        name="forward_layer",
        out_shape=(rows, edge, edge) + kinds,
        in_specs=spaces(*("saaaaav" + "a" * len(saved))),
        out_specs=spaces(*"aaaaaaaa"),
        scratch_shapes=[
            pltpu.VMEM((EXT, D), BF16),
            pltpu.VMEM((EXT, D), BF16),
            pltpu.VMEM((ROWS, PACK), BF16),
            pltpu.VMEM((EXT, 2 * WIDTH), BF16),
            pltpu.VMEM((ROWS, 128), F32),
            pltpu.VMEM((ROWS, D), BF16),
            pltpu.VMEM((ROWS, 128), F32),
            pltpu.VMEM((ROWS, EXT), F32),
            pltpu.SemaphoreType.DMA((4,)),
            pltpu.SemaphoreType.DMA((8,)),
        ],
        input_output_aliases={7 + i: 3 + i for i in range(len(saved))},
        compiler_params=pltpu.CompilerParams(vmem_limit_bytes=VMEM_LIMIT),
    )(position, x0, x, xl, xr, mask, w, *saved)
    return outs[:3], outs[3:]

ACROSS = 4
SPLIT = 112
REST = 256 - SPLIT
X_ORDER = (0, -1, 1, 2)
Z_ORDER = (0, -1, -2, -3, 4, 1, 2, 3)


def load_body(n_ctx, place_ref, *refs):
    sources, w_ref, sem = refs[:-2], refs[-2], refs[-1]
    depth = n_ctx // ACROSS
    z, x = place_ref[0] // ACROSS, lax.rem(place_ref[0], ACROSS)

    def owner(dx, dz):
        return lax.rem(z + dz + depth, depth) * ACROSS + lax.rem(x + dx + ACROSS, ACROSS)

    moves = []
    for ref, dz, blocks in zip(
        sources[:9],
        (0, -1, -2, -3, 4, 4, 1, 2, 3),
        (X_ORDER,) * 4 + (X_ORDER[:2], X_ORDER[2:]) + (X_ORDER,) * 3,
    ):
        for index, dx in enumerate(blocks):
            piece = ref.at[index * SPLIT : (index + 1) * SPLIT]
            moves.append((piece, w_ref.at[owner(dx, dz), 0:SPLIT]))
    for ref, dx, blocks in zip(
        sources[9:], (0, -1, 2, 2, 1), (Z_ORDER, Z_ORDER, Z_ORDER[:4], Z_ORDER[4:], Z_ORDER)
    ):
        for index, dz in enumerate(blocks):
            piece = ref.at[index * REST : (index + 1) * REST]
            moves.append((piece, w_ref.at[owner(dx, dz), SPLIT:256]))
    copies = [
        pltpu.make_async_copy(source, target, sem.at[index])
        for index, (source, target) in enumerate(moves)
    ]
    for copy in copies:
        copy.start()
    for copy in copies:
        copy.wait()


def load_call(place, n_ctx, pieces):
    return pl.pallas_call(
        functools.partial(load_body, n_ctx),
        name="load_weights",
        out_shape=pltpu.VMEM((n_ctx, 256, WIDTH), BF16),
        in_specs=spaces("s", *("a" * len(pieces))),
        out_specs=pl.BlockSpec(memory_space=pltpu.VMEM),
        scratch_shapes=[pltpu.SemaphoreType.DMA((2 * n_ctx,))],
        compiler_params=pltpu.CompilerParams(vmem_limit_bytes=40 << 20),
    )(place, *pieces)


def turn(block, dx, dz, n_ctx):
    depth = n_ctx // ACROSS
    pairs = [
        (z * ACROSS + x, (z + dz) % depth * ACROSS + (x + dx) % ACROSS)
        for z in range(depth)
        for x in range(ACROSS)
    ]
    return lax.ppermute(block, "ctx", pairs)


def ring_x(block, n_ctx):
    half = block.shape[0] // 2
    below, above = turn(block, 1, 0, n_ctx), turn(block, -1, 0, n_ctx)
    return below, turn(below[:half], 1, 0, n_ctx), turn(above[half:], -1, 0, n_ctx), above


def ring_z(block, n_ctx):
    half = block.shape[0] // 2
    below, above = [block], [block]
    for _ in range(n_ctx // ACROSS // 2 - 1):
        below.append(turn(below[-1], 0, 1, n_ctx))
        above.append(turn(above[-1], 0, -1, n_ctx))
    low, high = turn(below[-1][:half], 0, 1, n_ctx), turn(above[-1][half:], 0, -1, n_ctx)
    return (*below[1:], low, high, *above[1:])


def gather_weights(first, second, ends, place, n_ctx):
    below, low, high, above = ring_x(first, n_ctx)
    wide = jnp.concatenate([first, below, above, low, high])
    tall = jnp.concatenate([second, *ring_z(second, n_ctx)])
    wide, tall, ends = lax.optimization_barrier((wide, tall, ends))
    pieces = (wide, *ring_z(wide, n_ctx), tall, *ring_x(tall, n_ctx))
    return load_call(place, n_ctx, pieces), ends


def backward_body(
    step,
    section_ref,
    c0_ref,
    g_ref,
    gl_ref,
    gr_ref,
    mask_ref,
    w_ref,
    xs_ref,
    qa_ref,
    qal0_ref,
    qar0_ref,
    qal1_ref,
    qar1_ref,
    kv_ref,
    rr_ref,
    grad_in,
    next_ref,
    left_ref,
    right_ref,
    grad_ref,
    ge,
    xs,
    qa,
    kv,
    rr,
    dz,
    dn,
    result,
    mask,
    inner_ref,
    sem_in,
    sem_save,
    sem_out,
):
    active, slot, last = schedule(step, section_ref[0])
    own = slice(BLK, BLK + ROWS)

    @pl.when(active)
    def _():
        loads = [
            pltpu.make_async_copy(source.at[slot], target, sem_save.at[index])
            for index, (source, target) in enumerate(
                (
                    (qa_ref, qa.at[own]),
                    (kv_ref, kv),
                    (rr_ref, rr),
                    (xs_ref, xs),
                    (mask_ref, mask),
                )
            )
        ]

        def ends(left, right):
            return [
                pltpu.make_async_copy(left, qa.at[:BLK], sem_save.at[5]),
                pltpu.make_async_copy(right, qa.at[BLK + ROWS :], sem_save.at[6]),
            ]

        @pl.when(slot == 0)
        def _():
            for copy in ends(qal0_ref, qar0_ref):
                copy.start()

        @pl.when(slot == 1)
        def _():
            for copy in ends(qal1_ref, qar1_ref):
                copy.start()

        @pl.when(last)
        def _():
            copy = pltpu.make_async_copy(c0_ref.at[slot], ge, sem_in.at[0])
            copy.start()
            for load in loads:
                load.start()
            copy.wait()

        @pl.when(jnp.logical_not(last))
        def _():
            copies = [
                pltpu.make_async_copy(gl_ref, ge.at[:BLK], sem_in.at[0]),
                pltpu.make_async_copy(g_ref, ge.at[own], sem_in.at[1]),
                pltpu.make_async_copy(gr_ref, ge.at[BLK + ROWS :], sem_in.at[2]),
            ]
            for copy in copies:
                copy.start()
            for load in loads:
                load.start()
            for copy in copies:
                copy.wait()

        for load in loads + ends(qal0_ref, qar0_ref):
            load.wait()

        @pl.loop(0, 2)
        def _(pair):
            lane = lax.broadcasted_iota(jnp.int32, (EXT, 128), 1)
            rows = pl.ds(pl.multiple_of(16 * pair, 16), 16)
            low = w_ref[rows, 192:224, :].reshape(512, 1024)
            high = w_ref[rows, 224:256, :].reshape(512, 1024)
            spread = dot(ge[:, :1024], low, NT) + dot(ge[:, 1024:], high, NT)
            for half in range(4):
                head = pair * 4 + half
                at = pl.ds(pl.multiple_of(head * HDIM, HDIM), HDIM)
                beyond = pl.ds(pl.multiple_of(WIDTH + head * HDIM, HDIM), HDIM)
                third = pl.ds(pl.multiple_of(2 * WIDTH + head * HDIM, HDIM), HDIM)
                d_att = spread[:, half * HDIM : (half + 1) * HDIM].astype(BF16).astype(F32)
                query, key, value = qa[:, at], kv[:, at], kv[:, beyond]
                picked = (lane == head) | (lane == HEADS + head)
                inv = jnp.sum(
                    jnp.where(picked, qa[:, 2 * WIDTH :].astype(F32), 0.0),
                    axis=-1,
                    keepdims=True,
                )
                d_sum = (d_att * inv).astype(BF16)
                d_total = -inv * jnp.sum(
                    d_att * qa[:, beyond].astype(F32), axis=-1, keepdims=True
                )
                probs = jnp.exp(dot(query, key, NT) * SCALE) * mask[...]
                d_probs = dot(d_sum, value, NT)
                d_scores = (probs * (d_probs + d_total) * SCALE).astype(BF16)
                d_value = dot(probs.astype(BF16), d_sum, TN)[own]
                d_key = dot(d_scores, query, TN)[own]
                d_query = dot(d_scores[own], key)

                def unnorm(grad, unit, which):
                    grad = grad.astype(BF16).astype(F32)
                    unit = unit.astype(F32)
                    r = jnp.sum(
                        jnp.where(lane[:ROWS] == which, rr[...], 0.0), axis=-1, keepdims=True
                    )
                    return r * (grad - unit * jnp.mean(grad * unit, axis=-1, keepdims=True))

                dz[:, at] = unnorm(d_query, query[own], head).astype(BF16)
                dz[:, beyond] = unnorm(d_key, key[own], HEADS + head).astype(BF16)
                dz[:, third] = d_value.astype(BF16)

        inner_ref[...] = jnp.zeros((ROWS, 128), F32)

        @pl.loop(0, 4)
        def _(tile):
            rows = pl.ds(pl.multiple_of(8 * tile, 8), 8)
            cols = pl.ds(pl.multiple_of(tile * 512, 512), 512)
            grad = jnp.zeros((ROWS, 512), F32)
            for part in range(3):
                weight = w_ref[rows, 64 * part : 64 * part + 64, :].reshape(512, WIDTH)
                grad += dot(dz[:, part * WIDTH : (part + 1) * WIDTH], weight, NT)
            grad = grad.astype(BF16).astype(F32)
            dn[:, cols] = grad
            product = grad * xs[:, cols].astype(F32)
            inner_ref[...] += (product[:, :128] + product[:, 128:256]) + (product[:, 256:384] + product[:, 384:])

        @pl.loop(0, ROWS // BLK)
        def _(block):
            at = pl.ds(pl.multiple_of(block * BLK, BLK), BLK)
            x = xs[at].astype(F32)
            scale = lax.rsqrt(jnp.mean(x * x, axis=-1, keepdims=True) + EPS)
            inner = jnp.sum(inner_ref[at], axis=-1, keepdims=True) * scale * scale * (1.0 / D)
            through = ge[pl.ds(pl.multiple_of(block * BLK + BLK, BLK), BLK)].astype(F32)
            result[at] = (through + scale * (dn[at] - x * inner)).astype(BF16)

        saves = [
            pltpu.make_async_copy(source, target, sem_out.at[index])
            for index, (source, target) in enumerate(
                (
                    (result, next_ref),
                (result.at[:BLK], left_ref),
                (result.at[ROWS - BLK :], right_ref),
                    (result, grad_ref.at[slot]),
                )
            )
        ]
        for copy in saves:
            copy.start()
        for copy in saves:
            copy.wait()


def backward_call(step, position, c0, g, gl, gr, mask, w, xs, qa, ends, kv, rr, grads, kind):
    rows = jax.ShapeDtypeStruct((ROWS, D), BF16)
    edge = jax.ShapeDtypeStruct((BLK, D), BF16)
    body = functools.partial(backward_body, step)
    carried = () if grads is None else (grads,)
    if not carried:
        body = fresh(body, 15, 1)
    outs = pl.pallas_call(
        body,
        name="backward_layer",
        out_shape=(rows, edge, edge, kind),
        in_specs=spaces(*("saaaaav" + "a" * (8 + len(carried)))),
        out_specs=spaces(*"aaaa"),
        scratch_shapes=[
            pltpu.VMEM((EXT, D), BF16),
            pltpu.VMEM((ROWS, D), BF16),
            pltpu.VMEM((EXT, PACK), BF16),
            pltpu.VMEM((EXT, 2 * WIDTH), BF16),
            pltpu.VMEM((ROWS, 128), F32),
            pltpu.VMEM((ROWS, 3 * WIDTH), BF16),
            pltpu.VMEM((ROWS, D), F32),
            pltpu.VMEM((ROWS, D), BF16),
            pltpu.VMEM((EXT, EXT), F32),
            pltpu.VMEM((ROWS, 128), F32),
            pltpu.SemaphoreType.DMA((3,)),
            pltpu.SemaphoreType.DMA((7,)),
            pltpu.SemaphoreType.DMA((4,)),
        ],
        input_output_aliases={15: 3} if carried else {},
        compiler_params=pltpu.CompilerParams(vmem_limit_bytes=VMEM_LIMIT),
    )(position, c0, g, gl, gr, mask, w, xs, qa, *ends, kv, rr, *carried)
    return outs[:3], outs[3]


def pack_body(wq_ref, wk_ref, wv_ref, wo_ref, first_ref, second_ref):
    first_ref[0:64] = wq_ref[0]
    first_ref[64:SPLIT] = wk_ref[0, : SPLIT - 64]
    second_ref[: 128 - SPLIT] = wk_ref[0, SPLIT - 64 :]
    second_ref[128 - SPLIT : 192 - SPLIT] = wv_ref[0]
    second_ref[192 - SPLIT : 224 - SPLIT] = wo_ref[0, :, :WIDTH]
    second_ref[224 - SPLIT :] = wo_ref[0, :, WIDTH:]


def pack_call(*weights):
    return pl.pallas_call(
        pack_body,
        name="pack_weights",
        out_shape=(
            jax.ShapeDtypeStruct((SPLIT, WIDTH), BF16),
            jax.ShapeDtypeStruct((REST, WIDTH), BF16),
        ),
        in_specs=spaces(*"vvvv"),
        out_specs=spaces(*"vv"),
    )(*weights)

BOTH = ("section", "ctx")


def neighbours(n_ctx, distance):
    return [(c, c + distance) for c in range(n_ctx) if 0 <= c + distance < n_ctx]


def hop(sections, step, n_ctx):
    return [(s * n_ctx + c, (s + step) * n_ctx + c) for s in sections for c in range(n_ctx)]


def diagonal(n_section, step, n_ctx, distance):
    return [
        (s * n_ctx + source, (s + step) * n_ctx + target)
        for s in range(n_section)
        if 0 <= s + step < n_section
        for source, target in neighbours(n_ctx, distance)
    ]


def relay(parts, sections, step, n_section, n_ctx):
    rows, left, right = parts
    rows = lax.ppermute(rows, BOTH, hop(sections, step, n_ctx))
    from_left = lax.ppermute(right, BOTH, diagonal(n_section, step, n_ctx, 1))
    from_right = lax.ppermute(left, BOTH, diagonal(n_section, step, n_ctx, -1))
    return rows, from_left, from_right


def edges(block, dim, width, n_ctx):
    size = block.shape[dim]
    tail = lax.slice_in_dim(block, size - width, size, axis=dim)
    head = lax.slice_in_dim(block, 0, width, axis=dim)
    from_left = lax.ppermute(tail, "ctx", neighbours(n_ctx, 1))
    from_right = lax.ppermute(head, "ctx", neighbours(n_ctx, -1))
    return from_left, from_right


def allowed_keys(block_mask, place, n_ctx):
    block_ids = place * BLOCKS_DEV + jnp.arange(BLOCKS_DEV)
    mask = block_mask.astype(F32)
    left = mask[:, :, 0] * (block_ids > 0).astype(F32)
    right = mask[:, :, 1] * (block_ids < BLOCKS_DEV * n_ctx - 1).astype(F32)
    return jnp.stack([left, jnp.ones_like(left), right], axis=2)


def key_weights(before, allow, after):
    allow = jnp.concatenate([before, allow, after], axis=1)
    allow = jnp.repeat(allow, BLK, axis=1)
    block = jnp.arange(EXT) // BLK
    offset = block[None, :] - block[:, None] + 1
    return sum(
        jnp.where(offset == side, allow[:, :, side : side + 1], 0.0) for side in range(3)
    )


def per_device(section_input, cotangent, w_query, w_key, w_value, w_out, block_mask):
    n_section = lax.axis_size("section")
    n_ctx = lax.axis_size("ctx")
    section = lax.axis_index("section")
    place = lax.axis_index("ctx")
    micro = section_input.shape[0]
    steps = n_section + micro - 1

    first, second = pack_call(w_query, w_key, w_value, w_out)
    position = jnp.full((1,), section, jnp.int32)
    reverse = n_section - 1 - position
    allow = allowed_keys(block_mask, place, n_ctx)
    fields = jnp.stack([section_input, cotangent])

    def packed(part, block):
        lanes = jnp.pad(part.reshape(1, -1), ((0, 15), (0, D - part.size)))
        return jnp.concatenate([block.reshape(-1, D), lanes.astype(BF16)], axis=0)

    pieces = jnp.concatenate(
        [packed(allow[:, :1], fields[:, :, :BLK]), packed(allow[:, -1:], fields[:, :, -BLK:])]
    )
    size = pieces.shape[0] // 2
    before, after = edges(pieces, 0, size, n_ctx)
    weights, (before, after) = gather_weights(
        first, second, (before, after), jnp.full((1,), place, jnp.int32), n_ctx
    )

    def unpacked(piece):
        block = piece[: size - 16].reshape(2, micro, BLK, D)
        return block, piece[size - 16, : 3 * micro].astype(F32).reshape(micro, 1, 3)

    before, before_allow = unpacked(before)
    after, after_allow = unpacked(after)
    extended = jnp.concatenate([before, fields, after], axis=2)
    mask = key_weights(before_allow, allow, after_allow)
    forward_mask = mask[:, BLK : BLK + ROWS]

    kinds = (
        jax.ShapeDtypeStruct((micro, ROWS, D), BF16),
        jax.ShapeDtypeStruct((micro, ROWS, D), BF16),
        jax.ShapeDtypeStruct((micro, ROWS, PACK), BF16),
        jax.ShapeDtypeStruct((micro, EXT, 2 * WIDTH), BF16),
        jax.ShapeDtypeStruct((micro, ROWS, 128), F32),
    )
    zero_rows = jnp.zeros((ROWS, D), BF16)
    zero_edge = jnp.zeros((BLK, D), BF16)
    incoming = (zero_rows, zero_edge, zero_edge)

    def forward(step, incoming, saved):
        parts, saved = forward_call(
            step, position, extended[0], *incoming, forward_mask, weights, saved, kinds
        )
        senders = [s for s in range(step - micro + 1, step + 1) if 0 <= s < n_section - 1]
        if senders:
            incoming = relay(parts, senders, 1, n_section, n_ctx)
        return incoming, saved

    def backward(step, incoming, saved, ends, grads):
        xs, _, qa, kv, rr = saved
        parts, grads = backward_call(
            step, reverse, extended[1], *incoming, mask, weights, xs, qa, ends, kv, rr, grads, kinds[0]
        )
        top = n_section - 1 - step
        senders = [s for s in range(top, top + micro) if 0 < s < n_section]
        if senders:
            incoming = relay(parts, senders, -1, n_section, n_ctx)
        return incoming, grads

    saved = ()
    for step in range(n_section):
        incoming, saved = forward(step, incoming, saved)
    ends = edges(saved[2][0], 0, BLK, n_ctx)
    pulled, grads = backward(0, (zero_rows, zero_edge, zero_edge), saved, ends * 2, None)
    saved, grads = lax.optimization_barrier((saved, grads))
    for step in range(n_section, steps):
        incoming, saved = forward(step, incoming, saved)
    ends = ends + edges(saved[2][1], 0, BLK, n_ctx)
    for step in range(1, steps):
        pulled, grads = backward(step, pulled, saved, ends, grads)
    outputs = saved[1]
    return (outputs[None], grads[None])


def solution(mesh):
    return jax.shard_map(
        per_device,
        mesh=mesh,
        in_specs=(
            P(None, "ctx", None),
            P(None, "ctx", None),
            P("section", "ctx", None),
            P("section", "ctx", None),
            P("section", "ctx", None),
            P("section", "ctx", None),
            P(None, "ctx", None),
        ),
        out_specs=(P("section", None, "ctx", None), P("section", None, "ctx", None)),
        check_vma=False,
    )
```

```python
import functools

import jax
import jax.numpy as jnp
from jax import lax
from jax.experimental import pallas as pl
from jax.experimental.pallas import tpu as pltpu
from jax.sharding import PartitionSpec as P

D = 2048
HEADS = 8
HDIM = 128
BLOCKS_DEV = 4
BLK = 32
MICRO = 2
ROWS = BLK * BLOCKS_DEV
EXT = ROWS + 2 * BLK
WIDTH = HEADS * HDIM
PACK = 2 * WIDTH + 128
EPS = 1e-06
VMEM_LIMIT = 16 << 20
SCALE = HDIM ** (-0.5)
F32 = jnp.float32
BF16 = jnp.bfloat16

NT = (((1,), (1,)), ((), ()))
NN = (((1,), (0,)), ((), ()))
TN = (((0,), (0,)), ((), ()))


def dot(a, b, dims=NN):
    return lax.dot_general(a, b, dims, preferred_element_type=F32)


def wtile(w_ref, row, count, col, width):
    tile = w_ref[:, row : row + count, col : col + width]
    return tile.reshape(tile.shape[0] * count, width)


def schedule(step, position):
    micro_id = step - position
    active = (micro_id >= 0) & (micro_id < MICRO)
    return active, jnp.clip(micro_id, 0, MICRO - 1), position == 0


def forward_body(
    step,
    section_ref,
    x0_ref,
    x_ref,
    xl_ref,
    xr_ref,
    mask_ref,
    w_ref,
    xs_in,
    out_in,
    qa_in,
    kv_in,
    rr_in,
    next_ref,
    left_ref,
    right_ref,
    xs_ref,
    out_ref,
    qa_ref,
    kv_ref,
    rr_ref,
    xe,
    normed,
    qa,
    kv,
    rr,
    result,
    inverse,
    mask,
    sem_in,
    sem_out,
):
    active, slot, first = schedule(step, section_ref[0])

    @pl.when(active)
    def _():
        mask_copy = pltpu.make_async_copy(mask_ref.at[slot], mask, sem_in.at[3])
        mask_copy.start()

        @pl.when(first)
        def _():
            copy = pltpu.make_async_copy(x0_ref.at[slot], xe, sem_in.at[0])
            copy.start()
            copy.wait()

        @pl.when(jnp.logical_not(first))
        def _():
            copies = [
                pltpu.make_async_copy(xl_ref, xe.at[:BLK], sem_in.at[0]),
                pltpu.make_async_copy(x_ref, xe.at[BLK : BLK + ROWS], sem_in.at[1]),
                pltpu.make_async_copy(xr_ref, xe.at[BLK + ROWS :], sem_in.at[2]),
            ]
            for copy in copies:
                copy.start()
            for copy in copies:
                copy.wait()

        saves = [pltpu.make_async_copy(xe.at[BLK : BLK + ROWS], xs_ref.at[slot], sem_out.at[0])]
        saves[0].start()

        @pl.loop(0, EXT // BLK)
        def _(block):
            at = pl.ds(pl.multiple_of(block * BLK, BLK), BLK)
            rows = xe[at].astype(F32)
            scale = lax.rsqrt(jnp.mean(rows * rows, axis=-1, keepdims=True) + EPS)
            normed[at] = (rows * scale).astype(BF16)

        rr[...] = jnp.zeros((ROWS, 128), F32)
        inverse[...] = jnp.zeros((ROWS, 128), F32)
        mask_copy.wait()

        @pl.loop(0, 2)
        def _(pair):
            lane = lax.broadcasted_iota(jnp.int32, (ROWS, 128), 1)
            tile = pl.ds(pl.multiple_of(pair * 512, 512), 512)
            queries = dot(normed[BLK : BLK + ROWS], w_ref[:, 0:64, tile].reshape(D, 512))
            keys = dot(normed[...], w_ref[:, 64:128, tile].reshape(D, 512))
            values = dot(normed[...], w_ref[:, 128:192, tile].reshape(D, 512))
            for half in range(4):
                head = pair * 4 + half
                cols = slice(half * HDIM, (half + 1) * HDIM)
                at = pl.ds(pl.multiple_of(head * HDIM, HDIM), HDIM)
                beyond = pl.ds(pl.multiple_of(WIDTH + head * HDIM, HDIM), HDIM)
                query, key, value = queries[:, cols], keys[:, cols], values[:, cols]
                rq = lax.rsqrt(jnp.mean(query * query, axis=-1, keepdims=True) + EPS)
                rk = lax.rsqrt(jnp.mean(key * key, axis=-1, keepdims=True) + EPS)
                query = (query * rq).astype(BF16)
                key = (key * rk).astype(BF16)
                value = value.astype(BF16)
                probs = jnp.exp(dot(query, key, NT) * SCALE) * mask[...]
                inv = 1.0 / jnp.sum(probs, axis=-1, keepdims=True)
                attended = dot(probs.astype(BF16), value) * inv
                qa[:, at] = query
                qa[:, beyond] = attended.astype(BF16)
                kv[:, at] = key
                kv[:, beyond] = value
                high = inv.astype(BF16).astype(F32)
                stored = jnp.where(lane == head, rq, rr[...])
                rr[...] = jnp.where(lane == HEADS + head, rk[BLK : BLK + ROWS], stored)
                stored = jnp.where(lane == head, high, inverse[...])
                inverse[...] = jnp.where(lane == HEADS + head, inv - high, stored)

        qa[:, 2 * WIDTH :] = inverse[...].astype(BF16)
        for index, (source, target) in enumerate(((qa, qa_ref), (kv, kv_ref), (rr, rr_ref))):
            copy = pltpu.make_async_copy(source, target.at[slot], sem_out.at[1 + index])
            copy.start()
            saves.append(copy)

        for half in range(2):
            @pl.loop(0, 2)
            def _(tile):
                source = pl.ds(pl.multiple_of(tile * 512, 512), 512)
                cols = pl.ds(pl.multiple_of(half * 1024 + tile * 512, 512), 512)
                low = 192 + 32 * half
                weight = w_ref[:, low : low + 32, source].reshape(WIDTH, 512)
                update = dot(qa[:, WIDTH : 2 * WIDTH], weight)
                result[:, cols] = (xe[BLK : BLK + ROWS, cols].astype(F32) + update).astype(BF16)

        for index, (source, target) in enumerate(
            (
                (result, next_ref),
                (result.at[:BLK], left_ref),
                (result.at[ROWS - BLK :], right_ref),
                (result, out_ref.at[slot]),
            )
        ):
            copy = pltpu.make_async_copy(source, target, sem_out.at[4 + index])
            copy.start()
            saves.append(copy)
        for copy in saves:
            copy.wait()


def spaces(*names):
    table = dict(s=pltpu.SMEM, v=pltpu.VMEM, a=pltpu.HBM)
    return [pl.BlockSpec(memory_space=table[n]) for n in names]


def shape_of(a):
    return jax.ShapeDtypeStruct(a.shape, a.dtype)


def fresh(body, position, count):
    def wrapped(*refs):
        return body(*refs[:position], *([None] * count), *refs[position:])

    return wrapped


def forward_call(step, position, x0, x, xl, xr, mask, w, saved, kinds):
    rows = jax.ShapeDtypeStruct((ROWS, D), BF16)
    edge = jax.ShapeDtypeStruct((BLK, D), BF16)
    body = functools.partial(forward_body, step)
    if not saved:
        body = fresh(body, 7, len(kinds))
    outs = pl.pallas_call(
        body,
        name="forward_layer",
        out_shape=(rows, edge, edge) + kinds,
        in_specs=spaces(*("saaaaav" + "a" * len(saved))),
        out_specs=spaces(*"aaaaaaaa"),
        scratch_shapes=[
            pltpu.VMEM((EXT, D), BF16),
            pltpu.VMEM((EXT, D), BF16),
            pltpu.VMEM((ROWS, PACK), BF16),
            pltpu.VMEM((EXT, 2 * WIDTH), BF16),
            pltpu.VMEM((ROWS, 128), F32),
            pltpu.VMEM((ROWS, D), BF16),
            pltpu.VMEM((ROWS, 128), F32),
            pltpu.VMEM((ROWS, EXT), F32),
            pltpu.SemaphoreType.DMA((4,)),
            pltpu.SemaphoreType.DMA((8,)),
        ],
        input_output_aliases={7 + i: 3 + i for i in range(len(saved))},
        compiler_params=pltpu.CompilerParams(vmem_limit_bytes=VMEM_LIMIT),
    )(position, x0, x, xl, xr, mask, w, *saved)
    return outs[:3], outs[3:]

ACROSS = 4
SPLIT = 112
REST = 256 - SPLIT
X_ORDER = (0, -1, 1, 2)
Z_ORDER = (0, -1, -2, -3, 4, 1, 2, 3)


def load_body(n_ctx, place_ref, *refs):
    sources, w_ref, sem = refs[:-2], refs[-2], refs[-1]
    depth = n_ctx // ACROSS
    z, x = place_ref[0] // ACROSS, lax.rem(place_ref[0], ACROSS)

    def owner(dx, dz):
        return lax.rem(z + dz + depth, depth) * ACROSS + lax.rem(x + dx + ACROSS, ACROSS)

    moves = []
    for ref, dz, blocks in zip(
        sources[:9],
        (0, -1, -2, -3, 4, 4, 1, 2, 3),
        (X_ORDER,) * 4 + (X_ORDER[:2], X_ORDER[2:]) + (X_ORDER,) * 3,
    ):
        for index, dx in enumerate(blocks):
            piece = ref.at[index * SPLIT : (index + 1) * SPLIT]
            moves.append((piece, w_ref.at[owner(dx, dz), 0:SPLIT]))
    for ref, dx, blocks in zip(
        sources[9:], (0, -1, 2, 2, 1), (Z_ORDER, Z_ORDER, Z_ORDER[:4], Z_ORDER[4:], Z_ORDER)
    ):
        for index, dz in enumerate(blocks):
            piece = ref.at[index * REST : (index + 1) * REST]
            moves.append((piece, w_ref.at[owner(dx, dz), SPLIT:256]))
    copies = [
        pltpu.make_async_copy(source, target, sem.at[index])
        for index, (source, target) in enumerate(moves)
    ]
    for copy in copies:
        copy.start()
    for copy in copies:
        copy.wait()


def load_call(place, n_ctx, pieces):
    return pl.pallas_call(
        functools.partial(load_body, n_ctx),
        name="load_weights",
        out_shape=pltpu.VMEM((n_ctx, 256, WIDTH), BF16),
        in_specs=spaces("s", *("a" * len(pieces))),
        out_specs=pl.BlockSpec(memory_space=pltpu.VMEM),
        scratch_shapes=[pltpu.SemaphoreType.DMA((2 * n_ctx,))],
        compiler_params=pltpu.CompilerParams(vmem_limit_bytes=40 << 20),
    )(place, *pieces)


def turn(block, dx, dz, n_ctx):
    depth = n_ctx // ACROSS
    pairs = [
        (z * ACROSS + x, (z + dz) % depth * ACROSS + (x + dx) % ACROSS)
        for z in range(depth)
        for x in range(ACROSS)
    ]
    return lax.ppermute(block, "ctx", pairs)


def ring_x(block, n_ctx):
    half = block.shape[0] // 2
    below, above = turn(block, 1, 0, n_ctx), turn(block, -1, 0, n_ctx)
    return below, turn(below[:half], 1, 0, n_ctx), turn(above[half:], -1, 0, n_ctx), above


def ring_z(block, n_ctx):
    half = block.shape[0] // 2
    below, above = [block], [block]
    for _ in range(n_ctx // ACROSS // 2 - 1):
        below.append(turn(below[-1], 0, 1, n_ctx))
        above.append(turn(above[-1], 0, -1, n_ctx))
    low, high = turn(below[-1][:half], 0, 1, n_ctx), turn(above[-1][half:], 0, -1, n_ctx)
    return (*below[1:], low, high, *above[1:])


def gather_weights(first, second, ends, place, n_ctx):
    wide = jnp.concatenate([first] + [turn(first, -dx, 0, n_ctx) for dx in X_ORDER[1:]])
    tall = jnp.concatenate([second, *ring_z(second, n_ctx)])
    wide, tall, ends = lax.optimization_barrier((wide, tall, ends))
    pieces = (wide, *ring_z(wide, n_ctx), tall, *ring_x(tall, n_ctx))
    return load_call(place, n_ctx, pieces), ends


def backward_body(
    step,
    section_ref,
    c0_ref,
    g_ref,
    gl_ref,
    gr_ref,
    mask_ref,
    w_ref,
    xs_ref,
    qa_ref,
    qal0_ref,
    qar0_ref,
    qal1_ref,
    qar1_ref,
    kv_ref,
    rr_ref,
    grad_in,
    next_ref,
    left_ref,
    right_ref,
    grad_ref,
    ge,
    xs,
    qa,
    kv,
    rr,
    dz,
    dn,
    result,
    mask,
    inner_ref,
    sem_in,
    sem_save,
    sem_out,
):
    active, slot, last = schedule(step, section_ref[0])
    own = slice(BLK, BLK + ROWS)

    @pl.when(active)
    def _():
        loads = [
            pltpu.make_async_copy(source.at[slot], target, sem_save.at[index])
            for index, (source, target) in enumerate(
                (
                    (qa_ref, qa.at[own]),
                    (kv_ref, kv),
                    (rr_ref, rr),
                    (xs_ref, xs),
                    (mask_ref, mask),
                )
            )
        ]

        def ends(left, right):
            return [
                pltpu.make_async_copy(left, qa.at[:BLK], sem_save.at[5]),
                pltpu.make_async_copy(right, qa.at[BLK + ROWS :], sem_save.at[6]),
            ]

        @pl.when(slot == 0)
        def _():
            for copy in ends(qal0_ref, qar0_ref):
                copy.start()

        @pl.when(slot == 1)
        def _():
            for copy in ends(qal1_ref, qar1_ref):
                copy.start()

        @pl.when(last)
        def _():
            copy = pltpu.make_async_copy(c0_ref.at[slot], ge, sem_in.at[0])
            copy.start()
            for load in loads:
                load.start()
            copy.wait()

        @pl.when(jnp.logical_not(last))
        def _():
            copies = [
                pltpu.make_async_copy(gl_ref, ge.at[:BLK], sem_in.at[0]),
                pltpu.make_async_copy(g_ref, ge.at[own], sem_in.at[1]),
                pltpu.make_async_copy(gr_ref, ge.at[BLK + ROWS :], sem_in.at[2]),
            ]
            for copy in copies:
                copy.start()
            for load in loads:
                load.start()
            for copy in copies:
                copy.wait()

        for load in loads + ends(qal0_ref, qar0_ref):
            load.wait()

        @pl.loop(0, 2)
        def _(pair):
            lane = lax.broadcasted_iota(jnp.int32, (EXT, 128), 1)
            rows = pl.ds(pl.multiple_of(16 * pair, 16), 16)
            low = w_ref[rows, 192:224, :].reshape(512, 1024)
            high = w_ref[rows, 224:256, :].reshape(512, 1024)
            spread = dot(ge[:, :1024], low, NT) + dot(ge[:, 1024:], high, NT)
            for half in range(4):
                head = pair * 4 + half
                at = pl.ds(pl.multiple_of(head * HDIM, HDIM), HDIM)
                beyond = pl.ds(pl.multiple_of(WIDTH + head * HDIM, HDIM), HDIM)
                third = pl.ds(pl.multiple_of(2 * WIDTH + head * HDIM, HDIM), HDIM)
                d_att = spread[:, half * HDIM : (half + 1) * HDIM].astype(BF16).astype(F32)
                query, key, value = qa[:, at], kv[:, at], kv[:, beyond]
                picked = (lane == head) | (lane == HEADS + head)
                inv = jnp.sum(
                    jnp.where(picked, qa[:, 2 * WIDTH :].astype(F32), 0.0),
                    axis=-1,
                    keepdims=True,
                )
                d_sum = (d_att * inv).astype(BF16)
                d_total = -inv * jnp.sum(
                    d_att * qa[:, beyond].astype(F32), axis=-1, keepdims=True
                )
                probs = jnp.exp(dot(query, key, NT) * SCALE) * mask[...]
                d_probs = dot(d_sum, value, NT)
                d_scores = (probs * (d_probs + d_total) * SCALE).astype(BF16)
                d_value = dot(probs.astype(BF16), d_sum, TN)[own]
                d_key = dot(d_scores, query, TN)[own]
                d_query = dot(d_scores[own], key)

                def unnorm(grad, unit, which):
                    grad = grad.astype(BF16).astype(F32)
                    unit = unit.astype(F32)
                    r = jnp.sum(
                        jnp.where(lane[:ROWS] == which, rr[...], 0.0), axis=-1, keepdims=True
                    )
                    return r * (grad - unit * jnp.mean(grad * unit, axis=-1, keepdims=True))

                dz[:, at] = unnorm(d_query, query[own], head).astype(BF16)
                dz[:, beyond] = unnorm(d_key, key[own], HEADS + head).astype(BF16)
                dz[:, third] = d_value.astype(BF16)

        inner_ref[...] = jnp.zeros((ROWS, 128), F32)

        @pl.loop(0, 4)
        def _(tile):
            rows = pl.ds(pl.multiple_of(8 * tile, 8), 8)
            cols = pl.ds(pl.multiple_of(tile * 512, 512), 512)
            grad = jnp.zeros((ROWS, 512), F32)
            for part in range(3):
                weight = w_ref[rows, 64 * part : 64 * part + 64, :].reshape(512, WIDTH)
                grad += dot(dz[:, part * WIDTH : (part + 1) * WIDTH], weight, NT)
            grad = grad.astype(BF16).astype(F32)
            dn[:, cols] = grad
            product = grad * xs[:, cols].astype(F32)
            inner_ref[...] += (product[:, :128] + product[:, 128:256]) + (product[:, 256:384] + product[:, 384:])

        @pl.loop(0, ROWS // BLK)
        def _(block):
            at = pl.ds(pl.multiple_of(block * BLK, BLK), BLK)
            x = xs[at].astype(F32)
            scale = lax.rsqrt(jnp.mean(x * x, axis=-1, keepdims=True) + EPS)
            inner = jnp.sum(inner_ref[at], axis=-1, keepdims=True) * scale * scale * (1.0 / D)
            through = ge[pl.ds(pl.multiple_of(block * BLK + BLK, BLK), BLK)].astype(F32)
            result[at] = (through + scale * (dn[at] - x * inner)).astype(BF16)

        saves = [
            pltpu.make_async_copy(source, target, sem_out.at[index])
            for index, (source, target) in enumerate(
                (
                    (result, next_ref),
                (result.at[:BLK], left_ref),
                (result.at[ROWS - BLK :], right_ref),
                    (result, grad_ref.at[slot]),
                )
            )
        ]
        for copy in saves:
            copy.start()
        for copy in saves:
            copy.wait()


def backward_call(step, position, c0, g, gl, gr, mask, w, xs, qa, ends, kv, rr, grads, kind):
    rows = jax.ShapeDtypeStruct((ROWS, D), BF16)
    edge = jax.ShapeDtypeStruct((BLK, D), BF16)
    body = functools.partial(backward_body, step)
    carried = () if grads is None else (grads,)
    if not carried:
        body = fresh(body, 15, 1)
    outs = pl.pallas_call(
        body,
        name="backward_layer",
        out_shape=(rows, edge, edge, kind),
        in_specs=spaces(*("saaaaav" + "a" * (8 + len(carried)))),
        out_specs=spaces(*"aaaa"),
        scratch_shapes=[
            pltpu.VMEM((EXT, D), BF16),
            pltpu.VMEM((ROWS, D), BF16),
            pltpu.VMEM((EXT, PACK), BF16),
            pltpu.VMEM((EXT, 2 * WIDTH), BF16),
            pltpu.VMEM((ROWS, 128), F32),
            pltpu.VMEM((ROWS, 3 * WIDTH), BF16),
            pltpu.VMEM((ROWS, D), F32),
            pltpu.VMEM((ROWS, D), BF16),
            pltpu.VMEM((EXT, EXT), F32),
            pltpu.VMEM((ROWS, 128), F32),
            pltpu.SemaphoreType.DMA((3,)),
            pltpu.SemaphoreType.DMA((7,)),
            pltpu.SemaphoreType.DMA((4,)),
        ],
        input_output_aliases={15: 3} if carried else {},
        compiler_params=pltpu.CompilerParams(vmem_limit_bytes=VMEM_LIMIT),
    )(position, c0, g, gl, gr, mask, w, xs, qa, *ends, kv, rr, *carried)
    return outs[:3], outs[3]


def pack_body(wq_ref, wk_ref, wv_ref, wo_ref, first_ref, second_ref):
    first_ref[0:64] = wq_ref[0]
    first_ref[64:SPLIT] = wk_ref[0, : SPLIT - 64]
    second_ref[: 128 - SPLIT] = wk_ref[0, SPLIT - 64 :]
    second_ref[128 - SPLIT : 192 - SPLIT] = wv_ref[0]
    second_ref[192 - SPLIT : 224 - SPLIT] = wo_ref[0, :, :WIDTH]
    second_ref[224 - SPLIT :] = wo_ref[0, :, WIDTH:]


def pack_call(*weights):
    return pl.pallas_call(
        pack_body,
        name="pack_weights",
        out_shape=(
            jax.ShapeDtypeStruct((SPLIT, WIDTH), BF16),
            jax.ShapeDtypeStruct((REST, WIDTH), BF16),
        ),
        in_specs=spaces(*"vvvv"),
        out_specs=spaces(*"vv"),
    )(*weights)

BOTH = ("section", "ctx")


def neighbours(n_ctx, distance):
    return [(c, c + distance) for c in range(n_ctx) if 0 <= c + distance < n_ctx]


def hop(sections, step, n_ctx):
    return [(s * n_ctx + c, (s + step) * n_ctx + c) for s in sections for c in range(n_ctx)]


def diagonal(n_section, step, n_ctx, distance):
    return [
        (s * n_ctx + source, (s + step) * n_ctx + target)
        for s in range(n_section)
        if 0 <= s + step < n_section
        for source, target in neighbours(n_ctx, distance)
    ]


def relay(parts, sections, step, n_section, n_ctx):
    rows, left, right = parts
    rows = lax.ppermute(rows, BOTH, hop(sections, step, n_ctx))
    from_left = lax.ppermute(right, BOTH, diagonal(n_section, step, n_ctx, 1))
    from_right = lax.ppermute(left, BOTH, diagonal(n_section, step, n_ctx, -1))
    return rows, from_left, from_right


def edges(block, dim, width, n_ctx):
    size = block.shape[dim]
    tail = lax.slice_in_dim(block, size - width, size, axis=dim)
    head = lax.slice_in_dim(block, 0, width, axis=dim)
    from_left = lax.ppermute(tail, "ctx", neighbours(n_ctx, 1))
    from_right = lax.ppermute(head, "ctx", neighbours(n_ctx, -1))
    return from_left, from_right


def allowed_keys(block_mask, place, n_ctx):
    block_ids = place * BLOCKS_DEV + jnp.arange(BLOCKS_DEV)
    mask = block_mask.astype(F32)
    left = mask[:, :, 0] * (block_ids > 0).astype(F32)
    right = mask[:, :, 1] * (block_ids < BLOCKS_DEV * n_ctx - 1).astype(F32)
    return jnp.stack([left, jnp.ones_like(left), right], axis=2)


def key_weights(before, allow, after):
    allow = jnp.concatenate([before, allow, after], axis=1)
    allow = jnp.repeat(allow, BLK, axis=1)
    block = jnp.arange(EXT) // BLK
    offset = block[None, :] - block[:, None] + 1
    return sum(
        jnp.where(offset == side, allow[:, :, side : side + 1], 0.0) for side in range(3)
    )


def per_device(section_input, cotangent, w_query, w_key, w_value, w_out, block_mask):
    n_section = lax.axis_size("section")
    n_ctx = lax.axis_size("ctx")
    section = lax.axis_index("section")
    place = lax.axis_index("ctx")
    micro = section_input.shape[0]
    steps = n_section + micro - 1

    first, second = pack_call(w_query, w_key, w_value, w_out)
    position = jnp.full((1,), section, jnp.int32)
    reverse = n_section - 1 - position
    allow = allowed_keys(block_mask, place, n_ctx)
    fields = jnp.stack([section_input, cotangent])

    def packed(part, block):
        lanes = jnp.pad(part.reshape(1, -1), ((0, 15), (0, D - part.size)))
        return jnp.concatenate([block.reshape(-1, D), lanes.astype(BF16)], axis=0)

    pieces = jnp.concatenate(
        [packed(allow[:, :1], fields[:, :, :BLK]), packed(allow[:, -1:], fields[:, :, -BLK:])]
    )
    size = pieces.shape[0] // 2
    before, after = edges(pieces, 0, size, n_ctx)
    weights, (before, after) = gather_weights(
        first, second, (before, after), jnp.full((1,), place, jnp.int32), n_ctx
    )

    def unpacked(piece):
        block = piece[: size - 16].reshape(2, micro, BLK, D)
        return block, piece[size - 16, : 3 * micro].astype(F32).reshape(micro, 1, 3)

    before, before_allow = unpacked(before)
    after, after_allow = unpacked(after)
    extended = jnp.concatenate([before, fields, after], axis=2)
    mask = key_weights(before_allow, allow, after_allow)
    forward_mask = mask[:, BLK : BLK + ROWS]

    kinds = (
        jax.ShapeDtypeStruct((micro, ROWS, D), BF16),
        jax.ShapeDtypeStruct((micro, ROWS, D), BF16),
        jax.ShapeDtypeStruct((micro, ROWS, PACK), BF16),
        jax.ShapeDtypeStruct((micro, EXT, 2 * WIDTH), BF16),
        jax.ShapeDtypeStruct((micro, ROWS, 128), F32),
    )
    zero_rows = jnp.zeros((ROWS, D), BF16)
    zero_edge = jnp.zeros((BLK, D), BF16)
    incoming = (zero_rows, zero_edge, zero_edge)

    def forward(step, incoming, saved):
        parts, saved = forward_call(
            step, position, extended[0], *incoming, forward_mask, weights, saved, kinds
        )
        senders = [s for s in range(step - micro + 1, step + 1) if 0 <= s < n_section - 1]
        if senders:
            incoming = relay(parts, senders, 1, n_section, n_ctx)
        return incoming, saved

    def backward(step, incoming, saved, ends, grads):
        xs, _, qa, kv, rr = saved
        parts, grads = backward_call(
            step, reverse, extended[1], *incoming, mask, weights, xs, qa, ends, kv, rr, grads, kinds[0]
        )
        top = n_section - 1 - step
        senders = [s for s in range(top, top + micro) if 0 < s < n_section]
        if senders:
            incoming = relay(parts, senders, -1, n_section, n_ctx)
        return incoming, grads

    saved = ()
    for step in range(n_section):
        incoming, saved = forward(step, incoming, saved)
    ends = edges(saved[2][0], 0, BLK, n_ctx)
    pulled, grads = backward(0, (zero_rows, zero_edge, zero_edge), saved, ends * 2, None)
    saved, grads = lax.optimization_barrier((saved, grads))
    for step in range(n_section, steps):
        incoming, saved = forward(step, incoming, saved)
    ends = ends + edges(saved[2][1], 0, BLK, n_ctx)
    for step in range(1, steps):
        pulled, grads = backward(step, pulled, saved, ends, grads)
    outputs = saved[1]
    return (outputs[None], grads[None])


def solution(mesh):
    return jax.shard_map(
        per_device,
        mesh=mesh,
        in_specs=(
            P(None, "ctx", None),
            P(None, "ctx", None),
            P("section", "ctx", None),
            P("section", "ctx", None),
            P("section", "ctx", None),
            P("section", "ctx", None),
            P(None, "ctx", None),
        ),
        out_specs=(P("section", None, "ctx", None), P("section", None, "ctx", None)),
        check_vma=False,
    )
```

```python
import functools

import jax
import jax.numpy as jnp
from jax import lax
from jax.experimental import pallas as pl
from jax.experimental.pallas import tpu as pltpu
from jax.sharding import PartitionSpec as P

D = 2048
HEADS = 8
HDIM = 128
BLOCKS_DEV = 4
BLK = 32
MICRO = 2
ROWS = BLK * BLOCKS_DEV
EXT = ROWS + 2 * BLK
WIDTH = HEADS * HDIM
PACK = 2 * WIDTH + 128
EPS = 1e-06
VMEM_LIMIT = 16 << 20
SCALE = HDIM ** (-0.5)
F32 = jnp.float32
BF16 = jnp.bfloat16

NT = (((1,), (1,)), ((), ()))
NN = (((1,), (0,)), ((), ()))
TN = (((0,), (0,)), ((), ()))


def dot(a, b, dims=NN):
    return lax.dot_general(a, b, dims, preferred_element_type=F32)


def wtile(w_ref, row, count, col, width):
    tile = w_ref[:, row : row + count, col : col + width]
    return tile.reshape(tile.shape[0] * count, width)


def schedule(step, position):
    micro_id = step - position
    active = (micro_id >= 0) & (micro_id < MICRO)
    return active, jnp.clip(micro_id, 0, MICRO - 1), position == 0


def forward_body(
    step,
    section_ref,
    x0_ref,
    x_ref,
    xl_ref,
    xr_ref,
    mask_ref,
    w_ref,
    xs_in,
    out_in,
    qa_in,
    kv_in,
    rr_in,
    next_ref,
    left_ref,
    right_ref,
    xs_ref,
    out_ref,
    qa_ref,
    kv_ref,
    rr_ref,
    xe,
    normed,
    qa,
    kv,
    rr,
    result,
    inverse,
    mask,
    sem_in,
    sem_out,
):
    active, slot, first = schedule(step, section_ref[0])

    @pl.when(active)
    def _():
        mask_copy = pltpu.make_async_copy(mask_ref.at[slot], mask, sem_in.at[3])
        mask_copy.start()

        @pl.when(first)
        def _():
            copy = pltpu.make_async_copy(x0_ref.at[slot], xe, sem_in.at[0])
            copy.start()
            copy.wait()

        @pl.when(jnp.logical_not(first))
        def _():
            copies = [
                pltpu.make_async_copy(xl_ref, xe.at[:BLK], sem_in.at[0]),
                pltpu.make_async_copy(x_ref, xe.at[BLK : BLK + ROWS], sem_in.at[1]),
                pltpu.make_async_copy(xr_ref, xe.at[BLK + ROWS :], sem_in.at[2]),
            ]
            for copy in copies:
                copy.start()
            for copy in copies:
                copy.wait()

        saves = [pltpu.make_async_copy(xe.at[BLK : BLK + ROWS], xs_ref.at[slot], sem_out.at[0])]
        saves[0].start()

        @pl.loop(0, EXT // BLK)
        def _(block):
            at = pl.ds(pl.multiple_of(block * BLK, BLK), BLK)
            rows = xe[at].astype(F32)
            scale = lax.rsqrt(jnp.mean(rows * rows, axis=-1, keepdims=True) + EPS)
            normed[at] = (rows * scale).astype(BF16)

        rr[...] = jnp.zeros((ROWS, 128), F32)
        inverse[...] = jnp.zeros((ROWS, 128), F32)
        mask_copy.wait()

        @pl.loop(0, 2)
        def _(pair):
            lane = lax.broadcasted_iota(jnp.int32, (ROWS, 128), 1)
            tile = pl.ds(pl.multiple_of(pair * 512, 512), 512)
            queries = dot(normed[BLK : BLK + ROWS], w_ref[:, 0:64, tile].reshape(D, 512))
            keys = dot(normed[...], w_ref[:, 64:128, tile].reshape(D, 512))
            values = dot(normed[...], w_ref[:, 128:192, tile].reshape(D, 512))
            for half in range(4):
                head = pair * 4 + half
                cols = slice(half * HDIM, (half + 1) * HDIM)
                at = pl.ds(pl.multiple_of(head * HDIM, HDIM), HDIM)
                beyond = pl.ds(pl.multiple_of(WIDTH + head * HDIM, HDIM), HDIM)
                query, key, value = queries[:, cols], keys[:, cols], values[:, cols]
                rq = lax.rsqrt(jnp.mean(query * query, axis=-1, keepdims=True) + EPS)
                rk = lax.rsqrt(jnp.mean(key * key, axis=-1, keepdims=True) + EPS)
                query = (query * rq).astype(BF16)
                key = (key * rk).astype(BF16)
                value = value.astype(BF16)
                probs = jnp.exp(dot(query, key, NT) * SCALE) * mask[...]
                inv = 1.0 / jnp.sum(probs, axis=-1, keepdims=True)
                attended = dot(probs.astype(BF16), value) * inv
                qa[:, at] = query
                qa[:, beyond] = attended.astype(BF16)
                kv[:, at] = key
                kv[:, beyond] = value
                high = inv.astype(BF16).astype(F32)
                stored = jnp.where(lane == head, rq, rr[...])
                rr[...] = jnp.where(lane == HEADS + head, rk[BLK : BLK + ROWS], stored)
                stored = jnp.where(lane == head, high, inverse[...])
                inverse[...] = jnp.where(lane == HEADS + head, inv - high, stored)

        qa[:, 2 * WIDTH :] = inverse[...].astype(BF16)
        for index, (source, target) in enumerate(((qa, qa_ref), (kv, kv_ref), (rr, rr_ref))):
            copy = pltpu.make_async_copy(source, target.at[slot], sem_out.at[1 + index])
            copy.start()
            saves.append(copy)

        for half in range(2):
            @pl.loop(0, 1)
            def _(tile):
                source = pl.ds(pl.multiple_of(tile * 1024, 1024), 1024)
                cols = pl.ds(pl.multiple_of(half * 1024 + tile * 1024, 1024), 1024)
                low = 192 + 32 * half
                weight = w_ref[:, low : low + 32, source].reshape(WIDTH, 1024)
                update = dot(qa[:, WIDTH : 2 * WIDTH], weight)
                result[:, cols] = (xe[BLK : BLK + ROWS, cols].astype(F32) + update).astype(BF16)

        for index, (source, target) in enumerate(
            (
                (result, next_ref),
                (result.at[:BLK], left_ref),
                (result.at[ROWS - BLK :], right_ref),
                (result, out_ref.at[slot]),
            )
        ):
            copy = pltpu.make_async_copy(source, target, sem_out.at[4 + index])
            copy.start()
            saves.append(copy)
        for copy in saves:
            copy.wait()


def spaces(*names):
    table = dict(s=pltpu.SMEM, v=pltpu.VMEM, a=pltpu.HBM)
    return [pl.BlockSpec(memory_space=table[n]) for n in names]


def shape_of(a):
    return jax.ShapeDtypeStruct(a.shape, a.dtype)


def fresh(body, position, count):
    def wrapped(*refs):
        return body(*refs[:position], *([None] * count), *refs[position:])

    return wrapped


def forward_call(step, position, x0, x, xl, xr, mask, w, saved, kinds):
    rows = jax.ShapeDtypeStruct((ROWS, D), BF16)
    edge = jax.ShapeDtypeStruct((BLK, D), BF16)
    body = functools.partial(forward_body, step)
    if not saved:
        body = fresh(body, 7, len(kinds))
    outs = pl.pallas_call(
        body,
        name="forward_layer",
        out_shape=(rows, edge, edge) + kinds,
        in_specs=spaces(*("saaaaav" + "a" * len(saved))),
        out_specs=spaces(*"aaaaaaaa"),
        scratch_shapes=[
            pltpu.VMEM((EXT, D), BF16),
            pltpu.VMEM((EXT, D), BF16),
            pltpu.VMEM((ROWS, PACK), BF16),
            pltpu.VMEM((EXT, 2 * WIDTH), BF16),
            pltpu.VMEM((ROWS, 128), F32),
            pltpu.VMEM((ROWS, D), BF16),
            pltpu.VMEM((ROWS, 128), F32),
            pltpu.VMEM((ROWS, EXT), F32),
            pltpu.SemaphoreType.DMA((4,)),
            pltpu.SemaphoreType.DMA((8,)),
        ],
        input_output_aliases={7 + i: 3 + i for i in range(len(saved))},
        compiler_params=pltpu.CompilerParams(vmem_limit_bytes=VMEM_LIMIT),
    )(position, x0, x, xl, xr, mask, w, *saved)
    return outs[:3], outs[3:]

ACROSS = 4
SPLIT = 112
REST = 256 - SPLIT
X_ORDER = (0, -1, 1, 2)
Z_ORDER = (0, -1, -2, -3, 4, 1, 2, 3)


def load_body(n_ctx, place_ref, *refs):
    sources, w_ref, sem = refs[:-2], refs[-2], refs[-1]
    depth = n_ctx // ACROSS
    z, x = place_ref[0] // ACROSS, lax.rem(place_ref[0], ACROSS)

    def owner(dx, dz):
        return lax.rem(z + dz + depth, depth) * ACROSS + lax.rem(x + dx + ACROSS, ACROSS)

    moves = []
    for ref, dz, blocks in zip(
        sources[:9],
        (0, -1, -2, -3, 4, 4, 1, 2, 3),
        (X_ORDER,) * 4 + (X_ORDER[:2], X_ORDER[2:]) + (X_ORDER,) * 3,
    ):
        for index, dx in enumerate(blocks):
            piece = ref.at[index * SPLIT : (index + 1) * SPLIT]
            moves.append((piece, w_ref.at[owner(dx, dz), 0:SPLIT]))
    for ref, dx, blocks in zip(
        sources[9:], (0, -1, 2, 2, 1), (Z_ORDER, Z_ORDER, Z_ORDER[:4], Z_ORDER[4:], Z_ORDER)
    ):
        for index, dz in enumerate(blocks):
            piece = ref.at[index * REST : (index + 1) * REST]
            moves.append((piece, w_ref.at[owner(dx, dz), SPLIT:256]))
    copies = [
        pltpu.make_async_copy(source, target, sem.at[index])
        for index, (source, target) in enumerate(moves)
    ]
    for copy in copies:
        copy.start()
    for copy in copies:
        copy.wait()


def load_call(place, n_ctx, pieces):
    return pl.pallas_call(
        functools.partial(load_body, n_ctx),
        name="load_weights",
        out_shape=pltpu.VMEM((n_ctx, 256, WIDTH), BF16),
        in_specs=spaces("s", *("a" * len(pieces))),
        out_specs=pl.BlockSpec(memory_space=pltpu.VMEM),
        scratch_shapes=[pltpu.SemaphoreType.DMA((2 * n_ctx,))],
        compiler_params=pltpu.CompilerParams(vmem_limit_bytes=40 << 20),
    )(place, *pieces)


def turn(block, dx, dz, n_ctx):
    depth = n_ctx // ACROSS
    pairs = [
        (z * ACROSS + x, (z + dz) % depth * ACROSS + (x + dx) % ACROSS)
        for z in range(depth)
        for x in range(ACROSS)
    ]
    return lax.ppermute(block, "ctx", pairs)


def ring_x(block, n_ctx):
    half = block.shape[0] // 2
    below, above = turn(block, 1, 0, n_ctx), turn(block, -1, 0, n_ctx)
    return below, turn(below[:half], 1, 0, n_ctx), turn(above[half:], -1, 0, n_ctx), above


def ring_z(block, n_ctx):
    half = block.shape[0] // 2
    below, above = [block], [block]
    for _ in range(n_ctx // ACROSS // 2 - 1):
        below.append(turn(below[-1], 0, 1, n_ctx))
        above.append(turn(above[-1], 0, -1, n_ctx))
    low, high = turn(below[-1][:half], 0, 1, n_ctx), turn(above[-1][half:], 0, -1, n_ctx)
    return (*below[1:], low, high, *above[1:])


def gather_weights(first, second, ends, place, n_ctx):
    wide = jnp.concatenate([first] + [turn(first, -dx, 0, n_ctx) for dx in X_ORDER[1:]])
    tall = jnp.concatenate([second, *ring_z(second, n_ctx)])
    wide, tall, ends = lax.optimization_barrier((wide, tall, ends))
    pieces = (wide, *ring_z(wide, n_ctx), tall, *ring_x(tall, n_ctx))
    return load_call(place, n_ctx, pieces), ends


def backward_body(
    step,
    section_ref,
    c0_ref,
    g_ref,
    gl_ref,
    gr_ref,
    mask_ref,
    w_ref,
    xs_ref,
    qa_ref,
    qal0_ref,
    qar0_ref,
    qal1_ref,
    qar1_ref,
    kv_ref,
    rr_ref,
    grad_in,
    next_ref,
    left_ref,
    right_ref,
    grad_ref,
    ge,
    xs,
    qa,
    kv,
    rr,
    dz,
    dn,
    result,
    mask,
    inner_ref,
    sem_in,
    sem_save,
    sem_out,
):
    active, slot, last = schedule(step, section_ref[0])
    own = slice(BLK, BLK + ROWS)

    @pl.when(active)
    def _():
        loads = [
            pltpu.make_async_copy(source.at[slot], target, sem_save.at[index])
            for index, (source, target) in enumerate(
                (
                    (qa_ref, qa.at[own]),
                    (kv_ref, kv),
                    (rr_ref, rr),
                    (xs_ref, xs),
                    (mask_ref, mask),
                )
            )
        ]

        def ends(left, right):
            return [
                pltpu.make_async_copy(left, qa.at[:BLK], sem_save.at[5]),
                pltpu.make_async_copy(right, qa.at[BLK + ROWS :], sem_save.at[6]),
            ]

        @pl.when(slot == 0)
        def _():
            for copy in ends(qal0_ref, qar0_ref):
                copy.start()

        @pl.when(slot == 1)
        def _():
            for copy in ends(qal1_ref, qar1_ref):
                copy.start()

        @pl.when(last)
        def _():
            copy = pltpu.make_async_copy(c0_ref.at[slot], ge, sem_in.at[0])
            copy.start()
            for load in loads:
                load.start()
            copy.wait()

        @pl.when(jnp.logical_not(last))
        def _():
            copies = [
                pltpu.make_async_copy(gl_ref, ge.at[:BLK], sem_in.at[0]),
                pltpu.make_async_copy(g_ref, ge.at[own], sem_in.at[1]),
                pltpu.make_async_copy(gr_ref, ge.at[BLK + ROWS :], sem_in.at[2]),
            ]
            for copy in copies:
                copy.start()
            for load in loads:
                load.start()
            for copy in copies:
                copy.wait()

        for load in loads + ends(qal0_ref, qar0_ref):
            load.wait()

        @pl.loop(0, 2)
        def _(pair):
            lane = lax.broadcasted_iota(jnp.int32, (EXT, 128), 1)
            rows = pl.ds(pl.multiple_of(16 * pair, 16), 16)
            low = w_ref[rows, 192:224, :].reshape(512, 1024)
            high = w_ref[rows, 224:256, :].reshape(512, 1024)
            spread = dot(ge[:, :1024], low, NT) + dot(ge[:, 1024:], high, NT)
            for half in range(4):
                head = pair * 4 + half
                at = pl.ds(pl.multiple_of(head * HDIM, HDIM), HDIM)
                beyond = pl.ds(pl.multiple_of(WIDTH + head * HDIM, HDIM), HDIM)
                third = pl.ds(pl.multiple_of(2 * WIDTH + head * HDIM, HDIM), HDIM)
                d_att = spread[:, half * HDIM : (half + 1) * HDIM].astype(BF16).astype(F32)
                query, key, value = qa[:, at], kv[:, at], kv[:, beyond]
                picked = (lane == head) | (lane == HEADS + head)
                inv = jnp.sum(
                    jnp.where(picked, qa[:, 2 * WIDTH :].astype(F32), 0.0),
                    axis=-1,
                    keepdims=True,
                )
                d_sum = (d_att * inv).astype(BF16)
                d_total = -inv * jnp.sum(
                    d_att * qa[:, beyond].astype(F32), axis=-1, keepdims=True
                )
                probs = jnp.exp(dot(query, key, NT) * SCALE) * mask[...]
                d_probs = dot(d_sum, value, NT)
                d_scores = (probs * (d_probs + d_total) * SCALE).astype(BF16)
                d_value = dot(probs.astype(BF16), d_sum, TN)[own]
                d_key = dot(d_scores, query, TN)[own]
                d_query = dot(d_scores[own], key)

                def unnorm(grad, unit, which):
                    grad = grad.astype(BF16).astype(F32)
                    unit = unit.astype(F32)
                    r = jnp.sum(
                        jnp.where(lane[:ROWS] == which, rr[...], 0.0), axis=-1, keepdims=True
                    )
                    return r * (grad - unit * jnp.mean(grad * unit, axis=-1, keepdims=True))

                dz[:, at] = unnorm(d_query, query[own], head).astype(BF16)
                dz[:, beyond] = unnorm(d_key, key[own], HEADS + head).astype(BF16)
                dz[:, third] = d_value.astype(BF16)

        inner_ref[...] = jnp.zeros((ROWS, 128), F32)

        @pl.loop(0, 2)
        def _(tile):
            rows = pl.ds(pl.multiple_of(16 * tile, 16), 16)
            cols = pl.ds(pl.multiple_of(tile * 1024, 1024), 1024)
            grad = jnp.zeros((ROWS, 1024), F32)
            for part in range(3):
                weight = w_ref[rows, 64 * part : 64 * part + 64, :].reshape(1024, WIDTH)
                grad += dot(dz[:, part * WIDTH : (part + 1) * WIDTH], weight, NT)
            grad = grad.astype(BF16).astype(F32)
            dn[:, cols] = grad
            product = grad * xs[:, cols].astype(F32)
            inner_ref[...] += sum(product[:, at : at + 128] for at in range(0, 1024, 128))

        @pl.loop(0, ROWS // BLK)
        def _(block):
            at = pl.ds(pl.multiple_of(block * BLK, BLK), BLK)
            x = xs[at].astype(F32)
            scale = lax.rsqrt(jnp.mean(x * x, axis=-1, keepdims=True) + EPS)
            inner = jnp.sum(inner_ref[at], axis=-1, keepdims=True) * scale * scale * (1.0 / D)
            through = ge[pl.ds(pl.multiple_of(block * BLK + BLK, BLK), BLK)].astype(F32)
            result[at] = (through + scale * (dn[at] - x * inner)).astype(BF16)

        saves = [
            pltpu.make_async_copy(source, target, sem_out.at[index])
            for index, (source, target) in enumerate(
                (
                    (result, next_ref),
                (result.at[:BLK], left_ref),
                (result.at[ROWS - BLK :], right_ref),
                    (result, grad_ref.at[slot]),
                )
            )
        ]
        for copy in saves:
            copy.start()
        for copy in saves:
            copy.wait()


def backward_call(step, position, c0, g, gl, gr, mask, w, xs, qa, ends, kv, rr, grads, kind):
    rows = jax.ShapeDtypeStruct((ROWS, D), BF16)
    edge = jax.ShapeDtypeStruct((BLK, D), BF16)
    body = functools.partial(backward_body, step)
    carried = () if grads is None else (grads,)
    if not carried:
        body = fresh(body, 15, 1)
    outs = pl.pallas_call(
        body,
        name="backward_layer",
        out_shape=(rows, edge, edge, kind),
        in_specs=spaces(*("saaaaav" + "a" * (8 + len(carried)))),
        out_specs=spaces(*"aaaa"),
        scratch_shapes=[
            pltpu.VMEM((EXT, D), BF16),
            pltpu.VMEM((ROWS, D), BF16),
            pltpu.VMEM((EXT, PACK), BF16),
            pltpu.VMEM((EXT, 2 * WIDTH), BF16),
            pltpu.VMEM((ROWS, 128), F32),
            pltpu.VMEM((ROWS, 3 * WIDTH), BF16),
            pltpu.VMEM((ROWS, D), F32),
            pltpu.VMEM((ROWS, D), BF16),
            pltpu.VMEM((EXT, EXT), F32),
            pltpu.VMEM((ROWS, 128), F32),
            pltpu.SemaphoreType.DMA((3,)),
            pltpu.SemaphoreType.DMA((7,)),
            pltpu.SemaphoreType.DMA((4,)),
        ],
        input_output_aliases={15: 3} if carried else {},
        compiler_params=pltpu.CompilerParams(vmem_limit_bytes=VMEM_LIMIT),
    )(position, c0, g, gl, gr, mask, w, xs, qa, *ends, kv, rr, *carried)
    return outs[:3], outs[3]


def pack_body(wq_ref, wk_ref, wv_ref, wo_ref, first_ref, second_ref):
    first_ref[0:64] = wq_ref[0]
    first_ref[64:SPLIT] = wk_ref[0, : SPLIT - 64]
    second_ref[: 128 - SPLIT] = wk_ref[0, SPLIT - 64 :]
    second_ref[128 - SPLIT : 192 - SPLIT] = wv_ref[0]
    second_ref[192 - SPLIT : 224 - SPLIT] = wo_ref[0, :, :WIDTH]
    second_ref[224 - SPLIT :] = wo_ref[0, :, WIDTH:]


def pack_call(*weights):
    return pl.pallas_call(
        pack_body,
        name="pack_weights",
        out_shape=(
            jax.ShapeDtypeStruct((SPLIT, WIDTH), BF16),
            jax.ShapeDtypeStruct((REST, WIDTH), BF16),
        ),
        in_specs=spaces(*"vvvv"),
        out_specs=spaces(*"vv"),
    )(*weights)

BOTH = ("section", "ctx")


def neighbours(n_ctx, distance):
    return [(c, c + distance) for c in range(n_ctx) if 0 <= c + distance < n_ctx]


def hop(sections, step, n_ctx):
    return [(s * n_ctx + c, (s + step) * n_ctx + c) for s in sections for c in range(n_ctx)]


def diagonal(n_section, step, n_ctx, distance):
    return [
        (s * n_ctx + source, (s + step) * n_ctx + target)
        for s in range(n_section)
        if 0 <= s + step < n_section
        for source, target in neighbours(n_ctx, distance)
    ]


def relay(parts, sections, step, n_section, n_ctx):
    rows, left, right = parts
    rows = lax.ppermute(rows, BOTH, hop(sections, step, n_ctx))
    from_left = lax.ppermute(right, BOTH, diagonal(n_section, step, n_ctx, 1))
    from_right = lax.ppermute(left, BOTH, diagonal(n_section, step, n_ctx, -1))
    return rows, from_left, from_right


def edges(block, dim, width, n_ctx):
    size = block.shape[dim]
    tail = lax.slice_in_dim(block, size - width, size, axis=dim)
    head = lax.slice_in_dim(block, 0, width, axis=dim)
    from_left = lax.ppermute(tail, "ctx", neighbours(n_ctx, 1))
    from_right = lax.ppermute(head, "ctx", neighbours(n_ctx, -1))
    return from_left, from_right


def allowed_keys(block_mask, place, n_ctx):
    block_ids = place * BLOCKS_DEV + jnp.arange(BLOCKS_DEV)
    mask = block_mask.astype(F32)
    left = mask[:, :, 0] * (block_ids > 0).astype(F32)
    right = mask[:, :, 1] * (block_ids < BLOCKS_DEV * n_ctx - 1).astype(F32)
    return jnp.stack([left, jnp.ones_like(left), right], axis=2)


def key_weights(before, allow, after):
    allow = jnp.concatenate([before, allow, after], axis=1)
    allow = jnp.repeat(allow, BLK, axis=1)
    block = jnp.arange(EXT) // BLK
    offset = block[None, :] - block[:, None] + 1
    return sum(
        jnp.where(offset == side, allow[:, :, side : side + 1], 0.0) for side in range(3)
    )


def per_device(section_input, cotangent, w_query, w_key, w_value, w_out, block_mask):
    n_section = lax.axis_size("section")
    n_ctx = lax.axis_size("ctx")
    section = lax.axis_index("section")
    place = lax.axis_index("ctx")
    micro = section_input.shape[0]
    steps = n_section + micro - 1

    first, second = pack_call(w_query, w_key, w_value, w_out)
    position = jnp.full((1,), section, jnp.int32)
    reverse = n_section - 1 - position
    allow = allowed_keys(block_mask, place, n_ctx)
    fields = jnp.stack([section_input, cotangent])

    def packed(part, block):
        lanes = jnp.pad(part.reshape(1, -1), ((0, 15), (0, D - part.size)))
        return jnp.concatenate([block.reshape(-1, D), lanes.astype(BF16)], axis=0)

    pieces = jnp.concatenate(
        [packed(allow[:, :1], fields[:, :, :BLK]), packed(allow[:, -1:], fields[:, :, -BLK:])]
    )
    size = pieces.shape[0] // 2
    before, after = edges(pieces, 0, size, n_ctx)
    weights, (before, after) = gather_weights(
        first, second, (before, after), jnp.full((1,), place, jnp.int32), n_ctx
    )

    def unpacked(piece):
        block = piece[: size - 16].reshape(2, micro, BLK, D)
        return block, piece[size - 16, : 3 * micro].astype(F32).reshape(micro, 1, 3)

    before, before_allow = unpacked(before)
    after, after_allow = unpacked(after)
    extended = jnp.concatenate([before, fields, after], axis=2)
    mask = key_weights(before_allow, allow, after_allow)
    forward_mask = mask[:, BLK : BLK + ROWS]

    kinds = (
        jax.ShapeDtypeStruct((micro, ROWS, D), BF16),
        jax.ShapeDtypeStruct((micro, ROWS, D), BF16),
        jax.ShapeDtypeStruct((micro, ROWS, PACK), BF16),
        jax.ShapeDtypeStruct((micro, EXT, 2 * WIDTH), BF16),
        jax.ShapeDtypeStruct((micro, ROWS, 128), F32),
    )
    zero_rows = jnp.zeros((ROWS, D), BF16)
    zero_edge = jnp.zeros((BLK, D), BF16)
    incoming = (zero_rows, zero_edge, zero_edge)

    def forward(step, incoming, saved):
        parts, saved = forward_call(
            step, position, extended[0], *incoming, forward_mask, weights, saved, kinds
        )
        senders = [s for s in range(step - micro + 1, step + 1) if 0 <= s < n_section - 1]
        if senders:
            incoming = relay(parts, senders, 1, n_section, n_ctx)
        return incoming, saved

    def backward(step, incoming, saved, ends, grads):
        xs, _, qa, kv, rr = saved
        parts, grads = backward_call(
            step, reverse, extended[1], *incoming, mask, weights, xs, qa, ends, kv, rr, grads, kinds[0]
        )
        top = n_section - 1 - step
        senders = [s for s in range(top, top + micro) if 0 < s < n_section]
        if senders:
            incoming = relay(parts, senders, -1, n_section, n_ctx)
        return incoming, grads

    saved = ()
    for step in range(n_section):
        incoming, saved = forward(step, incoming, saved)
    ends = edges(saved[2][0], 0, BLK, n_ctx)
    pulled, grads = backward(0, (zero_rows, zero_edge, zero_edge), saved, ends * 2, None)
    saved, grads = lax.optimization_barrier((saved, grads))
    for step in range(n_section, steps):
        incoming, saved = forward(step, incoming, saved)
    ends = ends + edges(saved[2][1], 0, BLK, n_ctx)
    for step in range(1, steps):
        pulled, grads = backward(step, pulled, saved, ends, grads)
    outputs = saved[1]
    return (outputs[None], grads[None])


def solution(mesh):
    return jax.shard_map(
        per_device,
        mesh=mesh,
        in_specs=(
            P(None, "ctx", None),
            P(None, "ctx", None),
            P("section", "ctx", None),
            P("section", "ctx", None),
            P("section", "ctx", None),
            P("section", "ctx", None),
            P(None, "ctx", None),
        ),
        out_specs=(P("section", None, "ctx", None), P("section", None, "ctx", None)),
        check_vma=False,
    )
```
